128 devices in a mesh: row: 8 (over y_lo, z), col: 16 (over y_hi, x, core).
Axes of the slice: x: 4, y: 4 (y_hi: 2, y_lo: 2; y = y_hi * 2 + y_lo), z: 4, core: 2. Of those that a mesh axis runs over, the one named last changes fastest.
Arguments:
- features: bfloat16 [24576, 512], P(('col', 'row')), may hold values from -6 to 6
- out_grad: bfloat16 [24576, 512], P(('row', 'col')), may hold values from -6 to 6
- weight: bfloat16 [512, 512], replicated, may hold values from -0.25 to 0.25
- block_values: bfloat16 [8, 16, 288, 4096], P('row', 'col'), may hold values from -0.125 to 0.125
- block_coords: int32 [8, 16, 2, 288], P('row', 'col'), may hold values from 0 to 47, as said below
- block_counts: int32 [8, 16], P('row', 'col'), may hold values from 1 to 288, as said below
Outputs:
- activations: bfloat16 [24576, 512], P(('row', 'col'))
- weight_grad: float32 [512, 512], replicated
- feature_grad: bfloat16 [24576, 512], P(('col', 'row'))
The draws below stay inside these ranges and needn't reach their ends.
Inputs may be any that keep to these rules, and one draw needn't show every extreme that they name: `block_coords`: entry 0 of a slot is a block row below 48, entry 1 a block column below 24; the 288 slots of a tile name distinct blocks. `block_counts`: slots from the count onward are padding: their coordinates and values are ignored. Some tile has exactly 288 live slots.
All inputs are finite; a program needn't handle non-finite values.
Results may differ from the reference program's by a relative error of at most 0.025.
Values may be sent and summed in bfloat16 or wider, within the bound.
No kernel may reach another device: no remote copies, remote signals or barrier semaphores. Data moves between devices by JAX's collectives and lax.ppermute only.
A program may use at most 128 MiB of HBM per device.

```python
import math
import jax
import jax.numpy as jnp
from jax import lax

D = 512
BLOCK = 64
NODES = 24576
BR = 48
BC = 24
MAXB = 288
N_ROW = 8
N_COL = 16


def draw_block_coords(key, part):
    tiles = N_ROW * N_COL
    keys = jax.random.split(jax.random.fold_in(key, 11), tiles)
    orders = jax.vmap(lambda single: jax.random.permutation(single, BR * BC))(keys)[:, :MAXB]
    stacked = jnp.stack([orders // BC, orders % BC], axis=1)
    return stacked.reshape(N_ROW, N_COL, 2, MAXB).astype(jnp.int32)


def draw_block_counts(key, part):
    tiles = N_ROW * N_COL
    first_key, second_key, third_key = jax.random.split(jax.random.fold_in(key, 23), 3)
    first = jax.random.randint(first_key, (tiles,), 1, MAXB + 1)
    second = jax.random.randint(second_key, (tiles,), 1, MAXB + 1)
    chosen = jax.random.randint(third_key, (), 0, tiles)
    counts = jnp.minimum(first, second)
    counts = jnp.where(jnp.arange(tiles) == chosen, MAXB, counts)
    return counts.reshape(N_ROW, N_COL).astype(jnp.int32)


def block_levels(rng, dims, pieces, low, high):
    loudness = 1.0
    for position, blocks in pieces:
        heights = jax.random.uniform(jax.random.fold_in(jax.random.fold_in(rng, 6), position), (blocks,), jnp.float32, low / len(pieces), high / len(pieces))
        loudness = loudness * jnp.repeat(jnp.exp(heights), dims[position] // blocks).reshape((-1,) + (1,) * (len(dims) - 1 - position))
    return loudness


def centred(rng, shape, width, bound, cuts=(), kind=jnp.bfloat16):
    array = width * jax.random.normal(rng, shape, jnp.float32)
    if cuts:
        array = array * block_levels(rng, shape, cuts, -0.22, 0.18)
    return jnp.clip(array, -bound, bound).astype(kind)


def setup_inputs(seed: int = 0) -> dict:
    seeds = jax.random.split(jax.random.key(seed), 7)
    return {
        "features": centred(seeds[0], (NODES, D), 1.0, 6.0, ((0, 128),)),
        "out_grad": centred(seeds[1], (NODES, D), 1.0, 6.0, ((0, 128),)),
        "weight": centred(seeds[2], (D, D), D ** -0.5, 0.25),
        "block_values": centred(seeds[3], (N_ROW, N_COL, MAXB, BLOCK * BLOCK), (NODES // 12) ** -0.5, 0.125, ((0, 8), (1, 16))),
        "block_coords": draw_block_coords(jax.random.fold_in(seeds[6], 71), 0),
        "block_counts": draw_block_counts(jax.random.fold_in(seeds[6], 71), 0),
    }


def forward_tile(slot_vals, coords, panel):
    panel_blocks = panel.reshape(BC, BLOCK, D).astype(jnp.float32)
    gathered = panel_blocks[coords[1]]
    products = jnp.einsum('mrc,mcd->mrd', slot_vals, gathered)
    totals = jnp.zeros((BR, BLOCK, D), jnp.float32).at[coords[0]].add(products)
    return totals.reshape(BR * BLOCK, D)

def backward_tile(slot_vals, coords, grad_rows):
    grad_blocks = grad_rows.reshape(BR, BLOCK, D).astype(jnp.float32)
    gathered = grad_blocks[coords[0]]
    products = jnp.einsum('mrc,mrd->mcd', slot_vals, gathered)
    totals = jnp.zeros((BC, BLOCK, D), jnp.float32).at[coords[1]].add(products)
    return totals.reshape(BC * BLOCK, D)

def reference(features, out_grad, weight, block_values, block_coords, block_counts):
    all_vals = block_values.astype(jnp.float32).reshape(N_ROW, N_COL, MAXB, BLOCK, BLOCK)
    live = jnp.arange(MAXB, dtype=jnp.int32)[None, None, :] < block_counts[:, :, None]
    all_vals = jnp.where(live[:, :, :, None, None], all_vals, jnp.float32(0.0))
    panels = features.reshape(N_COL, BC * BLOCK, D)

    def forward_row(i):

        def advance(totals, j):
            piece = forward_tile(all_vals[i, j], block_coords[i, j], panels[j])
            return (totals + piece.astype(jnp.bfloat16).astype(jnp.float32), None)
        totals, _ = lax.scan(advance, jnp.zeros((BR * BLOCK, D), jnp.float32), jnp.arange(N_COL, dtype=jnp.int32))
        return totals.astype(jnp.bfloat16)
    aggregated = lax.map(forward_row, jnp.arange(N_ROW, dtype=jnp.int32)).reshape(NODES, D)
    pre_act = jnp.dot(aggregated, weight, preferred_element_type=jnp.float32)
    sigmoid_pre = jax.nn.sigmoid(pre_act)
    activations = (pre_act * sigmoid_pre).astype(jnp.bfloat16)
    grad_pre = (out_grad.astype(jnp.float32) * sigmoid_pre * (1.0 + pre_act * (1.0 - sigmoid_pre))).astype(jnp.bfloat16)
    weight_grad = lax.dot_general(aggregated, grad_pre, (((0,), (0,)), ((), ())), preferred_element_type=jnp.float32)
    weight_grad = weight_grad * jnp.float32(1.0 / math.sqrt(NODES))
    grad_agg = lax.dot_general(grad_pre, weight, (((1,), (1,)), ((), ())), preferred_element_type=jnp.float32).astype(jnp.bfloat16)
    grad_rows = grad_agg.reshape(N_ROW, BR * BLOCK, D)

    def backward_col(j):

        def advance(totals, i):
            piece = backward_tile(all_vals[i, j], block_coords[i, j], grad_rows[i])
            return (totals + piece.astype(jnp.bfloat16).astype(jnp.float32), None)
        totals, _ = lax.scan(advance, jnp.zeros((BC * BLOCK, D), jnp.float32), jnp.arange(N_ROW, dtype=jnp.int32))
        return totals.astype(jnp.bfloat16)
    feature_grad = lax.map(backward_col, jnp.arange(N_COL, dtype=jnp.int32)).reshape(NODES, D)
    return (activations, weight_grad, feature_grad)
```

```python
import math

import jax
import jax.numpy as jnp
from jax import lax
from jax.experimental import pallas as pl
from jax.experimental.pallas import tpu as pltpu
from jax.sharding import Mesh, PartitionSpec as P

AXES = ("y_lo", "z", "y_hi", "x", "core")
SIZES = (2, 4, 2, 4, 2)
ROW = ("y_lo", "z")
CHIP = ("y_hi", "x")
COL = ("y_hi", "x", "core")
SIDE = 64
PEERS = 8
OWN = 192
WIDTH = 512


def shift(array, axes, count, step):
    return lax.ppermute(array, axes, [(i, (i + step) % count) for i in range(count)])


def build_kernel(coords, counts, values, dense):
    rows, cols = dense.shape
    per_owner = OWN // SIDE
    me_row = lax.axis_index(ROW)
    me_chip = lax.axis_index(CHIP)
    me_core = lax.axis_index("core")

    @pl.loop(0, rows // SIDE)
    def _(r):
        dense[pl.ds(pl.multiple_of(r * SIDE, SIDE), SIDE), :] = jnp.zeros((SIDE, cols), dense.dtype)

    count = counts[0, 0]
    lane = lax.broadcasted_iota(jnp.int32, (SIDE, 2 * SIDE), 1)

    @pl.loop(0, (count + 15) // 16)
    def _(g):
        group = values[0, 0, pl.ds(pl.multiple_of(g * 16, 16), 16), :]
        pairs = group.astype(jnp.float32).reshape(16, SIDE // 2, 2 * SIDE)
        for k in range(16):
            slot = g * 16 + k
            live = slot < count
            block_row = jnp.where(live, coords[0, 0, 0, slot], 0)
            block_col = jnp.where(live, coords[0, 0, 1, slot], 0)
            owner = block_row // per_owner
            side = (owner + me_core) & 1
            chip = ((owner >> 1) - me_chip) & (PEERS - 1)
            at_row = (side * PEERS + chip) * per_owner + block_row % per_owner
            source = (me_row - block_col // per_owner) & (PEERS - 1)
            at_col = source * per_owner + block_col % per_owner
            odd = (at_col & 1) == 1
            plain = pairs[k]
            turned = pltpu.roll(plain, SIDE, 1)
            block = jnp.concatenate(
                [jnp.where(odd, turned, plain), jnp.where(odd, plain, turned)], axis=0
            ).astype(dense.dtype)
            first = jnp.where(live, (at_col & 1) * SIDE, 4 * SIDE)
            mask = (lane >= first) & (lane < first + SIDE)
            place = dense.at[
                pl.ds(pl.multiple_of(at_row * SIDE, SIDE), SIDE),
                pl.ds(pl.multiple_of((at_col >> 1) * 2 * SIDE, 2 * SIDE), 2 * SIDE),
            ]
            place[...] = jnp.where(mask, block, place[...])


def build(coords, counts, values):
    return pl.pallas_call(
        build_kernel,
        out_shape=jax.ShapeDtypeStruct((2 * PEERS * OWN, PEERS * OWN), jnp.bfloat16),
        in_specs=[pl.BlockSpec(memory_space=pltpu.SMEM)] * 2 + [pl.BlockSpec(memory_space=pltpu.VMEM)],
        out_specs=pl.BlockSpec(memory_space=pltpu.VMEM),
        compiler_params=pltpu.CompilerParams(vmem_limit_bytes=24 << 20),
        cost_estimate=pl.CostEstimate(flops=0, bytes_accessed=30 << 20, transcendentals=0),
        name="build",
    )(coords, counts, values)


def middle_kernel(*refs):
    parts = refs[:PEERS]
    out_grad, weight, activations, grad_agg, local_wgrad = refs[PEERS:]
    total = parts[0][...].astype(jnp.float32)
    for part in parts[1:]:
        total = total + part[...].astype(jnp.float32)
    aggregated = total.astype(jnp.bfloat16)
    at = lax.broadcasted_iota(jnp.int32, (OWN, OWN), 0)
    to = lax.broadcasted_iota(jnp.int32, (OWN, OWN), 1)
    half = SIDE // 2
    turn = jnp.where(
        (at // SIDE == to // SIDE) & (to % SIDE == 2 * (at % half) + (at % SIDE) // half), 1.0, 0.0
    ).astype(jnp.bfloat16)
    w = weight[...]
    pre_act = jnp.dot(aggregated, w, preferred_element_type=jnp.float32)
    sig = jax.nn.sigmoid(pre_act)
    act = (pre_act * sig).astype(jnp.bfloat16)
    activations[...] = lax.dot_general(
        turn, act, (((0,), (0,)), ((), ())), preferred_element_type=jnp.float32
    ).astype(jnp.bfloat16)
    cotangent = jnp.dot(turn, out_grad[...], preferred_element_type=jnp.float32)
    grad_pre = (cotangent * sig * (1.0 + pre_act * (1.0 - sig))).astype(jnp.bfloat16)
    grad_agg[...] = lax.dot_general(
        grad_pre, w, (((1,), (1,)), ((), ())), preferred_element_type=jnp.float32
    ).astype(jnp.bfloat16)
    local_wgrad[...] = lax.dot_general(
        aggregated, grad_pre, (((0,), (0,)), ((), ())), preferred_element_type=jnp.float32
    ).astype(local_wgrad.dtype)


def middle(parts, out_grad, weight):
    vmem = pl.BlockSpec(memory_space=pltpu.VMEM)
    return pl.pallas_call(
        middle_kernel,
        out_shape=(
            jax.ShapeDtypeStruct((OWN, WIDTH), jnp.bfloat16),
            jax.ShapeDtypeStruct((OWN, WIDTH), jnp.bfloat16),
            jax.ShapeDtypeStruct((WIDTH, WIDTH), jnp.bfloat16),
        ),
        in_specs=[vmem] * (PEERS + 2),
        out_specs=(vmem,) * 3,
        compiler_params=pltpu.CompilerParams(vmem_limit_bytes=24 << 20),
        cost_estimate=pl.CostEstimate(flops=2 * 3 * OWN * WIDTH * WIDTH, bytes_accessed=4 << 20, transcendentals=0),
        name="middle",
    )(*parts, out_grad, weight)


def fsum(parts):
    total = parts[0].astype(jnp.float32)
    for part in parts[1:]:
        total = total + part.astype(jnp.float32)
    return total


def per_device(features, out_grad, weight, block_values, block_coords, block_counts):
    panel = [features] + [shift(features, ROW, PEERS, k) for k in range(1, PEERS)]
    dense = build(block_coords, block_counts, block_values)
    panel = jnp.concatenate(panel, axis=0)

    half = PEERS * OWN
    partial_agg = jnp.dot(dense, panel, preferred_element_type=jnp.float32).astype(jnp.bfloat16)
    other = lax.ppermute(partial_agg[half:], "core", [(0, 1), (1, 0)])
    parts = []
    for k in range(PEERS):
        rows = slice(k * OWN, (k + 1) * OWN)
        both = (partial_agg[rows].astype(jnp.float32) + other[rows].astype(jnp.float32)).astype(jnp.bfloat16)
        parts.append(shift(both, CHIP, PEERS, k) if k else both)

    activations, grad_agg, local_wgrad = middle(parts, out_grad, weight)

    mine = [grad_agg] + [shift(grad_agg, CHIP, PEERS, PEERS - p) for p in range(1, PEERS)]
    mine = jnp.concatenate(mine, axis=0)
    theirs = lax.ppermute(mine, "core", [(0, 1), (1, 0)])
    grad_rows = jnp.concatenate([mine, theirs], axis=0)
    partial_grad = lax.dot_general(
        dense, grad_rows, (((0,), (0,)), ((), ())), preferred_element_type=jnp.float32
    ).astype(jnp.bfloat16)
    pieces = []
    for p in range(PEERS):
        piece = partial_grad[p * OWN : (p + 1) * OWN]
        pieces.append(shift(piece, ROW, PEERS, PEERS - p) if p else piece)
    feature_grad = fsum(pieces).astype(jnp.bfloat16)

    slices = lax.all_to_all(local_wgrad.reshape(16, 32, WIDTH), COL, 0, 0)
    summed = fsum([slices[k] for k in range(16)]).astype(jnp.bfloat16)
    rows_sum = [summed] + [shift(summed, ROW, PEERS, k) for k in range(1, PEERS)]
    summed = fsum(rows_sum).astype(jnp.bfloat16)
    weight_grad = lax.all_to_all(jnp.broadcast_to(summed[None], (16, 32, WIDTH)), COL, 0, 0)
    total_nodes = OWN * 128
    weight_grad = weight_grad.reshape(WIDTH, WIDTH).astype(jnp.float32) * jnp.float32(1.0 / math.sqrt(total_nodes))
    return (activations, weight_grad, feature_grad)


def solution(mesh):
    fine = Mesh(mesh.devices.reshape(SIZES), AXES)
    return jax.shard_map(
        per_device,
        mesh=fine,
        in_specs=(
            P(COL + ROW, None),
            P(ROW + COL, None),
            P(),
            P(ROW, COL, None, None),
            P(ROW, COL, None, None),
            P(ROW, COL),
        ),
        out_specs=(P(ROW + COL, None), P(), P(COL + ROW, None)),
        check_vma=False,
    )
```

```python
import math

import jax
import jax.numpy as jnp
from jax import lax
from jax.experimental import pallas as pl
from jax.experimental.pallas import tpu as pltpu
from jax.sharding import Mesh, PartitionSpec as P

AXES = ("y_lo", "z", "y_hi", "x", "core")
SIZES = (2, 4, 2, 4, 2)
ROW = ("y_lo", "z")
CHIP = ("y_hi", "x")
COL = ("y_hi", "x", "core")
SIDE = 64
PEERS = 8
OWN = 192
WIDTH = 512


def build_kernel(coords, counts, values, near, far):
    rows, cols = near.shape
    per_owner = OWN // SIDE
    me_core = lax.axis_index("core")

    @pl.loop(0, rows // SIDE)
    def _(r):
        at = pl.ds(pl.multiple_of(r * SIDE, SIDE), SIDE)
        near[at, :] = jnp.zeros((SIDE, cols), near.dtype)
        far[at, :] = jnp.zeros((SIDE, cols), far.dtype)

    count = counts[0, 0]
    lane = lax.broadcasted_iota(jnp.int32, (SIDE, 2 * SIDE), 1)

    @pl.loop(0, (count + 15) // 16)
    def _(g):
        group = values[0, 0, pl.ds(pl.multiple_of(g * 16, 16), 16), :]
        pairs = group.astype(jnp.float32).reshape(16, SIDE // 2, 2 * SIDE)
        for k in range(16):
            slot = g * 16 + k
            live = slot < count
            block_row = jnp.where(live, coords[0, 0, 0, slot], 0)
            block_col = jnp.where(live, coords[0, 0, 1, slot], 0)
            owner = block_row // per_owner
            is_far = ((owner + me_core) & 1) == 1
            at_row = (owner >> 1) * per_owner + block_row % per_owner
            odd = (block_col & 1) == 1
            plain = pairs[k]
            turned = pltpu.roll(plain, SIDE, 1)
            block = jnp.concatenate(
                [jnp.where(odd, turned, plain), jnp.where(odd, plain, turned)], axis=0
            ).astype(near.dtype)
            first = jnp.where(live, (block_col & 1) * SIDE, 4 * SIDE)
            mask = (lane >= first) & (lane < first + SIDE)
            place = (
                pl.ds(pl.multiple_of(at_row * SIDE, SIDE), SIDE),
                pl.ds(pl.multiple_of((block_col >> 1) * 2 * SIDE, 2 * SIDE), 2 * SIDE),
            )

            @pl.when(is_far)
            def _():
                far[place] = jnp.where(mask, block, far[place])

            @pl.when(jnp.logical_not(is_far))
            def _():
                near[place] = jnp.where(mask, block, near[place])


def build(coords, counts, values):
    tile = jax.ShapeDtypeStruct((PEERS * OWN, PEERS * OWN), jnp.bfloat16)
    return pl.pallas_call(
        build_kernel,
        out_shape=(tile, tile),
        in_specs=[pl.BlockSpec(memory_space=pltpu.SMEM)] * 2 + [pl.BlockSpec(memory_space=pltpu.VMEM)],
        out_specs=(pl.BlockSpec(memory_space=pltpu.VMEM),) * 2,
        compiler_params=pltpu.CompilerParams(vmem_limit_bytes=24 << 20),
        cost_estimate=pl.CostEstimate(flops=0, bytes_accessed=30 << 20, transcendentals=0),
        name="build",
    )(coords, counts, values)


def middle_kernel(parts, out_grad, weight, activations, send, wgrad_near, wgrad_far):
    total = parts[0].astype(jnp.float32)
    for k in range(1, PEERS):
        total = total + parts[k].astype(jnp.float32)
    aggregated = total.astype(jnp.bfloat16)
    at = lax.broadcasted_iota(jnp.int32, (OWN, OWN), 0)
    to = lax.broadcasted_iota(jnp.int32, (OWN, OWN), 1)
    half = SIDE // 2
    turn = jnp.where(
        (at // SIDE == to // SIDE) & (to % SIDE == 2 * (at % half) + (at % SIDE) // half), 1.0, 0.0
    ).astype(jnp.bfloat16)
    w = weight[...]
    pre_act = jnp.dot(aggregated, w, preferred_element_type=jnp.float32)
    sig = jax.nn.sigmoid(pre_act)
    act = (pre_act * sig).astype(jnp.bfloat16)
    activations[...] = lax.dot_general(
        turn, act, (((0,), (0,)), ((), ())), preferred_element_type=jnp.float32
    ).astype(jnp.bfloat16)
    cotangent = jnp.dot(turn, out_grad[...], preferred_element_type=jnp.float32)
    grad_pre = (cotangent * sig * (1.0 + pre_act * (1.0 - sig))).astype(jnp.bfloat16)
    grad_agg = lax.dot_general(
        grad_pre, w, (((1,), (1,)), ((), ())), preferred_element_type=jnp.float32
    ).astype(jnp.bfloat16)
    for k in range(PEERS):
        send[k] = grad_agg
    local = lax.dot_general(
        aggregated, grad_pre, (((0,), (0,)), ((), ())), preferred_element_type=jnp.float32
    ).astype(jnp.bfloat16)
    first, last = local[: WIDTH // 2], local[WIDTH // 2 :]
    core = lax.axis_index("core")
    wgrad_near[...] = jnp.where(core == 0, first, last)
    wgrad_far[...] = jnp.where(core == 0, last, first)


def middle(parts, out_grad, weight):
    vmem = pl.BlockSpec(memory_space=pltpu.VMEM)
    wgrad = jax.ShapeDtypeStruct((WIDTH // 2, WIDTH), jnp.bfloat16)
    return pl.pallas_call(
        middle_kernel,
        out_shape=(
            jax.ShapeDtypeStruct((OWN, WIDTH), jnp.bfloat16),
            jax.ShapeDtypeStruct((PEERS, OWN, WIDTH), jnp.bfloat16),
            wgrad,
            wgrad,
        ),
        in_specs=[vmem] * 3,
        out_specs=(vmem,) * 4,
        compiler_params=pltpu.CompilerParams(vmem_limit_bytes=24 << 20),
        cost_estimate=pl.CostEstimate(flops=2 * 3 * OWN * WIDTH * WIDTH, bytes_accessed=4 << 20, transcendentals=0),
        name="middle",
    )(parts, out_grad, weight)


def fsum(parts):
    total = parts[0].astype(jnp.float32)
    for k in range(1, parts.shape[0]):
        total = total + parts[k].astype(jnp.float32)
    return total


def exchange(parts, axes):
    return lax.all_to_all(parts, axes, 0, 0)


def trade(array, axis, bit=1):
    return lax.ppermute(array, axis, [(i, i ^ bit) for i in range(lax.axis_size(axis))])


def add(a, b):
    return (a.astype(jnp.float32) + b.astype(jnp.float32)).astype(jnp.bfloat16)


def sum_wgrad(near, far):
    total = add(near, trade(far, "core"))
    steps = (("x", 1), ("y_hi", 1), ("x", 2))
    high = [(lax.axis_index(axis) & bit) != 0 for axis, bit in steps]
    for (axis, bit), up in zip(steps, high):
        few = total.shape[0] // 2
        low_part, high_part = total[:few], total[few:]
        sent = jnp.where(up, low_part, high_part)
        kept = jnp.where(up, high_part, low_part)
        total = add(kept, trade(sent, axis, bit))
    for axis, bit in (("z", 1), ("z", 2), ("y_lo", 1)):
        total = add(total, trade(total, axis, bit))
    return total, steps, high


def gather_wgrad(total, steps, high):
    for (axis, bit), up in reversed(list(zip(steps, high))):
        other = trade(total, axis, bit)
        total = jnp.concatenate([jnp.where(up, other, total), jnp.where(up, total, other)], axis=0)
    other = trade(total, "core")
    up = lax.axis_index("core") != 0
    return jnp.concatenate([jnp.where(up, other, total), jnp.where(up, total, other)], axis=0)


def per_device(features, out_grad, weight, block_values, block_coords, block_counts):
    rows = PEERS * OWN
    panel = exchange(jnp.broadcast_to(features[None], (PEERS, OWN, WIDTH)), ROW).reshape(rows, WIDTH)
    near, far = build(block_coords, block_counts, block_values)

    other = jnp.dot(far, panel, preferred_element_type=jnp.float32).astype(jnp.bfloat16)
    other = trade(other, "core")
    own = jnp.dot(near, panel, preferred_element_type=jnp.float32)
    both = (own + other.astype(jnp.float32)).astype(jnp.bfloat16)
    parts = exchange(both.reshape(PEERS, OWN, WIDTH), CHIP)

    activations, send, wgrad_near, wgrad_far = middle(parts, out_grad, weight)

    mine = exchange(send, CHIP).reshape(rows, WIDTH)
    theirs = trade(mine, "core")
    down = (((0,), (0,)), ((), ()))
    partial_grad = lax.dot_general(near, mine, down, preferred_element_type=jnp.float32)
    partial_grad = partial_grad + lax.dot_general(far, theirs, down, preferred_element_type=jnp.float32)
    received = exchange(partial_grad.astype(jnp.bfloat16).reshape(PEERS, OWN, WIDTH), ROW)
    feature_grad = fsum(received).astype(jnp.bfloat16)

    weight_grad = gather_wgrad(*sum_wgrad(wgrad_near, wgrad_far))
    total_nodes = OWN * PEERS * 2 * PEERS
    weight_grad = weight_grad.astype(jnp.float32) * jnp.float32(1.0 / math.sqrt(total_nodes))
    return (activations, weight_grad, feature_grad)


def solution(mesh):
    fine = Mesh(mesh.devices.reshape(SIZES), AXES)
    return jax.shard_map(
        per_device,
        mesh=fine,
        in_specs=(
            P(COL + ROW, None),
            P(ROW + COL, None),
            P(),
            P(ROW, COL, None, None),
            P(ROW, COL, None, None),
            P(ROW, COL),
        ),
        out_specs=(P(ROW + COL, None), P(), P(COL + ROW, None)),
        check_vma=False,
    )
```

```python
import math

import jax
import jax.numpy as jnp
from jax import lax
from jax.experimental import pallas as pl
from jax.experimental.pallas import tpu as pltpu
from jax.sharding import Mesh, PartitionSpec as P

AXES = ("y_lo", "z", "y_hi", "x", "core")
SIZES = (2, 4, 2, 4, 2)
ROW = ("y_lo", "z")
CHIP = ("y_hi", "x")
COL = ("y_hi", "x", "core")
SIDE = 64
PEERS = 8
OWN = 192
WIDTH = 512
ROWS = PEERS * OWN
STEP = 256
RING = 4
PIECE = WIDTH // 2 // RING
LANES = WIDTH // RING


def vmem_call(kernel, outs, name, scratch=(), flops=0, moved=1 << 20, limit=16 << 20):
    vmem = pl.BlockSpec(memory_space=pltpu.VMEM)

    def call(*args):
        return pl.pallas_call(
            kernel,
            out_shape=outs,
            in_specs=[vmem] * len(args),
            out_specs=jax.tree.map(lambda _: vmem, outs),
            scratch_shapes=scratch,
            compiler_params=pltpu.CompilerParams(vmem_limit_bytes=limit),
            cost_estimate=pl.CostEstimate(flops=flops, bytes_accessed=moved, transcendentals=0),
            name=name,
        )(*args)

    return call


def bf16(*shape):
    return jax.ShapeDtypeStruct(shape, jnp.bfloat16)


def build_kernel(coords, counts, values, dense):
    rows, cols = dense.shape
    per_owner = OWN // SIDE
    me_core = lax.axis_index("core")

    @pl.loop(0, rows // SIDE)
    def _(r):
        dense[pl.ds(pl.multiple_of(r * SIDE, SIDE), SIDE), :] = jnp.zeros((SIDE, cols), dense.dtype)

    count = counts[0, 0]
    lane = lax.broadcasted_iota(jnp.int32, (SIDE, 2 * SIDE), 1)

    @pl.loop(0, (count + 15) // 16)
    def _(g):
        group = values[0, 0, pl.ds(pl.multiple_of(g * 16, 16), 16), :]
        pairs = group.astype(jnp.float32).reshape(16, SIDE // 2, 2 * SIDE)
        for k in range(16):
            slot = g * 16 + k
            live = slot < count
            block_row = jnp.where(live, coords[0, 0, 0, slot], 0)
            block_col = jnp.where(live, coords[0, 0, 1, slot], 0)
            owner = block_row // per_owner
            far = (owner + me_core) & 1
            at_row = (far * PEERS + (owner >> 1)) * per_owner + block_row % per_owner
            odd = (block_col & 1) == 1
            plain = pairs[k]
            turned = pltpu.roll(plain, SIDE, 1)
            block = jnp.concatenate(
                [jnp.where(odd, turned, plain), jnp.where(odd, plain, turned)], axis=0
            ).astype(dense.dtype)
            first = jnp.where(live, (block_col & 1) * SIDE, 4 * SIDE)
            mask = (lane >= first) & (lane < first + SIDE)
            place = dense.at[
                pl.ds(pl.multiple_of(at_row * SIDE, SIDE), SIDE),
                pl.ds(pl.multiple_of((block_col >> 1) * 2 * SIDE, 2 * SIDE), 2 * SIDE),
            ]
            place[...] = jnp.where(mask, block, place[...])


def build(coords, counts, values):
    return pl.pallas_call(
        build_kernel,
        out_shape=bf16(2 * ROWS, ROWS),
        in_specs=[pl.BlockSpec(memory_space=pltpu.SMEM)] * 2 + [pl.BlockSpec(memory_space=pltpu.VMEM)],
        out_specs=pl.BlockSpec(memory_space=pltpu.VMEM),
        compiler_params=pltpu.CompilerParams(vmem_limit_bytes=16 << 20),
        cost_estimate=pl.CostEstimate(flops=0, bytes_accessed=30 << 20, transcendentals=0),
        name="build",
    )(coords, counts, values)


def over_rows(a, b):
    return lax.dot_general(a, b, (((0,), (0,)), ((), ())), preferred_element_type=jnp.float32)


def down_kernel(dense, panel, out):
    out[...] = jnp.dot(dense[...], panel[...], preferred_element_type=jnp.float32).astype(out.dtype)


def down_add_kernel(dense, panel, other, *rest):
    out = rest[-1]
    own = jnp.dot(dense[...], panel[...], preferred_element_type=jnp.float32)
    out[...] = (own + other[...].astype(jnp.float32)).astype(out.dtype)


def up_kernel(dense, rows, out):
    out[...] = over_rows(dense[...], rows[...]).astype(out.dtype)


def up_add_kernel(dense, rows, other, out):
    out[...] = (over_rows(dense[...], rows[...]) + other[...]).astype(out.dtype)


def product(kernel, name, steps, dense_spec, extra_specs, out_spec, out_shape, *args, aliases={}):
    return pl.pallas_call(
        kernel,
        grid=(steps,),
        out_shape=out_shape,
        in_specs=[dense_spec, pl.BlockSpec((ROWS, WIDTH), lambda r: (0, 0))] + extra_specs,
        out_specs=out_spec,
        input_output_aliases=aliases,
        compiler_params=pltpu.CompilerParams(vmem_limit_bytes=56 << 20),
        cost_estimate=pl.CostEstimate(
            flops=2 * STEP * steps * ROWS * WIDTH, bytes_accessed=8 << 20, transcendentals=0
        ),
        name=name,
    )(*args)


def strip(first=0):
    return pl.BlockSpec((STEP, WIDTH), lambda r: (first + r, 0))


def down_both(dense, panel):
    all_steps = ROWS // STEP
    runs = ((0, all_steps // 2), (all_steps // 2, all_steps - all_steps // 2))

    def tile(first):
        return pl.BlockSpec((STEP, ROWS), lambda r: (first + r, 0))

    others = []
    for n, (first, steps) in enumerate(runs):
        far = product(
            down_kernel, f"down_far_{n}", steps, tile(all_steps + first), [], strip(),
            bf16(steps * STEP, WIDTH), dense, panel,
        )
        others.append(trade(far, "core"))
    out = []
    for n, (first, steps) in enumerate(runs):
        out = product(
            down_add_kernel, f"down_near_{n}", steps, tile(first),
            [strip()] + [pl.BlockSpec(memory_space=pl.ANY)] * (n > 0), strip(first),
            bf16(ROWS, WIDTH), dense, panel, others[n], *([out] if n else []),
            aliases={3: 0} if n else {},
        )
    return out


def up_both(dense, mine, theirs):
    def tile(half):
        return pl.BlockSpec((ROWS, STEP), lambda r: (half, r))

    steps = ROWS // STEP
    near = product(
        up_kernel, "up_near", steps, tile(0), [], strip(),
        jax.ShapeDtypeStruct((ROWS, WIDTH), jnp.float32), dense, mine,
    )
    return product(up_add_kernel, "up_far", steps, tile(1), [strip()], strip(), bf16(ROWS, WIDTH), dense, theirs, near)


def middle_kernel(parts, out_grad, weight, activations, send, wgrad_near, wgrad_far, local):
    total = parts[0].astype(jnp.float32)
    for k in range(1, PEERS):
        total = total + parts[k].astype(jnp.float32)
    aggregated = total.astype(jnp.bfloat16)
    at = lax.broadcasted_iota(jnp.int32, (OWN, OWN), 0)
    to = lax.broadcasted_iota(jnp.int32, (OWN, OWN), 1)
    half = SIDE // 2
    turn = jnp.where(
        (at // SIDE == to // SIDE) & (to % SIDE == 2 * (at % half) + (at % SIDE) // half), 1.0, 0.0
    ).astype(jnp.bfloat16)
    w = weight[...]
    pre_act = jnp.dot(aggregated, w, preferred_element_type=jnp.float32)
    sig = jax.nn.sigmoid(pre_act)
    act = (pre_act * sig).astype(jnp.bfloat16)
    activations[...] = over_rows(turn, act).astype(jnp.bfloat16)
    cotangent = jnp.dot(turn, out_grad[...], preferred_element_type=jnp.float32)
    grad_pre = (cotangent * sig * (1.0 + pre_act * (1.0 - sig))).astype(jnp.bfloat16)
    grad_agg = lax.dot_general(
        grad_pre, w, (((1,), (1,)), ((), ())), preferred_element_type=jnp.float32
    ).astype(jnp.bfloat16)
    for k in range(PEERS):
        send[k] = grad_agg
    local[...] = over_rows(aggregated, grad_pre).astype(jnp.bfloat16)
    core = lax.axis_index("core")
    for k in range(RING):
        for g in range(RING):
            for out, half_of in ((wgrad_near, core), (wgrad_far, 1 - core)):
                rows, cols = wgrad_place(half_of, k, g)
                out[k * PIECE : (k + 1) * PIECE, g * LANES : (g + 1) * LANES] = local[rows, cols]


def wgrad_place(half_of, k, g):
    row = half_of * (WIDTH // 2) + ((lax.axis_index("z") + k) & (RING - 1)) * PIECE
    col = ((lax.axis_index("x") + g) & (RING - 1)) * LANES
    return pl.ds(pl.multiple_of(row, PIECE), PIECE), pl.ds(pl.multiple_of(col, LANES), LANES)


def add(a, b):
    return (a.astype(jnp.float32) + b.astype(jnp.float32)).astype(jnp.bfloat16)


def pair_kernel(near, other, *outs):
    for k, out in enumerate(outs):
        rows = slice(k * PIECE, (k + 1) * PIECE)
        out[...] = add(near[rows], other[rows])


def sum_kernel(*refs):
    *parts, out = refs
    total = parts[0][...].astype(jnp.float32)
    for part in parts[1:]:
        total = total + part[...].astype(jnp.float32)
    out[...] = total.astype(out.dtype)


def square_kernel(a, b, c, d, out):
    first = a[...].astype(jnp.float32) + b[...].astype(jnp.float32)
    out[...] = (first + (c[...].astype(jnp.float32) + d[...].astype(jnp.float32))).astype(out.dtype)


def turn_kernel(*refs):
    pieces, outs = refs[:RING], refs[RING:]
    for g, out in enumerate(outs):
        for k, piece in enumerate(pieces):
            out[k * PIECE : (k + 1) * PIECE] = piece[:, g * LANES : (g + 1) * LANES]


def join_kernel(*refs):
    *parts, out = refs
    for g, part in enumerate(parts):
        out[:, g * LANES : (g + 1) * LANES] = part[...]


def place_kernel(mine, theirs, out):
    core = lax.axis_index("core")
    scale = 1.0 / math.sqrt(OWN * PEERS * 2 * PEERS)
    for k in range(RING):
        for g in range(RING):
            for part, half_of in ((mine, core), (theirs, 1 - core)):
                value = part[k * PIECE : (k + 1) * PIECE, g * LANES : (g + 1) * LANES].astype(jnp.float32)
                rows, cols = wgrad_place(half_of, k, g)
                out[rows, cols] = value * jnp.float32(scale)


def spread_kernel(array, out, sems):
    copies = [pltpu.make_async_copy(array, out.at[k], sems.at[k]) for k in range(PEERS)]
    for copy in copies:
        copy.start()
    for copy in copies:
        copy.wait()


def spread(array):
    anywhere = pl.BlockSpec(memory_space=pl.ANY)
    return pl.pallas_call(
        spread_kernel,
        out_shape=jax.ShapeDtypeStruct((PEERS,) + array.shape, array.dtype),
        in_specs=[anywhere],
        out_specs=anywhere,
        scratch_shapes=[pltpu.SemaphoreType.DMA((PEERS,))],
        cost_estimate=pl.CostEstimate(flops=0, bytes_accessed=2 << 20, transcendentals=0),
        name="spread",
    )(array)


def exchange(parts, axes):
    return lax.all_to_all(parts, axes, 0, 0)


def trade(array, axes, bits=1):
    return lax.ppermute(array, axes, [(i, i ^ bits) for i in range(lax.axis_size(axes))])


def scatter_ring(pieces, axis, name):
    arrived = [pieces[0]]
    for k in range(1, RING):
        arrived.append(lax.ppermute(pieces[k], axis, [(i, (i + k) % RING) for i in range(RING)]))
    return vmem_call(sum_kernel, bf16(*pieces[0].shape), name)(*arrived)


def gather_ring(piece, axis):
    pieces = [piece]
    for k in range(1, RING):
        pieces.append(lax.ppermute(piece, axis, [(i, (i - k) % RING) for i in range(RING)]))
    return pieces


def per_device(features, out_grad, weight, block_values, block_coords, block_counts):
    panel = exchange(spread(features), ROW).reshape(ROWS, WIDTH)
    dense = build(block_coords, block_counts, block_values)

    parts = exchange(down_both(dense, panel).reshape(PEERS, OWN, WIDTH), CHIP)

    half = bf16(WIDTH // 2, WIDTH)
    activations, send, wgrad_near, wgrad_far = vmem_call(
        middle_kernel,
        (bf16(OWN, WIDTH), bf16(PEERS, OWN, WIDTH), half, half),
        "middle",
        scratch=[pltpu.VMEM((WIDTH, WIDTH), jnp.bfloat16)],
        flops=2 * 3 * OWN * WIDTH * WIDTH,
    )(parts, out_grad, weight)

    mine = exchange(send, CHIP).reshape(ROWS, WIDTH)

    piece = bf16(PIECE, WIDTH)
    pieces = vmem_call(pair_kernel, (piece,) * RING, "pair")(wgrad_near, trade(wgrad_far, "core"))
    summed = scatter_ring(pieces, "z", "sum_z")
    ys = ("y_lo", "y_hi")
    summed = vmem_call(square_kernel, piece, "sum_y")(
        summed, trade(summed, ys, 1), trade(summed, ys, 2), trade(summed, ys, 3)
    )
    summed, mine = lax.optimization_barrier((summed, mine))
    pieces = gather_ring(summed, "z")
    theirs = trade(mine, "core")
    partial_grad = up_both(dense, mine, theirs)
    partial_grad, *pieces = lax.optimization_barrier((partial_grad, *pieces))
    received = exchange(partial_grad.reshape(PEERS, OWN, WIDTH), ROW)

    column = bf16(WIDTH // 2, LANES)
    columns = vmem_call(turn_kernel, (column,) * RING, "turn")(*pieces)
    summed = scatter_ring(columns, "x", "sum_x")
    columns = gather_ring(summed, "x")
    own_half = vmem_call(join_kernel, half, "join")(*columns)
    weight_grad = vmem_call(place_kernel, jax.ShapeDtypeStruct((WIDTH, WIDTH), jnp.float32), "place")(
        own_half, trade(own_half, "core")
    )

    total = received[0].astype(jnp.float32)
    for k in range(1, PEERS):
        total = total + received[k].astype(jnp.float32)
    feature_grad = total.astype(jnp.bfloat16)
    return (activations, weight_grad, feature_grad)


def solution(mesh):
    fine = Mesh(mesh.devices.reshape(SIZES), AXES)
    return jax.shard_map(
        per_device,
        mesh=fine,
        in_specs=(
            P(COL + ROW, None),
            P(ROW + COL, None),
            P(),
            P(ROW, COL, None, None),
            P(ROW, COL, None, None),
            P(ROW, COL),
        ),
        out_specs=(P(ROW + COL, None), P(), P(COL + ROW, None)),
        check_vma=False,
    )
```

```python
import functools
import math

import jax
import jax.numpy as jnp
from jax import lax
from jax.experimental import pallas as pl
from jax.experimental.pallas import tpu as pltpu
from jax.sharding import Mesh, PartitionSpec as P

AXES = ("y_lo", "z", "y_hi", "x", "core")
SIZES = (2, 4, 2, 4, 2)
ROW = ("y_lo", "z")
CHIP = ("y_hi", "x")
COL = ("y_hi", "x", "core")
SIDE = 64
PEERS = 8
OWN = 192
WIDTH = 512
ROWS = PEERS * OWN
STEP = 256
RING = 4
PIECE = WIDTH // 2 // RING
LANES = WIDTH // RING


def vmem_call(kernel, outs, name, scratch=(), flops=0, moved=1 << 20, limit=16 << 20, aliases={}):
    vmem = pl.BlockSpec(memory_space=pltpu.VMEM)

    def call(*args):
        return pl.pallas_call(
            kernel,
            out_shape=outs,
            in_specs=[vmem] * len(args),
            out_specs=jax.tree.map(lambda _: vmem, outs),
            scratch_shapes=scratch,
            input_output_aliases=aliases,
            compiler_params=pltpu.CompilerParams(vmem_limit_bytes=limit),
            cost_estimate=pl.CostEstimate(flops=flops, bytes_accessed=moved, transcendentals=0),
            name=name,
        )(*args)

    return call


def bf16(*shape):
    return jax.ShapeDtypeStruct(shape, jnp.bfloat16)


def build_kernel(coords, counts, values, near, far, dense, sems):
    rows, cols = dense.shape
    per_owner = OWN // SIDE
    me_core = lax.axis_index("core")

    @pl.loop(0, rows // SIDE)
    def _(r):
        dense[pl.ds(pl.multiple_of(r * SIDE, SIDE), SIDE), :] = jnp.zeros((SIDE, cols), dense.dtype)

    count = counts[0, 0]
    lane = lax.broadcasted_iota(jnp.int32, (SIDE, 2 * SIDE), 1)

    @pl.loop(0, (count + 15) // 16)
    def _(g):
        group = values[0, 0, pl.ds(pl.multiple_of(g * 16, 16), 16), :]
        pairs = group.astype(jnp.float32).reshape(16, SIDE // 2, 2 * SIDE)
        for k in range(16):
            slot = g * 16 + k
            live = slot < count
            block_row = jnp.where(live, coords[0, 0, 0, slot], 0)
            block_col = jnp.where(live, coords[0, 0, 1, slot], 0)
            owner = block_row // per_owner
            half = (owner + me_core) & 1
            at_row = (half * PEERS + (owner >> 1)) * per_owner + block_row % per_owner
            odd = (block_col & 1) == 1
            plain = pairs[k]
            turned = pltpu.roll(plain, SIDE, 1)
            block = jnp.concatenate(
                [jnp.where(odd, turned, plain), jnp.where(odd, plain, turned)], axis=0
            ).astype(dense.dtype)
            first = jnp.where(live, (block_col & 1) * SIDE, 4 * SIDE)
            mask = (lane >= first) & (lane < first + SIDE)
            place = dense.at[
                pl.ds(pl.multiple_of(at_row * SIDE, SIDE), SIDE),
                pl.ds(pl.multiple_of((block_col >> 1) * 2 * SIDE, 2 * SIDE), 2 * SIDE),
            ]
            place[...] = jnp.where(mask, block, place[...])

    copies = [
        pltpu.make_async_copy(dense.at[pl.ds(0, ROWS)], near, sems.at[0]),
        pltpu.make_async_copy(dense.at[pl.ds(ROWS, ROWS)], far, sems.at[1]),
    ]
    for copy in copies:
        copy.start()
    for copy in copies:
        copy.wait()


def build(coords, counts, values):
    anywhere = pl.BlockSpec(memory_space=pltpu.HBM)
    return pl.pallas_call(
        build_kernel,
        out_shape=(bf16(ROWS, ROWS),) * 2,
        in_specs=[pl.BlockSpec(memory_space=pltpu.SMEM)] * 2 + [pl.BlockSpec(memory_space=pltpu.VMEM)],
        out_specs=(anywhere,) * 2,
        scratch_shapes=[pltpu.VMEM((2 * ROWS, ROWS), jnp.bfloat16), pltpu.SemaphoreType.DMA((2,))],
        compiler_params=pltpu.CompilerParams(vmem_limit_bytes=24 << 20),
        cost_estimate=pl.CostEstimate(flops=0, bytes_accessed=30 << 20, transcendentals=0),
        name="build",
    )(coords, counts, values)


def over_rows(a, b):
    return lax.dot_general(a, b, (((0,), (0,)), ((), ())), preferred_element_type=jnp.float32)


def down_kernel(first, count, tile, panel, out):
    for r in range(0, count, STEP):
        rows = slice(first + r, first + r + STEP)
        out[r : r + STEP] = jnp.dot(tile[rows], panel[...], preferred_element_type=jnp.float32).astype(out.dtype)


def down_add_kernel(first, count, tile, panel, other, *rest):
    out = rest[-1]
    for r in range(0, count, STEP):
        rows = slice(first + r, first + r + STEP)
        own = jnp.dot(tile[rows], panel[...], preferred_element_type=jnp.float32)
        out[rows] = (own + other[r : r + STEP].astype(jnp.float32)).astype(out.dtype)


def up_kernel(tile, rows, out):
    for r in range(0, ROWS, STEP):
        out[r : r + STEP] = over_rows(tile[:, r : r + STEP], rows[...])


def up_add_kernel(tile, rows, other, out):
    for r in range(0, ROWS, STEP):
        total = over_rows(tile[:, r : r + STEP], rows[...]) + other[r : r + STEP]
        out[r : r + STEP] = total.astype(out.dtype)


def down_both(near, far, panel):
    count = ROWS // 2
    work = 2 * count * ROWS * WIDTH
    others = []
    for n in range(2):
        kernel = functools.partial(down_kernel, n * count, count)
        others.append(trade(vmem_call(kernel, bf16(count, WIDTH), f"down_far_{n}", flops=work)(far, panel), "core"))
    out = []
    for n in range(2):
        kernel = functools.partial(down_add_kernel, n * count, count)
        out = vmem_call(
            kernel, bf16(ROWS, WIDTH), f"down_near_{n}", flops=work, aliases={3: 0} if n else {}
        )(near, panel, others[n], *([out] if n else []))
    return out


def up_both(near, far, mine, theirs):
    work = 2 * ROWS * ROWS * WIDTH
    own = vmem_call(up_kernel, jax.ShapeDtypeStruct((ROWS, WIDTH), jnp.float32), "up_near", flops=work)(near, mine)
    return vmem_call(up_add_kernel, bf16(ROWS, WIDTH), "up_far", flops=work)(far, theirs, own)


def middle_kernel(parts, out_grad, weight, activations, send, wgrad_near, wgrad_far, local):
    total = parts[0].astype(jnp.float32)
    for k in range(1, PEERS):
        total = total + parts[k].astype(jnp.float32)
    aggregated = total.astype(jnp.bfloat16)
    at = lax.broadcasted_iota(jnp.int32, (OWN, OWN), 0)
    to = lax.broadcasted_iota(jnp.int32, (OWN, OWN), 1)
    half = SIDE // 2
    turn = jnp.where(
        (at // SIDE == to // SIDE) & (to % SIDE == 2 * (at % half) + (at % SIDE) // half), 1.0, 0.0
    ).astype(jnp.bfloat16)
    w = weight[...]
    pre_act = jnp.dot(aggregated, w, preferred_element_type=jnp.float32)
    sig = jax.nn.sigmoid(pre_act)
    act = (pre_act * sig).astype(jnp.bfloat16)
    activations[...] = over_rows(turn, act).astype(jnp.bfloat16)
    cotangent = jnp.dot(turn, out_grad[...], preferred_element_type=jnp.float32)
    grad_pre = (cotangent * sig * (1.0 + pre_act * (1.0 - sig))).astype(jnp.bfloat16)
    grad_agg = lax.dot_general(
        grad_pre, w, (((1,), (1,)), ((), ())), preferred_element_type=jnp.float32
    ).astype(jnp.bfloat16)
    for k in range(PEERS):
        send[k] = grad_agg
    local[...] = over_rows(aggregated, grad_pre).astype(jnp.bfloat16)
    core = lax.axis_index("core")
    for k in range(RING):
        for g in range(RING):
            for out, half_of in ((wgrad_near, core), (wgrad_far, 1 - core)):
                rows, cols = wgrad_place(half_of, k, g)
                out[k * PIECE : (k + 1) * PIECE, g * LANES : (g + 1) * LANES] = local[rows, cols]


def wgrad_place(half_of, k, g):
    row = half_of * (WIDTH // 2) + ((lax.axis_index("z") + k) & (RING - 1)) * PIECE
    col = ((lax.axis_index("x") + g) & (RING - 1)) * LANES
    return pl.ds(pl.multiple_of(row, PIECE), PIECE), pl.ds(pl.multiple_of(col, LANES), LANES)


def add(a, b):
    return (a.astype(jnp.float32) + b.astype(jnp.float32)).astype(jnp.bfloat16)


def pair_kernel(near, other, *outs):
    for k, out in enumerate(outs):
        rows = slice(k * PIECE, (k + 1) * PIECE)
        out[...] = add(near[rows], other[rows])


def sum_kernel(*refs):
    *parts, out = refs
    total = parts[0][...].astype(jnp.float32)
    for part in parts[1:]:
        total = total + part[...].astype(jnp.float32)
    out[...] = total.astype(out.dtype)


def square_kernel(a, b, c, d, out):
    first = a[...].astype(jnp.float32) + b[...].astype(jnp.float32)
    out[...] = (first + (c[...].astype(jnp.float32) + d[...].astype(jnp.float32))).astype(out.dtype)


def turn_kernel(*refs):
    pieces, outs = refs[:RING], refs[RING:]
    for g, out in enumerate(outs):
        for k, piece in enumerate(pieces):
            out[k * PIECE : (k + 1) * PIECE] = piece[:, g * LANES : (g + 1) * LANES]


def join_kernel(*refs):
    *parts, out = refs
    for g, part in enumerate(parts):
        out[:, g * LANES : (g + 1) * LANES] = part[...]


def place_kernel(mine, theirs, out):
    core = lax.axis_index("core")
    scale = 1.0 / math.sqrt(OWN * PEERS * 2 * PEERS)
    for k in range(RING):
        for g in range(RING):
            for part, half_of in ((mine, core), (theirs, 1 - core)):
                value = part[k * PIECE : (k + 1) * PIECE, g * LANES : (g + 1) * LANES].astype(jnp.float32)
                rows, cols = wgrad_place(half_of, k, g)
                out[rows, cols] = value * jnp.float32(scale)


def exchange(parts, axes):
    return lax.all_to_all(parts, axes, 0, 0)


def trade(array, axes, bits=1):
    return lax.ppermute(array, axes, [(i, i ^ bits) for i in range(lax.axis_size(axes))])


def scatter_ring(pieces, axis, name):
    arrived = [pieces[0]]
    for k in range(1, RING):
        arrived.append(lax.ppermute(pieces[k], axis, [(i, (i + k) % RING) for i in range(RING)]))
    return vmem_call(sum_kernel, bf16(*pieces[0].shape), name)(*arrived)


def gather_ring(piece, axis):
    pieces = [piece]
    for k in range(1, RING):
        pieces.append(lax.ppermute(piece, axis, [(i, (i - k) % RING) for i in range(RING)]))
    return pieces


def per_device(features, out_grad, weight, block_values, block_coords, block_counts):
    panel = exchange(jnp.broadcast_to(features[None], (PEERS, OWN, WIDTH)), ROW).reshape(ROWS, WIDTH)
    near, far = build(block_coords, block_counts, block_values)

    parts = exchange(down_both(near, far, panel).reshape(PEERS, OWN, WIDTH), CHIP)

    half = bf16(WIDTH // 2, WIDTH)
    activations, send, wgrad_near, wgrad_far = vmem_call(
        middle_kernel,
        (bf16(OWN, WIDTH), bf16(PEERS, OWN, WIDTH), half, half),
        "middle",
        scratch=[pltpu.VMEM((WIDTH, WIDTH), jnp.bfloat16)],
        flops=2 * 3 * OWN * WIDTH * WIDTH,
    )(parts, out_grad, weight)

    mine = exchange(send, CHIP).reshape(ROWS, WIDTH)

    piece = bf16(PIECE, WIDTH)
    pieces = vmem_call(pair_kernel, (piece,) * RING, "pair")(wgrad_near, trade(wgrad_far, "core"))
    summed = scatter_ring(pieces, "z", "sum_z")
    ys = ("y_lo", "y_hi")
    summed = vmem_call(square_kernel, piece, "sum_y")(
        summed, trade(summed, ys, 1), trade(summed, ys, 2), trade(summed, ys, 3)
    )
    summed, mine = lax.optimization_barrier((summed, mine))
    pieces = gather_ring(summed, "z")
    theirs = trade(mine, "core")
    partial_grad = up_both(near, far, mine, theirs)
    partial_grad, *pieces = lax.optimization_barrier((partial_grad, *pieces))
    received = exchange(partial_grad.reshape(PEERS, OWN, WIDTH), ROW)

    column = bf16(WIDTH // 2, LANES)
    columns = vmem_call(turn_kernel, (column,) * RING, "turn")(*pieces)
    summed = scatter_ring(columns, "x", "sum_x")
    columns = gather_ring(summed, "x")
    own_half = vmem_call(join_kernel, half, "join")(*columns)
    weight_grad = vmem_call(place_kernel, jax.ShapeDtypeStruct((WIDTH, WIDTH), jnp.float32), "place")(
        own_half, trade(own_half, "core")
    )

    total = received[0].astype(jnp.float32)
    for k in range(1, PEERS):
        total = total + received[k].astype(jnp.float32)
    feature_grad = total.astype(jnp.bfloat16)
    return (activations, weight_grad, feature_grad)


def solution(mesh):
    fine = Mesh(mesh.devices.reshape(SIZES), AXES)
    return jax.shard_map(
        per_device,
        mesh=fine,
        in_specs=(
            P(COL + ROW, None),
            P(ROW + COL, None),
            P(),
            P(ROW, COL, None, None),
            P(ROW, COL, None, None),
            P(ROW, COL),
        ),
        out_specs=(P(ROW + COL, None), P(), P(COL + ROW, None)),
        check_vma=False,
    )
```

```python
import functools
import math

import jax
import jax.numpy as jnp
from jax import lax
from jax.experimental import pallas as pl
from jax.experimental.pallas import tpu as pltpu
from jax.sharding import Mesh, PartitionSpec as P

AXES = ("y_lo", "z", "y_hi", "x", "core")
SIZES = (2, 4, 2, 4, 2)
ROW = ("y_lo", "z")
CHIP = ("y_hi", "x")
COL = ("y_hi", "x", "core")
SIDE = 64
PEERS = 8
OWN = 192
WIDTH = 512
ROWS = PEERS * OWN
STEP = 256
RING = 4
PIECE = WIDTH // 2 // RING
LANES = WIDTH // RING


def vmem_call(kernel, outs, name, scratch=(), flops=0, moved=1 << 20, limit=16 << 20, aliases={}):
    vmem = pl.BlockSpec(memory_space=pltpu.VMEM)

    def call(*args):
        return pl.pallas_call(
            kernel,
            out_shape=outs,
            in_specs=[vmem] * len(args),
            out_specs=jax.tree.map(lambda _: vmem, outs),
            scratch_shapes=scratch,
            input_output_aliases=aliases,
            compiler_params=pltpu.CompilerParams(vmem_limit_bytes=limit),
            cost_estimate=pl.CostEstimate(flops=flops, bytes_accessed=moved, transcendentals=0),
            name=name,
        )(*args)

    return call


def bf16(*shape):
    return jax.ShapeDtypeStruct(shape, jnp.bfloat16)


def relative(owner, slow, fast):
    apart = (owner >> 2) ^ lax.axis_index(slow)
    ahead = ((owner & (RING - 1)) - lax.axis_index(fast)) & (RING - 1)
    return apart * RING + ahead


def absolute(place, slow, fast):
    apart, ahead = divmod(place, RING)
    return (lax.axis_index(slow) ^ apart) * RING + ((lax.axis_index(fast) + ahead) & (RING - 1))


def build_kernel(coords, counts, values, dense):
    rows, cols = dense.shape
    per_owner = OWN // SIDE
    me_core = lax.axis_index("core")

    @pl.loop(0, rows // SIDE)
    def _(r):
        dense[pl.ds(pl.multiple_of(r * SIDE, SIDE), SIDE), :] = jnp.zeros((SIDE, cols), dense.dtype)

    count = counts[0, 0]
    lane = lax.broadcasted_iota(jnp.int32, (SIDE, 2 * SIDE), 1)

    @pl.loop(0, (count + 15) // 16)
    def _(g):
        group = values[0, 0, pl.ds(pl.multiple_of(g * 16, 16), 16), :]
        pairs = group.astype(jnp.float32).reshape(16, SIDE // 2, 2 * SIDE)
        for k in range(16):
            slot = g * 16 + k
            live = slot < count
            block_row = jnp.where(live, coords[0, 0, 0, slot], 0)
            block_col = jnp.where(live, coords[0, 0, 1, slot], 0)
            owner = block_row // per_owner
            half = (owner + me_core) & 1
            at_row = (half * PEERS + relative(owner >> 1, *CHIP)) * per_owner + block_row % per_owner
            at_col = relative(block_col // per_owner, *ROW) * per_owner + block_col % per_owner
            odd = (at_col & 1) == 1
            plain = pairs[k]
            turned = pltpu.roll(plain, SIDE, 1)
            block = jnp.concatenate(
                [jnp.where(odd, turned, plain), jnp.where(odd, plain, turned)], axis=0
            ).astype(dense.dtype)
            first = jnp.where(live, (at_col & 1) * SIDE, 4 * SIDE)
            mask = (lane >= first) & (lane < first + SIDE)
            place = dense.at[
                pl.ds(pl.multiple_of(at_row * SIDE, SIDE), SIDE),
                pl.ds(pl.multiple_of((at_col >> 1) * 2 * SIDE, 2 * SIDE), 2 * SIDE),
            ]
            place[...] = jnp.where(mask, block, place[...])


def build(coords, counts, values):
    return pl.pallas_call(
        build_kernel,
        out_shape=bf16(2 * ROWS, ROWS),
        in_specs=[pl.BlockSpec(memory_space=pltpu.SMEM)] * 2 + [pl.BlockSpec(memory_space=pltpu.VMEM)],
        out_specs=pl.BlockSpec(memory_space=pltpu.VMEM),
        compiler_params=pltpu.CompilerParams(vmem_limit_bytes=16 << 20),
        cost_estimate=pl.CostEstimate(flops=0, bytes_accessed=30 << 20, transcendentals=0),
        name="build",
    )(coords, counts, values)


def over_rows(a, b):
    return lax.dot_general(a, b, (((0,), (0,)), ((), ())), preferred_element_type=jnp.float32)


def down_kernel(first, count, dense, panel, out):
    for r in range(0, count, STEP):
        rows = slice(ROWS + first + r, ROWS + first + r + STEP)
        out[r : r + STEP] = jnp.dot(dense[rows], panel[...], preferred_element_type=jnp.float32).astype(out.dtype)


def store(out, place, axes, value):
    for k in range(2):
        out[absolute(place + k, *axes)] = value[k * OWN : (k + 1) * OWN].astype(out.dtype)


def down_add_kernel(first, count, dense, panel, other, *rest):
    for r in range(0, count, 2 * OWN):
        own = jnp.dot(dense[first + r : first + r + 2 * OWN], panel[...], preferred_element_type=jnp.float32)
        store(rest[-1], (first + r) // OWN, CHIP, own + other[r : r + 2 * OWN].astype(jnp.float32))


def up_kernel(dense, rows, out):
    for r in range(0, ROWS, STEP):
        out[r : r + STEP] = over_rows(dense[:ROWS, r : r + STEP], rows[...])


def up_add_kernel(dense, rows, other, out):
    for r in range(0, ROWS, 2 * OWN):
        total = over_rows(dense[ROWS:, r : r + 2 * OWN], rows[...]) + other[r : r + 2 * OWN]
        store(out, r // OWN, ROW, total)


def down_both(dense, panel):
    count = ROWS // 2
    work = 2 * count * ROWS * WIDTH
    others = []
    for n in range(2):
        kernel = functools.partial(down_kernel, n * count, count)
        others.append(trade(vmem_call(kernel, bf16(count, WIDTH), f"down_far_{n}", flops=work)(dense, panel), "core"))
    out = []
    for n in range(2):
        kernel = functools.partial(down_add_kernel, n * count, count)
        out = vmem_call(
            kernel, bf16(PEERS, OWN, WIDTH), f"down_near_{n}", flops=work, aliases={3: 0} if n else {}
        )(dense, panel, others[n], *([out] if n else []))
    return out


def up_both(dense, mine, theirs):
    work = 2 * ROWS * ROWS * WIDTH
    own = vmem_call(up_kernel, jax.ShapeDtypeStruct((ROWS, WIDTH), jnp.float32), "up_near", flops=work)(dense, mine)
    return vmem_call(up_add_kernel, bf16(PEERS, OWN, WIDTH), "up_far", flops=work)(dense, theirs, own)


def middle_kernel(parts, out_grad, weight, activations, send, wgrad_near, wgrad_far, local):
    total = parts[0].astype(jnp.float32)
    for k in range(1, PEERS):
        total = total + parts[k].astype(jnp.float32)
    aggregated = total.astype(jnp.bfloat16)
    at = lax.broadcasted_iota(jnp.int32, (OWN, OWN), 0)
    to = lax.broadcasted_iota(jnp.int32, (OWN, OWN), 1)
    half = SIDE // 2
    turn = jnp.where(
        (at // SIDE == to // SIDE) & (to % SIDE == 2 * (at % half) + (at % SIDE) // half), 1.0, 0.0
    ).astype(jnp.bfloat16)
    w = weight[...]
    pre_act = jnp.dot(aggregated, w, preferred_element_type=jnp.float32)
    sig = jax.nn.sigmoid(pre_act)
    act = (pre_act * sig).astype(jnp.bfloat16)
    activations[...] = over_rows(turn, act).astype(jnp.bfloat16)
    cotangent = jnp.dot(turn, out_grad[...], preferred_element_type=jnp.float32)
    grad_pre = (cotangent * sig * (1.0 + pre_act * (1.0 - sig))).astype(jnp.bfloat16)
    grad_agg = lax.dot_general(
        grad_pre, w, (((1,), (1,)), ((), ())), preferred_element_type=jnp.float32
    ).astype(jnp.bfloat16)
    send[...] = grad_agg
    local[...] = over_rows(aggregated, grad_pre).astype(jnp.bfloat16)
    core = lax.axis_index("core")
    for k in range(RING):
        for g in range(RING):
            for out, half_of in ((wgrad_near, core), (wgrad_far, 1 - core)):
                rows, cols = wgrad_place(half_of, k, g)
                out[k * PIECE : (k + 1) * PIECE, g * LANES : (g + 1) * LANES] = local[rows, cols]


def wgrad_place(half_of, k, g):
    row = half_of * (WIDTH // 2) + ((lax.axis_index("z") + k) & (RING - 1)) * PIECE
    col = ((lax.axis_index("x") + g) & (RING - 1)) * LANES
    return pl.ds(pl.multiple_of(row, PIECE), PIECE), pl.ds(pl.multiple_of(col, LANES), LANES)


def add(a, b):
    return (a.astype(jnp.float32) + b.astype(jnp.float32)).astype(jnp.bfloat16)


def pair_kernel(near, other, *outs):
    for k, out in enumerate(outs):
        rows = slice(k * PIECE, (k + 1) * PIECE)
        out[...] = add(near[rows], other[rows])


def sum_kernel(*refs):
    *parts, out = refs
    total = parts[0][...].astype(jnp.float32)
    for part in parts[1:]:
        total = total + part[...].astype(jnp.float32)
    out[...] = total.astype(out.dtype)


def square_kernel(a, b, c, d, out):
    first = a[...].astype(jnp.float32) + b[...].astype(jnp.float32)
    out[...] = (first + (c[...].astype(jnp.float32) + d[...].astype(jnp.float32))).astype(out.dtype)


def turn_kernel(*refs):
    pieces, outs = refs[:RING], refs[RING:]
    for g, out in enumerate(outs):
        for k, piece in enumerate(pieces):
            out[k * PIECE : (k + 1) * PIECE] = piece[:, g * LANES : (g + 1) * LANES]


def join_kernel(*refs):
    *parts, out = refs
    for g, part in enumerate(parts):
        out[:, g * LANES : (g + 1) * LANES] = part[...]


def place_kernel(mine, theirs, out):
    core = lax.axis_index("core")
    scale = 1.0 / math.sqrt(OWN * PEERS * 2 * PEERS)
    for k in range(RING):
        for g in range(RING):
            for part, half_of in ((mine, core), (theirs, 1 - core)):
                value = part[k * PIECE : (k + 1) * PIECE, g * LANES : (g + 1) * LANES].astype(jnp.float32)
                rows, cols = wgrad_place(half_of, k, g)
                out[rows, cols] = value * jnp.float32(scale)


def exchange(parts, axes):
    return lax.all_to_all(parts, axes, 0, 0)


def trade(array, axes, bits=1):
    return lax.ppermute(array, axes, [(i, i ^ bits) for i in range(lax.axis_size(axes))])


def stack_kernel(*refs):
    *parts, out = refs
    for k, part in enumerate(parts):
        out[k * OWN : (k + 1) * OWN] = part[...]


def gather(block, slow, fast):
    def ahead(array, step):
        return lax.ppermute(array, fast, [(i, (i - step) % RING) for i in range(RING)])

    across = trade(block, slow)
    before, after = ahead(block, -1), ahead(block, 1)
    across_before = trade(before, slow)
    across_after = ahead(across, 1)
    beyond = ahead(before, -1)
    across_beyond = ahead(across_after, 1)
    blocks = (block, after, beyond, before, across, across_after, across_beyond, across_before)
    return vmem_call(stack_kernel, bf16(ROWS, WIDTH), "stack_" + fast)(*blocks)


def scatter_ring(pieces, axis, name):
    arrived = [pieces[0]]
    for k in range(1, RING):
        arrived.append(lax.ppermute(pieces[k], axis, [(i, (i + k) % RING) for i in range(RING)]))
    return vmem_call(sum_kernel, bf16(*pieces[0].shape), name)(*arrived)


def gather_ring(piece, axis):
    pieces = [piece]
    for k in range(1, RING):
        pieces.append(lax.ppermute(piece, axis, [(i, (i - k) % RING) for i in range(RING)]))
    return pieces


def per_device(features, out_grad, weight, block_values, block_coords, block_counts):
    dense = build(block_coords, block_counts, block_values)
    panel = gather(features, *ROW)
    parts = exchange(down_both(dense, panel), CHIP)

    half = bf16(WIDTH // 2, WIDTH)
    activations, send, wgrad_near, wgrad_far = vmem_call(
        middle_kernel,
        (bf16(OWN, WIDTH), bf16(OWN, WIDTH), half, half),
        "middle",
        scratch=[pltpu.VMEM((WIDTH, WIDTH), jnp.bfloat16)],
        flops=2 * 3 * OWN * WIDTH * WIDTH,
    )(parts, out_grad, weight)

    mine = gather(send, *CHIP)

    piece = bf16(PIECE, WIDTH)
    pieces = vmem_call(pair_kernel, (piece,) * RING, "pair")(wgrad_near, trade(wgrad_far, "core"))
    summed = scatter_ring(pieces, "z", "sum_z")
    ys = ("y_lo", "y_hi")
    summed = vmem_call(square_kernel, piece, "sum_y")(
        summed, trade(summed, ys, 1), trade(summed, ys, 2), trade(summed, ys, 3)
    )
    summed, mine = lax.optimization_barrier((summed, mine))
    pieces = gather_ring(summed, "z")
    theirs = trade(mine, "core")
    partial_grad = up_both(dense, mine, theirs)
    partial_grad, *pieces = lax.optimization_barrier((partial_grad, *pieces))
    received = exchange(partial_grad, ROW)

    column = bf16(WIDTH // 2, LANES)
    columns = vmem_call(turn_kernel, (column,) * RING, "turn")(*pieces)
    summed = scatter_ring(columns, "x", "sum_x")
    columns = gather_ring(summed, "x")
    own_half = vmem_call(join_kernel, half, "join")(*columns)
    weight_grad = vmem_call(place_kernel, jax.ShapeDtypeStruct((WIDTH, WIDTH), jnp.float32), "place")(
        own_half, trade(own_half, "core")
    )

    total = received[0].astype(jnp.float32)
    for k in range(1, PEERS):
        total = total + received[k].astype(jnp.float32)
    feature_grad = total.astype(jnp.bfloat16)
    return (activations, weight_grad, feature_grad)


def solution(mesh):
    fine = Mesh(mesh.devices.reshape(SIZES), AXES)
    return jax.shard_map(
        per_device,
        mesh=fine,
        in_specs=(
            P(COL + ROW, None),
            P(ROW + COL, None),
            P(),
            P(ROW, COL, None, None),
            P(ROW, COL, None, None),
            P(ROW, COL),
        ),
        out_specs=(P(ROW + COL, None), P(), P(COL + ROW, None)),
        check_vma=False,
    )
```

```python
import functools
import math

import jax
import jax.numpy as jnp
from jax import lax
from jax.experimental import pallas as pl
from jax.experimental.pallas import tpu as pltpu
from jax.sharding import Mesh, PartitionSpec as P

AXES = ("y_lo", "z", "y_hi", "x", "core")
SIZES = (2, 4, 2, 4, 2)
ROW = ("y_lo", "z")
CHIP = ("y_hi", "x")
COL = ("y_hi", "x", "core")
SIDE = 64
PEERS = 8
OWN = 192
WIDTH = 512
ROWS = PEERS * OWN
STEP = 256
RING = 4
PARTS = 3
PIECE = WIDTH // 2 // RING
LANES = WIDTH // RING


def vmem_call(kernel, outs, name, scratch=(), flops=0, moved=1 << 20, limit=16 << 20, aliases={}):
    vmem = pl.BlockSpec(memory_space=pltpu.VMEM)

    def call(*args):
        return pl.pallas_call(
            kernel,
            out_shape=outs,
            in_specs=[vmem] * len(args),
            out_specs=jax.tree.map(lambda _: vmem, outs),
            scratch_shapes=scratch,
            input_output_aliases=aliases,
            compiler_params=pltpu.CompilerParams(vmem_limit_bytes=limit),
            cost_estimate=pl.CostEstimate(flops=flops, bytes_accessed=moved, transcendentals=0),
            name=name,
        )(*args)

    return call


def bf16(*shape):
    return jax.ShapeDtypeStruct(shape, jnp.bfloat16)


def relative(owner, slow, fast):
    apart = (owner >> 2) ^ lax.axis_index(slow)
    ahead = ((owner & (RING - 1)) - lax.axis_index(fast)) & (RING - 1)
    return apart * RING + ahead


def absolute(place, slow, fast):
    apart, ahead = divmod(place, RING)
    return (lax.axis_index(slow) ^ apart) * RING + ((lax.axis_index(fast) + ahead) & (RING - 1))


def build_kernel(part, coords, counts, values, *rest):
    dense = rest[-1]
    rows, cols = dense.shape
    per_owner = OWN // SIDE
    me_core = lax.axis_index("core")

    if part == 0:

        @pl.loop(0, rows // SIDE)
        def _(r):
            dense[pl.ds(pl.multiple_of(r * SIDE, SIDE), SIDE), :] = jnp.zeros((SIDE, cols), dense.dtype)

    count = counts[0, 0]
    lane = lax.broadcasted_iota(jnp.int32, (SIDE, 2 * SIDE), 1)

    groups = (count + 15) >> 4

    @pl.loop((groups * part) // PARTS, (groups * (part + 1)) // PARTS)
    def _(g):
        group = values[0, 0, pl.ds(pl.multiple_of(g * 16, 16), 16), :]
        pairs = group.astype(jnp.float32).reshape(16, SIDE // 2, 2 * SIDE)
        for k in range(16):
            slot = g * 16 + k
            live = slot < count
            block_row = jnp.where(live, coords[0, 0, 0, slot], 0)
            block_col = jnp.where(live, coords[0, 0, 1, slot], 0)
            owner = block_row // per_owner
            half = (owner + me_core) & 1
            at_row = (half * PEERS + relative(owner >> 1, *CHIP)) * per_owner + block_row % per_owner
            at_col = relative(block_col // per_owner, *ROW) * per_owner + block_col % per_owner
            odd = (at_col & 1) == 1
            plain = pairs[k]
            turned = pltpu.roll(plain, SIDE, 1)
            block = jnp.concatenate(
                [jnp.where(odd, turned, plain), jnp.where(odd, plain, turned)], axis=0
            ).astype(dense.dtype)
            first = jnp.where(live, (at_col & 1) * SIDE, 4 * SIDE)
            mask = (lane >= first) & (lane < first + SIDE)
            place = dense.at[
                pl.ds(pl.multiple_of(at_row * SIDE, SIDE), SIDE),
                pl.ds(pl.multiple_of((at_col >> 1) * 2 * SIDE, 2 * SIDE), 2 * SIDE),
            ]
            place[...] = jnp.where(mask, block, place[...])


def build(part, coords, counts, values, *dense):
    vmem = pl.BlockSpec(memory_space=pltpu.VMEM)
    return pl.pallas_call(
        functools.partial(build_kernel, part),
        out_shape=bf16(2 * ROWS, ROWS),
        in_specs=[pl.BlockSpec(memory_space=pltpu.SMEM)] * 2 + [vmem] * (1 + len(dense)),
        out_specs=vmem,
        input_output_aliases={3: 0} if dense else {},
        compiler_params=pltpu.CompilerParams(vmem_limit_bytes=16 << 20),
        cost_estimate=pl.CostEstimate(flops=0, bytes_accessed=8 << 20, transcendentals=0),
        name=f"build_{part}",
    )(coords, counts, values, *dense)


def over_rows(a, b):
    return lax.dot_general(a, b, (((0,), (0,)), ((), ())), preferred_element_type=jnp.float32)


def down_kernel(first, count, dense, panel, out):
    for r in range(0, count, STEP):
        rows = slice(ROWS + first + r, ROWS + first + r + STEP)
        out[r : r + STEP] = jnp.dot(dense[rows], panel[...], preferred_element_type=jnp.float32).astype(out.dtype)


def store(out, place, axes, value):
    for k in range(2):
        out[absolute(place + k, *axes)] = value[k * OWN : (k + 1) * OWN].astype(out.dtype)


def down_add_kernel(first, count, dense, panel, other, *rest):
    for r in range(0, count, 2 * OWN):
        own = jnp.dot(dense[first + r : first + r + 2 * OWN], panel[...], preferred_element_type=jnp.float32)
        store(rest[-1], (first + r) // OWN, CHIP, own + other[r : r + 2 * OWN].astype(jnp.float32))


def up_kernel(dense, rows, out):
    for r in range(0, ROWS, STEP):
        out[r : r + STEP] = over_rows(dense[:ROWS, r : r + STEP], rows[...])


def up_add_kernel(dense, rows, other, out):
    for r in range(0, ROWS, 2 * OWN):
        total = over_rows(dense[ROWS:, r : r + 2 * OWN], rows[...]) + other[r : r + 2 * OWN]
        store(out, r // OWN, ROW, total)


def down_both(dense, panel):
    count = ROWS // 2
    work = 2 * count * ROWS * WIDTH
    others = []
    for n in range(2):
        kernel = functools.partial(down_kernel, n * count, count)
        others.append(trade(vmem_call(kernel, bf16(count, WIDTH), f"down_far_{n}", flops=work)(dense, panel), "core"))
    out = []
    for n in range(2):
        kernel = functools.partial(down_add_kernel, n * count, count)
        out = vmem_call(
            kernel, bf16(PEERS, OWN, WIDTH), f"down_near_{n}", flops=work, aliases={3: 0} if n else {}
        )(dense, panel, others[n], *([out] if n else []))
    return out


def up_both(dense, mine, theirs):
    work = 2 * ROWS * ROWS * WIDTH
    own = vmem_call(up_kernel, jax.ShapeDtypeStruct((ROWS, WIDTH), jnp.float32), "up_near", flops=work)(dense, mine)
    return vmem_call(up_add_kernel, bf16(PEERS, OWN, WIDTH), "up_far", flops=work)(dense, theirs, own)


def middle_kernel(parts, out_grad, weight, activations, send, wgrad_near, wgrad_far, local):
    total = parts[0].astype(jnp.float32)
    for k in range(1, PEERS):
        total = total + parts[k].astype(jnp.float32)
    aggregated = total.astype(jnp.bfloat16)
    at = lax.broadcasted_iota(jnp.int32, (OWN, OWN), 0)
    to = lax.broadcasted_iota(jnp.int32, (OWN, OWN), 1)
    half = SIDE // 2
    turn = jnp.where(
        (at // SIDE == to // SIDE) & (to % SIDE == 2 * (at % half) + (at % SIDE) // half), 1.0, 0.0
    ).astype(jnp.bfloat16)
    w = weight[...]
    pre_act = jnp.dot(aggregated, w, preferred_element_type=jnp.float32)
    sig = jax.nn.sigmoid(pre_act)
    act = (pre_act * sig).astype(jnp.bfloat16)
    activations[...] = over_rows(turn, act).astype(jnp.bfloat16)
    cotangent = jnp.dot(turn, out_grad[...], preferred_element_type=jnp.float32)
    grad_pre = (cotangent * sig * (1.0 + pre_act * (1.0 - sig))).astype(jnp.bfloat16)
    grad_agg = lax.dot_general(
        grad_pre, w, (((1,), (1,)), ((), ())), preferred_element_type=jnp.float32
    ).astype(jnp.bfloat16)
    send[...] = grad_agg
    local[...] = over_rows(aggregated, grad_pre).astype(jnp.bfloat16)
    core = lax.axis_index("core")
    for k in range(RING):
        for g in range(RING):
            for out, half_of in ((wgrad_near, core), (wgrad_far, 1 - core)):
                rows, cols = wgrad_place(half_of, k, g)
                out[k * PIECE : (k + 1) * PIECE, g * LANES : (g + 1) * LANES] = local[rows, cols]


def wgrad_place(half_of, k, g):
    row = half_of * (WIDTH // 2) + ((lax.axis_index("z") + k) & (RING - 1)) * PIECE
    col = ((lax.axis_index("x") + g) & (RING - 1)) * LANES
    return pl.ds(pl.multiple_of(row, PIECE), PIECE), pl.ds(pl.multiple_of(col, LANES), LANES)


def add(a, b):
    return (a.astype(jnp.float32) + b.astype(jnp.float32)).astype(jnp.bfloat16)


def pair_kernel(near, other, *outs):
    for k, out in enumerate(outs):
        rows = slice(k * PIECE, (k + 1) * PIECE)
        out[...] = add(near[rows], other[rows])


def sum_kernel(*refs):
    *parts, out = refs
    total = parts[0][...].astype(jnp.float32)
    for part in parts[1:]:
        total = total + part[...].astype(jnp.float32)
    out[...] = total.astype(out.dtype)


def square_kernel(a, b, c, d, out):
    first = a[...].astype(jnp.float32) + b[...].astype(jnp.float32)
    out[...] = (first + (c[...].astype(jnp.float32) + d[...].astype(jnp.float32))).astype(out.dtype)


def turn_kernel(*refs):
    pieces, outs = refs[:RING], refs[RING:]
    for g, out in enumerate(outs):
        for k, piece in enumerate(pieces):
            out[k * PIECE : (k + 1) * PIECE] = piece[:, g * LANES : (g + 1) * LANES]


def join_kernel(*refs):
    *parts, out = refs
    for g, part in enumerate(parts):
        out[:, g * LANES : (g + 1) * LANES] = part[...]


def place_kernel(mine, theirs, out):
    core = lax.axis_index("core")
    scale = 1.0 / math.sqrt(OWN * PEERS * 2 * PEERS)
    for k in range(RING):
        for g in range(RING):
            for part, half_of in ((mine, core), (theirs, 1 - core)):
                value = part[k * PIECE : (k + 1) * PIECE, g * LANES : (g + 1) * LANES].astype(jnp.float32)
                rows, cols = wgrad_place(half_of, k, g)
                out[rows, cols] = value * jnp.float32(scale)


def exchange(parts, axes):
    return lax.all_to_all(parts, axes, 0, 0)


def trade(array, axes, bits=1):
    return lax.ppermute(array, axes, [(i, i ^ bits) for i in range(lax.axis_size(axes))])


def stack_kernel(*refs):
    *parts, out = refs
    for k, part in enumerate(parts):
        out[k * OWN : (k + 1) * OWN] = part[...]


def gather(block, slow, fast, tasks, state):
    def ahead(array, step):
        return lax.ppermute(array, fast, [(i, (i - step) % RING) for i in range(RING)])

    across = trade(block, slow)
    before, after = ahead(block, -1), ahead(block, 1)
    across, before, after, state = lax.optimization_barrier((across, before, after, tasks[0](state)))
    across_before = trade(before, slow)
    across_after = ahead(across, 1)
    beyond = ahead(before, -1)
    across_before, across_after, beyond, state = lax.optimization_barrier(
        (across_before, across_after, beyond, tasks[1](state))
    )
    across_beyond = ahead(across_after, 1)
    across_beyond, state = lax.optimization_barrier((across_beyond, tasks[2](state)))
    blocks = (block, after, beyond, before, across, across_after, across_beyond, across_before)
    return vmem_call(stack_kernel, bf16(ROWS, WIDTH), "stack_" + fast)(*blocks), state


def scatter_ring(pieces, axis, name):
    arrived = [pieces[0]]
    for k in range(1, RING):
        arrived.append(lax.ppermute(pieces[k], axis, [(i, (i + k) % RING) for i in range(RING)]))
    return vmem_call(sum_kernel, bf16(*pieces[0].shape), name)(*arrived)


def gather_ring(piece, axis):
    pieces = [piece]
    for k in range(1, RING):
        pieces.append(lax.ppermute(piece, axis, [(i, (i - k) % RING) for i in range(RING)]))
    return pieces


def per_device(features, out_grad, weight, block_values, block_coords, block_counts):
    raw = (block_coords, block_counts, block_values)
    tasks = [lambda dense, part=part: build(part, *raw, *dense) for part in range(PARTS)]
    tasks = [lambda dense, task=task: (task(dense),) for task in tasks]
    panel, (dense,) = gather(features, *ROW, tasks, ())
    parts = exchange(down_both(dense, panel), CHIP)

    half = bf16(WIDTH // 2, WIDTH)
    activations, send, wgrad_near, wgrad_far = vmem_call(
        middle_kernel,
        (bf16(OWN, WIDTH), bf16(OWN, WIDTH), half, half),
        "middle",
        scratch=[pltpu.VMEM((WIDTH, WIDTH), jnp.bfloat16)],
        flops=2 * 3 * OWN * WIDTH * WIDTH,
    )(parts, out_grad, weight)

    piece = bf16(PIECE, WIDTH)
    ys = ("y_lo", "y_hi")

    def over_core(terms):
        return vmem_call(pair_kernel, (piece,) * RING, "pair")(terms[0], trade(terms[1], "core"))

    def over_z(pieces):
        return scatter_ring(pieces, "z", "sum_z")

    def over_y(summed):
        return vmem_call(square_kernel, piece, "sum_y")(
            summed, trade(summed, ys, 1), trade(summed, ys, 2), trade(summed, ys, 3)
        )

    mine, summed = gather(send, *CHIP, (over_core, over_z, over_y), (wgrad_near, wgrad_far))
    pieces = gather_ring(summed, "z")
    theirs = trade(mine, "core")
    partial_grad = up_both(dense, mine, theirs)
    partial_grad, *pieces = lax.optimization_barrier((partial_grad, *pieces))
    received = exchange(partial_grad, ROW)

    column = bf16(WIDTH // 2, LANES)
    columns = vmem_call(turn_kernel, (column,) * RING, "turn")(*pieces)
    summed = scatter_ring(columns, "x", "sum_x")
    columns = gather_ring(summed, "x")
    own_half = vmem_call(join_kernel, half, "join")(*columns)
    weight_grad = vmem_call(place_kernel, jax.ShapeDtypeStruct((WIDTH, WIDTH), jnp.float32), "place")(
        own_half, trade(own_half, "core")
    )

    total = received[0].astype(jnp.float32)
    for k in range(1, PEERS):
        total = total + received[k].astype(jnp.float32)
    feature_grad = total.astype(jnp.bfloat16)
    return (activations, weight_grad, feature_grad)


def solution(mesh):
    fine = Mesh(mesh.devices.reshape(SIZES), AXES)
    return jax.shard_map(
        per_device,
        mesh=fine,
        in_specs=(
            P(COL + ROW, None),
            P(ROW + COL, None),
            P(),
            P(ROW, COL, None, None),
            P(ROW, COL, None, None),
            P(ROW, COL),
        ),
        out_specs=(P(ROW + COL, None), P(), P(COL + ROW, None)),
        check_vma=False,
    )
```

```python
import functools
import math

import jax
import jax.numpy as jnp
from jax import lax
from jax.experimental import pallas as pl
from jax.experimental.pallas import tpu as pltpu
from jax.sharding import Mesh, PartitionSpec as P

AXES = ("y_lo", "z", "y_hi", "x", "core")
SIZES = (2, 4, 2, 4, 2)
ROW = ("y_lo", "z")
CHIP = ("y_hi", "x")
COL = ("y_hi", "x", "core")
SIDE = 64
PEERS = 8
OWN = 192
WIDTH = 512
ROWS = PEERS * OWN
STEP = 256
RING = 4
PARTS = 3
PIECE = WIDTH // 2 // RING
LANES = WIDTH // RING


def vmem_call(kernel, outs, name, scratch=(), flops=0, moved=1 << 20, limit=16 << 20, aliases={}):
    vmem = pl.BlockSpec(memory_space=pltpu.VMEM)

    def call(*args):
        return pl.pallas_call(
            kernel,
            out_shape=outs,
            in_specs=[vmem] * len(args),
            out_specs=jax.tree.map(lambda _: vmem, outs),
            scratch_shapes=scratch,
            input_output_aliases=aliases,
            compiler_params=pltpu.CompilerParams(vmem_limit_bytes=limit),
            cost_estimate=pl.CostEstimate(flops=flops, bytes_accessed=moved, transcendentals=0),
            name=name,
        )(*args)

    return call


def bf16(*shape):
    return jax.ShapeDtypeStruct(shape, jnp.bfloat16)


def relative(owner, slow, fast):
    apart = (owner >> 2) ^ lax.axis_index(slow)
    ahead = ((owner & (RING - 1)) - lax.axis_index(fast)) & (RING - 1)
    return apart * RING + ahead


def absolute(place, slow, fast):
    apart, ahead = divmod(place, RING)
    return (lax.axis_index(slow) ^ apart) * RING + ((lax.axis_index(fast) + ahead) & (RING - 1))


def build_kernel(part, coords, counts, values, *rest):
    dense = rest[-1]
    rows, cols = dense.shape
    per_owner = OWN // SIDE
    me_core = lax.axis_index("core")

    if part == 0:

        @pl.loop(0, rows // SIDE)
        def _(r):
            dense[pl.ds(pl.multiple_of(r * SIDE, SIDE), SIDE), :] = jnp.zeros((SIDE, cols), dense.dtype)

    count = counts[0, 0]
    lane = lax.broadcasted_iota(jnp.int32, (SIDE, 2 * SIDE), 1)

    groups = (count + 15) >> 4

    @pl.loop((groups * part) // PARTS, (groups * (part + 1)) // PARTS)
    def _(g):
        group = values[0, 0, pl.ds(pl.multiple_of(g * 16, 16), 16), :]
        pairs = group.astype(jnp.float32).reshape(16, SIDE // 2, 2 * SIDE)
        for k in range(16):
            slot = g * 16 + k
            live = slot < count
            block_row = jnp.where(live, coords[0, 0, 0, slot], 0)
            block_col = jnp.where(live, coords[0, 0, 1, slot], 0)
            owner = block_row // per_owner
            half = (owner + me_core) & 1
            at_row = (half * PEERS + (owner >> 1)) * per_owner + block_row % per_owner
            at_col = relative(block_col // per_owner, *ROW) * per_owner + block_col % per_owner
            odd = (at_col & 1) == 1
            plain = pairs[k]
            turned = pltpu.roll(plain, SIDE, 1)
            block = jnp.concatenate(
                [jnp.where(odd, turned, plain), jnp.where(odd, plain, turned)], axis=0
            ).astype(dense.dtype)
            first = jnp.where(live, (at_col & 1) * SIDE, 4 * SIDE)
            mask = (lane >= first) & (lane < first + SIDE)
            place = dense.at[
                pl.ds(pl.multiple_of(at_row * SIDE, SIDE), SIDE),
                pl.ds(pl.multiple_of((at_col >> 1) * 2 * SIDE, 2 * SIDE), 2 * SIDE),
            ]
            place[...] = jnp.where(mask, block, place[...])


def build(part, coords, counts, values, *dense):
    vmem = pl.BlockSpec(memory_space=pltpu.VMEM)
    return pl.pallas_call(
        functools.partial(build_kernel, part),
        out_shape=bf16(2 * ROWS, ROWS),
        in_specs=[pl.BlockSpec(memory_space=pltpu.SMEM)] * 2 + [vmem] * (1 + len(dense)),
        out_specs=vmem,
        input_output_aliases={3: 0} if dense else {},
        compiler_params=pltpu.CompilerParams(vmem_limit_bytes=16 << 20),
        cost_estimate=pl.CostEstimate(flops=0, bytes_accessed=8 << 20, transcendentals=0),
        name=f"build_{part}",
    )(coords, counts, values, *dense)


def over_rows(a, b):
    return lax.dot_general(a, b, (((0,), (0,)), ((), ())), preferred_element_type=jnp.float32)


def down_kernel(first, count, dense, panel, out):
    for r in range(0, count, STEP):
        rows = slice(ROWS + first + r, ROWS + first + r + STEP)
        out[r : r + STEP] = jnp.dot(dense[rows], panel[...], preferred_element_type=jnp.float32).astype(out.dtype)


def down_add_kernel(first, count, dense, panel, other, *rest):
    out = rest[-1]
    for r in range(0, count, STEP):
        rows = slice(first + r, first + r + STEP)
        own = jnp.dot(dense[rows], panel[...], preferred_element_type=jnp.float32)
        out[rows] = (own + other[r : r + STEP].astype(jnp.float32)).astype(out.dtype)


def up_kernel(dense, rows, out, far, near, sems):
    strips = [pl.ds(r, STEP) for r in range(0, ROWS, STEP)]
    copies = [
        pltpu.make_async_copy(dense.at[pl.ds(0, ROWS), strip], near.at[:, strip], sems.at[n])
        for n, strip in enumerate(strips)
    ]
    copies.append(pltpu.make_async_copy(dense.at[pl.ds(ROWS, ROWS)], far, sems.at[len(strips)]))
    for copy in copies:
        copy.start()
    for copy, r in zip(copies, range(0, ROWS, STEP)):
        copy.wait()
        out[r : r + STEP] = over_rows(near[:, r : r + STEP], rows[...])
    copies[-1].wait()


def up_add_kernel(tile, rows, other, out):
    for r in range(0, ROWS, 2 * OWN):
        total = over_rows(tile[:, r : r + 2 * OWN], rows[...]) + other[r : r + 2 * OWN]
        for k in range(2):
            out[absolute(r // OWN + k, *ROW)] = total[k * OWN : (k + 1) * OWN].astype(out.dtype)


def down_both(dense, panel):
    count = ROWS // 2
    work = 2 * count * ROWS * WIDTH
    others = []
    for n in range(2):
        kernel = functools.partial(down_kernel, n * count, count)
        others.append(trade(vmem_call(kernel, bf16(count, WIDTH), f"down_far_{n}", flops=work)(dense, panel), "core"))
    out = []
    for n in range(2):
        kernel = functools.partial(down_add_kernel, n * count, count)
        out = vmem_call(
            kernel, bf16(ROWS, WIDTH), f"down_near_{n}", flops=work, aliases={3: 0} if n else {}
        )(dense, panel, others[n], *([out] if n else []))
    return out


def middle_kernel(parts, out_grad, weight, activations, send, wgrad_near, wgrad_far, local):
    total = parts[0].astype(jnp.float32)
    for k in range(1, PEERS):
        total = total + parts[k].astype(jnp.float32)
    aggregated = total.astype(jnp.bfloat16)
    at = lax.broadcasted_iota(jnp.int32, (OWN, OWN), 0)
    to = lax.broadcasted_iota(jnp.int32, (OWN, OWN), 1)
    half = SIDE // 2
    turn = jnp.where(
        (at // SIDE == to // SIDE) & (to % SIDE == 2 * (at % half) + (at % SIDE) // half), 1.0, 0.0
    ).astype(jnp.bfloat16)
    w = weight[...]
    pre_act = jnp.dot(aggregated, w, preferred_element_type=jnp.float32)
    sig = jax.nn.sigmoid(pre_act)
    act = (pre_act * sig).astype(jnp.bfloat16)
    activations[...] = over_rows(turn, act).astype(jnp.bfloat16)
    cotangent = jnp.dot(turn, out_grad[...], preferred_element_type=jnp.float32)
    grad_pre = (cotangent * sig * (1.0 + pre_act * (1.0 - sig))).astype(jnp.bfloat16)
    grad_agg = lax.dot_general(
        grad_pre, w, (((1,), (1,)), ((), ())), preferred_element_type=jnp.float32
    ).astype(jnp.bfloat16)
    for k in range(PEERS):
        send[k] = grad_agg
    local[...] = over_rows(aggregated, grad_pre).astype(jnp.bfloat16)
    core = lax.axis_index("core")
    for k in range(RING):
        for g in range(RING):
            for out, half_of in ((wgrad_near, core), (wgrad_far, 1 - core)):
                rows, cols = wgrad_place(half_of, k, g)
                out[k * PIECE : (k + 1) * PIECE, g * LANES : (g + 1) * LANES] = local[rows, cols]


def wgrad_place(half_of, k, g):
    row = half_of * (WIDTH // 2) + ((lax.axis_index("z") + k) & (RING - 1)) * PIECE
    col = ((lax.axis_index("x") + g) & (RING - 1)) * LANES
    return pl.ds(pl.multiple_of(row, PIECE), PIECE), pl.ds(pl.multiple_of(col, LANES), LANES)


def add(a, b):
    return (a.astype(jnp.float32) + b.astype(jnp.float32)).astype(jnp.bfloat16)


def pair_kernel(near, other, *outs):
    for k, out in enumerate(outs):
        rows = slice(k * PIECE, (k + 1) * PIECE)
        out[...] = add(near[rows], other[rows])


def sum_kernel(*refs):
    *parts, out = refs
    total = parts[0][...].astype(jnp.float32)
    for part in parts[1:]:
        total = total + part[...].astype(jnp.float32)
    out[...] = total.astype(out.dtype)


def square_kernel(a, b, c, d, out):
    first = a[...].astype(jnp.float32) + b[...].astype(jnp.float32)
    out[...] = (first + (c[...].astype(jnp.float32) + d[...].astype(jnp.float32))).astype(out.dtype)


def turn_kernel(*refs):
    pieces, outs = refs[:RING], refs[RING:]
    for g, out in enumerate(outs):
        for k, piece in enumerate(pieces):
            out[k * PIECE : (k + 1) * PIECE] = piece[:, g * LANES : (g + 1) * LANES]


def join_kernel(*refs):
    *parts, out = refs
    for g, part in enumerate(parts):
        out[:, g * LANES : (g + 1) * LANES] = part[...]


def place_kernel(mine, theirs, out):
    core = lax.axis_index("core")
    scale = 1.0 / math.sqrt(OWN * PEERS * 2 * PEERS)
    for k in range(RING):
        for g in range(RING):
            for part, half_of in ((mine, core), (theirs, 1 - core)):
                value = part[k * PIECE : (k + 1) * PIECE, g * LANES : (g + 1) * LANES].astype(jnp.float32)
                rows, cols = wgrad_place(half_of, k, g)
                out[rows, cols] = value * jnp.float32(scale)


def exchange(parts, axes):
    return lax.all_to_all(parts, axes, 0, 0)


def trade(array, axes, bits=1):
    return lax.ppermute(array, axes, [(i, i ^ bits) for i in range(lax.axis_size(axes))])


def stack_kernel(*refs):
    *parts, out = refs
    for k, part in enumerate(parts):
        out[k * OWN : (k + 1) * OWN] = part[...]


def gather(block, slow, fast, tasks, state):
    def ahead(array, step):
        return lax.ppermute(array, fast, [(i, (i - step) % RING) for i in range(RING)])

    across = trade(block, slow)
    before, after = ahead(block, -1), ahead(block, 1)
    across, before, after, state = lax.optimization_barrier((across, before, after, tasks[0](state)))
    across_before = trade(before, slow)
    across_after = ahead(across, 1)
    beyond = ahead(before, -1)
    across_before, across_after, beyond, state = lax.optimization_barrier(
        (across_before, across_after, beyond, tasks[1](state))
    )
    across_beyond = ahead(across_after, 1)
    across_beyond, state = lax.optimization_barrier((across_beyond, tasks[2](state)))
    blocks = (block, after, beyond, before, across, across_after, across_beyond, across_before)
    return vmem_call(stack_kernel, bf16(ROWS, WIDTH), "stack_" + fast)(*blocks), state


def scatter_ring(pieces, axis, name):
    arrived = [pieces[0]]
    for k in range(1, RING):
        arrived.append(lax.ppermute(pieces[k], axis, [(i, (i + k) % RING) for i in range(RING)]))
    return vmem_call(sum_kernel, bf16(*pieces[0].shape), name)(*arrived)


def gather_ring(piece, axis):
    pieces = [piece]
    for k in range(1, RING):
        pieces.append(lax.ppermute(piece, axis, [(i, (i - k) % RING) for i in range(RING)]))
    return pieces


def per_device(features, out_grad, weight, block_values, block_coords, block_counts):
    raw = (block_coords, block_counts, block_values)
    tasks = [lambda dense, part=part: build(part, *raw, *dense) for part in range(PARTS)]
    tasks = [lambda dense, task=task: (task(dense),) for task in tasks]
    panel, (dense,) = gather(features, *ROW, tasks, ())
    parts = exchange(down_both(dense, panel).reshape(PEERS, OWN, WIDTH), CHIP)

    half = bf16(WIDTH // 2, WIDTH)
    activations, send, wgrad_near, wgrad_far = vmem_call(
        middle_kernel,
        (bf16(OWN, WIDTH), bf16(PEERS, OWN, WIDTH), half, half),
        "middle",
        scratch=[pltpu.VMEM((WIDTH, WIDTH), jnp.bfloat16)],
        flops=2 * 3 * OWN * WIDTH * WIDTH,
    )(parts, out_grad, weight)

    piece = bf16(PIECE, WIDTH)
    ys = ("y_lo", "y_hi")

    def over_core(terms):
        return vmem_call(pair_kernel, (piece,) * RING, "pair")(terms[0], trade(terms[1], "core"))

    def over_z(pieces):
        return scatter_ring(pieces, "z", "sum_z")

    def over_y(summed):
        return vmem_call(square_kernel, piece, "sum_y")(
            summed, trade(summed, ys, 1), trade(summed, ys, 2), trade(summed, ys, 3)
        )

    mine = exchange(send, CHIP).reshape(ROWS, WIDTH)
    summed = over_y(over_z(over_core((wgrad_near, wgrad_far))))
    summed, mine = lax.optimization_barrier((summed, mine))

    theirs = trade(mine, "core")
    work = 2 * ROWS * ROWS * WIDTH
    vmem = pl.BlockSpec(memory_space=pltpu.VMEM)
    own, far = pl.pallas_call(
        up_kernel,
        out_shape=(jax.ShapeDtypeStruct((ROWS, WIDTH), jnp.float32), bf16(ROWS, ROWS)),
        in_specs=[pl.BlockSpec(memory_space=pltpu.HBM), vmem],
        out_specs=(vmem, vmem),
        scratch_shapes=[pltpu.VMEM((ROWS, ROWS), jnp.bfloat16), pltpu.SemaphoreType.DMA((ROWS // STEP + 1,))],
        compiler_params=pltpu.CompilerParams(vmem_limit_bytes=44 << 20),
        cost_estimate=pl.CostEstimate(flops=work, bytes_accessed=12 << 20, transcendentals=0),
        name="up_near",
    )(dense, mine)
    summed, own = lax.optimization_barrier((summed, own))
    pieces = gather_ring(summed, "z")
    partial_grad = vmem_call(up_add_kernel, bf16(PEERS, OWN, WIDTH), "up_far", flops=work)(far, theirs, own)
    partial_grad, *pieces = lax.optimization_barrier((partial_grad, *pieces))
    received = exchange(partial_grad, ROW)

    column = bf16(WIDTH // 2, LANES)
    columns = vmem_call(turn_kernel, (column,) * RING, "turn")(*pieces)
    summed = scatter_ring(columns, "x", "sum_x")
    columns = gather_ring(summed, "x")
    own_half = vmem_call(join_kernel, half, "join")(*columns)
    weight_grad = vmem_call(place_kernel, jax.ShapeDtypeStruct((WIDTH, WIDTH), jnp.float32), "place")(
        own_half, trade(own_half, "core")
    )

    total = received[0].astype(jnp.float32)
    for k in range(1, PEERS):
        total = total + received[k].astype(jnp.float32)
    feature_grad = total.astype(jnp.bfloat16)
    return (activations, weight_grad, feature_grad)


def solution(mesh):
    fine = Mesh(mesh.devices.reshape(SIZES), AXES)
    return jax.shard_map(
        per_device,
        mesh=fine,
        in_specs=(
            P(COL + ROW, None),
            P(ROW + COL, None),
            P(),
            P(ROW, COL, None, None),
            P(ROW, COL, None, None),
            P(ROW, COL),
        ),
        out_specs=(P(ROW + COL, None), P(), P(COL + ROW, None)),
        check_vma=False,
    )
```

```python
import functools
import math

import jax
import jax.numpy as jnp
from jax import lax
from jax.experimental import pallas as pl
from jax.experimental.pallas import tpu as pltpu
from jax.sharding import Mesh, PartitionSpec as P

AXES = ("y_lo", "z", "y_hi", "x", "core")
SIZES = (2, 4, 2, 4, 2)
ROW = ("y_lo", "z")
CHIP = ("y_hi", "x")
COL = ("y_hi", "x", "core")
SIDE = 64
PEERS = 8
OWN = 192
WIDTH = 512
ROWS = PEERS * OWN
STEP = 256
RING = 4
PARTS = 2
LAST = 2 * SIDE * 2
PIECE = WIDTH // 2 // RING
LANES = WIDTH // RING


def vmem_call(kernel, outs, name, scratch=(), flops=0, moved=1 << 20, limit=16 << 20, aliases={}):
    vmem = pl.BlockSpec(memory_space=pltpu.VMEM)

    def call(*args):
        return pl.pallas_call(
            kernel,
            out_shape=outs,
            in_specs=[vmem] * len(args),
            out_specs=jax.tree.map(lambda _: vmem, outs),
            scratch_shapes=scratch,
            input_output_aliases=aliases,
            compiler_params=pltpu.CompilerParams(vmem_limit_bytes=limit),
            cost_estimate=pl.CostEstimate(flops=flops, bytes_accessed=moved, transcendentals=0),
            name=name,
        )(*args)

    return call


def bf16(*shape):
    return jax.ShapeDtypeStruct(shape, jnp.bfloat16)


def relative(owner, slow, fast):
    apart = (owner >> 2) ^ lax.axis_index(slow)
    ahead = ((owner & (RING - 1)) - lax.axis_index(fast)) & (RING - 1)
    return apart * RING + (ahead ^ (ahead >> 1))


def absolute(place, slow, fast):
    apart, ahead = divmod(place, RING)
    ahead ^= ahead >> 1
    return (lax.axis_index(slow) ^ apart) * RING + ((lax.axis_index(fast) + ahead) & (RING - 1))


def build_kernel(part, coords, counts, values, *rest):
    dense = rest[-1]
    rows, cols = dense.shape
    per_owner = OWN // SIDE
    me_core = lax.axis_index("core")

    if part == 0:

        @pl.loop(0, rows // SIDE)
        def _(r):
            dense[pl.ds(pl.multiple_of(r * SIDE, SIDE), SIDE), :] = jnp.zeros((SIDE, cols), dense.dtype)

    count = counts[0, 0]
    lane = lax.broadcasted_iota(jnp.int32, (SIDE, 2 * SIDE), 1)

    groups = (count + 15) >> 4

    @pl.loop((groups * part) // PARTS, (groups * (part + 1)) // PARTS)
    def _(g):
        group = values[0, 0, pl.ds(pl.multiple_of(g * 16, 16), 16), :]
        pairs = group.astype(jnp.float32).reshape(16, SIDE // 2, 2 * SIDE)
        for k in range(16):
            slot = g * 16 + k
            live = slot < count
            block_row = jnp.where(live, coords[0, 0, 0, slot], 0)
            block_col = jnp.where(live, coords[0, 0, 1, slot], 0)
            owner = block_row // per_owner
            half = (owner + me_core) & 1
            at_row = (half * PEERS + (owner >> 1)) * per_owner + block_row % per_owner
            at_col = relative(block_col // per_owner, *ROW) * per_owner + block_col % per_owner
            odd = (at_col & 1) == 1
            plain = pairs[k]
            turned = pltpu.roll(plain, SIDE, 1)
            block = jnp.concatenate(
                [jnp.where(odd, turned, plain), jnp.where(odd, plain, turned)], axis=0
            ).astype(dense.dtype)
            first = jnp.where(live, (at_col & 1) * SIDE, 4 * SIDE)
            mask = (lane >= first) & (lane < first + SIDE)
            place = dense.at[
                pl.ds(pl.multiple_of(at_row * SIDE, SIDE), SIDE),
                pl.ds(pl.multiple_of((at_col >> 1) * 2 * SIDE, 2 * SIDE), 2 * SIDE),
            ]
            place[...] = jnp.where(mask, block, place[...])


def build(part, coords, counts, values, *dense):
    vmem = pl.BlockSpec(memory_space=pltpu.VMEM)
    return pl.pallas_call(
        functools.partial(build_kernel, part),
        out_shape=bf16(2 * ROWS, ROWS),
        in_specs=[pl.BlockSpec(memory_space=pltpu.SMEM)] * 2 + [vmem] * (1 + len(dense)),
        out_specs=vmem,
        input_output_aliases={3: 0} if dense else {},
        compiler_params=pltpu.CompilerParams(vmem_limit_bytes=16 << 20),
        cost_estimate=pl.CostEstimate(flops=0, bytes_accessed=8 << 20, transcendentals=0),
        name=f"build_{part}",
    )(coords, counts, values, *dense)


def over_rows(a, b):
    return lax.dot_general(a, b, (((0,), (0,)), ((), ())), preferred_element_type=jnp.float32)


def down_kernel(*refs):
    dense, *blocks, out, panel = refs
    for k, block in enumerate(blocks):
        panel[k * OWN : (k + 1) * OWN] = block[...]
    panel[ROWS - OWN :] = jnp.zeros((OWN, WIDTH), panel.dtype)
    for r in range(0, 2 * ROWS, STEP):
        out[r : r + STEP] = jnp.dot(dense[r : r + STEP], panel[...], preferred_element_type=jnp.float32)


def with_last(dense, block, rows):
    padded = jnp.concatenate([jnp.zeros((LAST - OWN, WIDTH), block.dtype), block[...]], axis=0)
    return jnp.dot(dense[rows, ROWS - LAST :], padded, preferred_element_type=jnp.float32)


def down_far_kernel(first, count, dense, block, most, out):
    for r in range(0, count, STEP):
        rows = slice(ROWS + first + r, ROWS + first + r + STEP)
        out[r : r + STEP] = (most[rows] + with_last(dense, block, rows)).astype(out.dtype)


def down_near_kernel(first, count, dense, block, most, other, *rest):
    out = rest[-1]
    for r in range(0, count, STEP):
        rows = slice(first + r, first + r + STEP)
        total = most[rows] + with_last(dense, block, rows) + other[r : r + STEP].astype(jnp.float32)
        out[rows] = total.astype(out.dtype)


def up_kernel(dense, rows, out, far, near, sems):
    strips = [pl.ds(r, STEP) for r in range(0, ROWS, STEP)]
    copies = [
        pltpu.make_async_copy(dense.at[pl.ds(0, ROWS), strip], near.at[:, strip], sems.at[n])
        for n, strip in enumerate(strips)
    ]
    copies.append(pltpu.make_async_copy(dense.at[pl.ds(ROWS, ROWS)], far, sems.at[len(strips)]))
    for copy in copies:
        copy.start()
    for copy, r in zip(copies, range(0, ROWS, STEP)):
        copy.wait()
        out[r : r + STEP] = over_rows(near[:, r : r + STEP], rows[...])
    copies[-1].wait()


def up_add_kernel(tile, rows, other, out):
    for r in range(0, ROWS, 2 * OWN):
        total = over_rows(tile[:, r : r + 2 * OWN], rows[...]) + other[r : r + 2 * OWN]
        for k in range(2):
            out[absolute(r // OWN + k, *ROW)] = total[k * OWN : (k + 1) * OWN].astype(out.dtype)


def down_most(dense, blocks):
    return vmem_call(
        down_kernel,
        jax.ShapeDtypeStruct((2 * ROWS, WIDTH), jnp.float32),
        "down_most",
        scratch=[pltpu.VMEM((ROWS, WIDTH), jnp.bfloat16)],
        flops=4 * ROWS * ROWS * WIDTH,
    )(dense, *blocks)


def down_both(dense, most, block):
    count = ROWS // 2
    work = 2 * count * LAST * WIDTH
    others = []
    for n in range(2):
        kernel = functools.partial(down_far_kernel, n * count, count)
        far = vmem_call(kernel, bf16(count, WIDTH), f"down_far_{n}", flops=work)(dense, block, most)
        others.append(trade(far, "core"))
    out = []
    for n in range(2):
        kernel = functools.partial(down_near_kernel, n * count, count)
        out = vmem_call(
            kernel, bf16(ROWS, WIDTH), f"down_near_{n}", flops=work, aliases={4: 0} if n else {}
        )(dense, block, most, others[n], *([out] if n else []))
    return out


def middle_kernel(parts, out_grad, weight, activations, send, aggregated_out, grad_pre_out):
    total = parts[0].astype(jnp.float32)
    for k in range(1, PEERS):
        total = total + parts[k].astype(jnp.float32)
    aggregated = total.astype(jnp.bfloat16)
    at = lax.broadcasted_iota(jnp.int32, (OWN, OWN), 0)
    to = lax.broadcasted_iota(jnp.int32, (OWN, OWN), 1)
    half = SIDE // 2
    turn = jnp.where(
        (at // SIDE == to // SIDE) & (to % SIDE == 2 * (at % half) + (at % SIDE) // half), 1.0, 0.0
    ).astype(jnp.bfloat16)
    w = weight[...]
    pre_act = jnp.dot(aggregated, w, preferred_element_type=jnp.float32)
    sig = jax.nn.sigmoid(pre_act)
    act = (pre_act * sig).astype(jnp.bfloat16)
    activations[...] = over_rows(turn, act).astype(jnp.bfloat16)
    cotangent = jnp.dot(turn, out_grad[...], preferred_element_type=jnp.float32)
    grad_pre = (cotangent * sig * (1.0 + pre_act * (1.0 - sig))).astype(jnp.bfloat16)
    grad_agg = lax.dot_general(
        grad_pre, w, (((1,), (1,)), ((), ())), preferred_element_type=jnp.float32
    ).astype(jnp.bfloat16)
    for k in range(PEERS):
        send[k] = grad_agg
    aggregated_out[...] = aggregated
    grad_pre_out[...] = grad_pre


def wgrad_kernel(aggregated, grad_pre, wgrad_near, wgrad_far, local):
    local[...] = over_rows(aggregated[...], grad_pre[...]).astype(jnp.bfloat16)
    core = lax.axis_index("core")
    for k in range(RING):
        for g in range(RING):
            for out, half_of in ((wgrad_near, core), (wgrad_far, 1 - core)):
                rows, cols = wgrad_place(half_of, k, g)
                out[k * PIECE : (k + 1) * PIECE, g * LANES : (g + 1) * LANES] = local[rows, cols]


def wgrad_place(half_of, k, g):
    row = half_of * (WIDTH // 2) + (lax.axis_index("z") ^ k) * PIECE
    col = ((lax.axis_index("x") + g) & (RING - 1)) * LANES
    return pl.ds(pl.multiple_of(row, PIECE), PIECE), pl.ds(pl.multiple_of(col, LANES), LANES)


def add(a, b):
    return (a.astype(jnp.float32) + b.astype(jnp.float32)).astype(jnp.bfloat16)


def pair_kernel(near, other, *outs):
    for k, out in enumerate(outs):
        rows = slice(k * PIECE, (k + 1) * PIECE)
        out[...] = add(near[rows], other[rows])


def sum_kernel(*refs):
    *parts, out = refs
    total = parts[0][...].astype(jnp.float32)
    for part in parts[1:]:
        total = total + part[...].astype(jnp.float32)
    out[...] = total.astype(out.dtype)


def square_kernel(a, b, c, d, out):
    first = a[...].astype(jnp.float32) + b[...].astype(jnp.float32)
    out[...] = (first + (c[...].astype(jnp.float32) + d[...].astype(jnp.float32))).astype(out.dtype)


def turn_kernel(low, high, *outs):
    rows = low.shape[0]
    for g, out in enumerate(outs):
        for n, part in enumerate((low, high)):
            out[n * rows : (n + 1) * rows] = part[:, g * LANES : (g + 1) * LANES]


def join_kernel(*refs):
    *parts, out = refs
    for g, part in enumerate(parts):
        out[:, g * LANES : (g + 1) * LANES] = part[...]


def place_kernel(mine, theirs, out):
    core = lax.axis_index("core")
    scale = 1.0 / math.sqrt(OWN * PEERS * 2 * PEERS)
    for k in range(RING):
        for g in range(RING):
            for part, half_of in ((mine, core), (theirs, 1 - core)):
                value = part[k * PIECE : (k + 1) * PIECE, g * LANES : (g + 1) * LANES].astype(jnp.float32)
                rows, cols = wgrad_place(half_of, k, g)
                out[rows, cols] = value * jnp.float32(scale)


def exchange(parts, axes):
    return lax.all_to_all(parts, axes, 0, 0)


def trade(array, axes, bits=1):
    return lax.ppermute(array, axes, [(i, i ^ bits) for i in range(lax.axis_size(axes))])


def double_kernel(first, second, out):
    rows = first.shape[0]
    out[:rows] = first[...]
    out[rows:] = second[...]


def gather(block, slow, fast, tasks):
    def ahead(array, step):
        return lax.ppermute(array, fast, [(i, (i - step) % RING) for i in range(RING)])

    across = trade(block, slow)
    before, after = ahead(block, -1), ahead(block, 1)
    across, before, after, state = lax.optimization_barrier((across, before, after, tasks[0](None, None)))
    across_before = trade(before, slow)
    across_after = ahead(across, 1)
    beyond = ahead(before, -1)
    across_before, across_after, beyond, state = lax.optimization_barrier(
        (across_before, across_after, beyond, tasks[1](None, state))
    )
    across_beyond = ahead(across_after, 1)
    blocks = (block, after, before, beyond, across, across_after, across_before)
    return lax.optimization_barrier((across_beyond, tasks[2](blocks, state)))


def scatter_ring(pieces, axis, name):
    arrived = [pieces[0]]
    for k in range(1, RING):
        arrived.append(lax.ppermute(pieces[k], axis, [(i, (i + k) % RING) for i in range(RING)]))
    return vmem_call(sum_kernel, bf16(*pieces[0].shape), name)(*arrived)


def gather_ring(piece, axis):
    pieces = [piece]
    for k in range(1, RING):
        pieces.append(lax.ppermute(piece, axis, [(i, (i - k) % RING) for i in range(RING)]))
    return pieces


def per_device(features, out_grad, weight, block_values, block_coords, block_counts):
    raw = (block_coords, block_counts, block_values)
    tasks = (
        lambda blocks, dense: build(0, *raw),
        lambda blocks, dense: build(1, *raw, dense),
        lambda blocks, dense: (dense, down_most(dense, blocks)),
    )
    block, (dense, most) = gather(features, *ROW, tasks)
    parts = exchange(down_both(dense, most, block).reshape(PEERS, OWN, WIDTH), CHIP)

    half = bf16(WIDTH // 2, WIDTH)
    own = bf16(OWN, WIDTH)
    activations, send, aggregated, grad_pre = vmem_call(
        middle_kernel, (own, bf16(PEERS, OWN, WIDTH), own, own), "middle", flops=2 * 2 * OWN * WIDTH * WIDTH
    )(parts, out_grad, weight)
    wgrads = vmem_call(
        wgrad_kernel,
        (half, half),
        "wgrad",
        scratch=[pltpu.VMEM((WIDTH, WIDTH), jnp.bfloat16)],
        flops=2 * OWN * WIDTH * WIDTH,
    )(aggregated, grad_pre)

    piece = bf16(PIECE, WIDTH)
    ys = ("y_lo", "y_hi")

    def over_core(terms):
        return vmem_call(pair_kernel, (piece,) * RING, "pair")(terms[0], trade(terms[1], "core"))

    def over_z(pieces):
        arrived = [pieces[0]] + [trade(pieces[k], "z", k) for k in range(1, RING)]
        return vmem_call(sum_kernel, piece, "sum_z")(*arrived)

    def over_y(summed):
        return vmem_call(square_kernel, piece, "sum_y")(
            summed, trade(summed, ys, 1), trade(summed, ys, 2), trade(summed, ys, 3)
        )

    mine = exchange(send, CHIP).reshape(ROWS, WIDTH)
    summed = over_y(over_z(over_core(wgrads)))
    summed, mine = lax.optimization_barrier((summed, mine))

    theirs = trade(mine, "core")
    work = 2 * ROWS * ROWS * WIDTH
    vmem = pl.BlockSpec(memory_space=pltpu.VMEM)
    own, far = pl.pallas_call(
        up_kernel,
        out_shape=(jax.ShapeDtypeStruct((ROWS, WIDTH), jnp.float32), bf16(ROWS, ROWS)),
        in_specs=[pl.BlockSpec(memory_space=pltpu.HBM), vmem],
        out_specs=(vmem, vmem),
        scratch_shapes=[pltpu.VMEM((ROWS, ROWS), jnp.bfloat16), pltpu.SemaphoreType.DMA((ROWS // STEP + 1,))],
        compiler_params=pltpu.CompilerParams(vmem_limit_bytes=44 << 20),
        cost_estimate=pl.CostEstimate(flops=work, bytes_accessed=12 << 20, transcendentals=0),
        name="up_near",
    )(dense, mine)
    next_piece, own = lax.optimization_barrier((trade(summed, "z", 1), own))
    pair = vmem_call(double_kernel, bf16(2 * PIECE, WIDTH), "double")(summed, next_piece)
    partial_grad = vmem_call(up_add_kernel, bf16(PEERS, OWN, WIDTH), "up_far", flops=work)(far, theirs, own)
    pairs = (pair, trade(pair, "z", 2))
    partial_grad, *pairs = lax.optimization_barrier((partial_grad, *pairs))
    received = exchange(partial_grad, ROW)

    column = bf16(WIDTH // 2, LANES)
    columns = vmem_call(turn_kernel, (column,) * RING, "turn")(*pairs)
    summed = scatter_ring(columns, "x", "sum_x")
    columns = gather_ring(summed, "x")
    own_half = vmem_call(join_kernel, half, "join")(*columns)
    weight_grad = vmem_call(place_kernel, jax.ShapeDtypeStruct((WIDTH, WIDTH), jnp.float32), "place")(
        own_half, trade(own_half, "core")
    )

    total = received[0].astype(jnp.float32)
    for k in range(1, PEERS):
        total = total + received[k].astype(jnp.float32)
    feature_grad = total.astype(jnp.bfloat16)
    return (activations, weight_grad, feature_grad)


def solution(mesh):
    fine = Mesh(mesh.devices.reshape(SIZES), AXES)
    return jax.shard_map(
        per_device,
        mesh=fine,
        in_specs=(
            P(COL + ROW, None),
            P(ROW + COL, None),
            P(),
            P(ROW, COL, None, None),
            P(ROW, COL, None, None),
            P(ROW, COL),
        ),
        out_specs=(P(ROW + COL, None), P(), P(COL + ROW, None)),
        check_vma=False,
    )
```

```python
import functools
import math

import jax
import jax.numpy as jnp
from jax import lax
from jax.experimental import pallas as pl
from jax.experimental.pallas import tpu as pltpu
from jax.sharding import Mesh, PartitionSpec as P

AXES = ("y_lo", "z", "y_hi", "x", "core")
SIZES = (2, 4, 2, 4, 2)
ROW = ("y_lo", "z")
CHIP = ("y_hi", "x")
COL = ("y_hi", "x", "core")
SIDE = 64
PEERS = 8
OWN = 192
WIDTH = 512
ROWS = PEERS * OWN
STEP = 256
RING = 4
PARTS = 2
LAST = 2 * SIDE * 2
PIECE = WIDTH // 2 // RING
LANES = WIDTH // RING


def vmem_call(kernel, outs, name, scratch=(), flops=0, moved=1 << 20, limit=16 << 20, aliases={}):
    vmem = pl.BlockSpec(memory_space=pltpu.VMEM)

    def call(*args):
        return pl.pallas_call(
            kernel,
            out_shape=outs,
            in_specs=[vmem] * len(args),
            out_specs=jax.tree.map(lambda _: vmem, outs),
            scratch_shapes=scratch,
            input_output_aliases=aliases,
            compiler_params=pltpu.CompilerParams(vmem_limit_bytes=limit),
            cost_estimate=pl.CostEstimate(flops=flops, bytes_accessed=moved, transcendentals=0),
            name=name,
        )(*args)

    return call


def bf16(*shape):
    return jax.ShapeDtypeStruct(shape, jnp.bfloat16)


def relative(owner, slow, fast):
    apart = (owner >> 2) ^ lax.axis_index(slow)
    ahead = ((owner & (RING - 1)) - lax.axis_index(fast)) & (RING - 1)
    return apart * RING + (ahead ^ (ahead >> 1))


def absolute(place, slow, fast):
    apart, ahead = divmod(place, RING)
    ahead ^= ahead >> 1
    return (lax.axis_index(slow) ^ apart) * RING + ((lax.axis_index(fast) + ahead) & (RING - 1))


LEAVING = ((0, 2), (1, 2), (1, 3), (1, 1), (0, 3), (1, 0), (0, 1), (0, 0))
FIRST = 3


def leaving_place(chip):
    table = sum(place << 4 * (RING * apart + ahead) for place, (apart, ahead) in enumerate(LEAVING))
    apart = (chip >> 2) ^ lax.axis_index("y_hi")
    ahead = ((chip & (RING - 1)) - lax.axis_index("x")) & (RING - 1)
    return (table >> (4 * (RING * apart + ahead))) & 15


def leaving_chip(place):
    apart, ahead = LEAVING[place]
    return (lax.axis_index("y_hi") ^ apart) * RING + ((lax.axis_index("x") + ahead) & (RING - 1))


def build_kernel(part, coords, counts, values, *rest):
    dense = rest[-1]
    rows, cols = dense.shape
    per_owner = OWN // SIDE
    me_core = lax.axis_index("core")

    if part == 0:

        @pl.loop(0, rows // SIDE)
        def _(r):
            dense[pl.ds(pl.multiple_of(r * SIDE, SIDE), SIDE), :] = jnp.zeros((SIDE, cols), dense.dtype)

    count = counts[0, 0]
    lane = lax.broadcasted_iota(jnp.int32, (SIDE, 2 * SIDE), 1)

    groups = (count + 15) >> 4

    @pl.loop((groups * part) // PARTS, (groups * (part + 1)) // PARTS)
    def _(g):
        group = values[0, 0, pl.ds(pl.multiple_of(g * 16, 16), 16), :]
        pairs = group.astype(jnp.float32).reshape(16, SIDE // 2, 2 * SIDE)
        for k in range(16):
            slot = g * 16 + k
            live = slot < count
            block_row = jnp.where(live, coords[0, 0, 0, slot], 0)
            block_col = jnp.where(live, coords[0, 0, 1, slot], 0)
            owner = block_row // per_owner
            half = (owner + me_core) & 1
            at_row = (half * PEERS + leaving_place(owner >> 1)) * per_owner + block_row % per_owner
            at_col = relative(block_col // per_owner, *ROW) * per_owner + block_col % per_owner
            odd = (at_col & 1) == 1
            plain = pairs[k]
            turned = pltpu.roll(plain, SIDE, 1)
            block = jnp.concatenate(
                [jnp.where(odd, turned, plain), jnp.where(odd, plain, turned)], axis=0
            ).astype(dense.dtype)
            first = jnp.where(live, (at_col & 1) * SIDE, 4 * SIDE)
            mask = (lane >= first) & (lane < first + SIDE)
            place = dense.at[
                pl.ds(pl.multiple_of(at_row * SIDE, SIDE), SIDE),
                pl.ds(pl.multiple_of((at_col >> 1) * 2 * SIDE, 2 * SIDE), 2 * SIDE),
            ]
            place[...] = jnp.where(mask, block, place[...])


def build(part, coords, counts, values, *dense):
    vmem = pl.BlockSpec(memory_space=pltpu.VMEM)
    return pl.pallas_call(
        functools.partial(build_kernel, part),
        out_shape=bf16(2 * ROWS, ROWS),
        in_specs=[pl.BlockSpec(memory_space=pltpu.SMEM)] * 2 + [vmem] * (1 + len(dense)),
        out_specs=vmem,
        input_output_aliases={3: 0} if dense else {},
        compiler_params=pltpu.CompilerParams(vmem_limit_bytes=16 << 20),
        cost_estimate=pl.CostEstimate(flops=0, bytes_accessed=8 << 20, transcendentals=0),
        name=f"build_{part}",
    )(coords, counts, values, *dense)


def over_rows(a, b):
    return lax.dot_general(a, b, (((0,), (0,)), ((), ())), preferred_element_type=jnp.float32)


def down_kernel(*refs):
    dense, *blocks, out, panel = refs
    for k, block in enumerate(blocks):
        panel[k * OWN : (k + 1) * OWN] = block[...]
    panel[ROWS - OWN :] = jnp.zeros((OWN, WIDTH), panel.dtype)
    for r in range(0, 2 * ROWS, STEP):
        out[r : r + STEP] = jnp.dot(dense[r : r + STEP], panel[...], preferred_element_type=jnp.float32)


def with_last(dense, block, rows):
    padded = jnp.concatenate([jnp.zeros((LAST - OWN, WIDTH), block.dtype), block[...]], axis=0)
    return jnp.dot(dense[rows, ROWS - LAST :], padded, preferred_element_type=jnp.float32)


def down_far_kernel(first, dense, block, most, out):
    for r in range(0, out.shape[0], OWN):
        rows = slice(ROWS + first + r, ROWS + first + r + OWN)
        out[r : r + OWN] = (most[rows] + with_last(dense, block, rows)).astype(out.dtype)


def down_near_kernel(first, dense, block, most, other, *outs):
    for k, out in enumerate(outs):
        rows = slice(first + k * OWN, first + (k + 1) * OWN)
        total = most[rows] + with_last(dense, block, rows)
        out[...] = (total + other[k * OWN : (k + 1) * OWN].astype(jnp.float32)).astype(out.dtype)


def in_order(rows, ordered):
    for place in range(PEERS):
        ordered[place * OWN : (place + 1) * OWN] = rows[leaving_chip(place)]


def up_kernel(dense, rows, out, far, near, ordered, sems):
    strips = [pl.ds(r, STEP) for r in range(0, ROWS, STEP)]
    copies = [
        pltpu.make_async_copy(dense.at[pl.ds(0, ROWS), strip], near.at[:, strip], sems.at[n])
        for n, strip in enumerate(strips)
    ]
    copies.append(pltpu.make_async_copy(dense.at[pl.ds(ROWS, ROWS)], far, sems.at[len(strips)]))
    for copy in copies:
        copy.start()
    in_order(rows, ordered)
    for copy, r in zip(copies, range(0, ROWS, STEP)):
        copy.wait()
        out[r : r + STEP] = over_rows(near[:, r : r + STEP], ordered[...])
    copies[-1].wait()


def up_add_kernel(tile, rows, other, out, ordered):
    in_order(rows, ordered)
    for r in range(0, ROWS, 2 * OWN):
        total = over_rows(tile[:, r : r + 2 * OWN], ordered[...]) + other[r : r + 2 * OWN]
        for k in range(2):
            out[absolute(r // OWN + k, *ROW)] = total[k * OWN : (k + 1) * OWN].astype(out.dtype)


def down_most(dense, blocks):
    return vmem_call(
        down_kernel,
        jax.ShapeDtypeStruct((2 * ROWS, WIDTH), jnp.float32),
        "down_most",
        scratch=[pltpu.VMEM((ROWS, WIDTH), jnp.bfloat16)],
        flops=4 * ROWS * ROWS * WIDTH,
    )(dense, *blocks)


def down_blocks(dense, most, block):
    runs = ((0, FIRST), (FIRST, PEERS - FIRST))
    others = []
    for n, (first, count) in enumerate(runs):
        kernel = functools.partial(down_far_kernel, first * OWN)
        far = vmem_call(kernel, bf16(count * OWN, WIDTH), f"down_far_{n}", flops=2 * count * OWN * LAST * WIDTH)(
            dense, block, most
        )
        far, most = lax.optimization_barrier((far, most))
        others.append(trade(far, "core"))

    def near(n):
        first, count = runs[n]
        kernel = functools.partial(down_near_kernel, first * OWN)
        return vmem_call(
            kernel, (bf16(OWN, WIDTH),) * count, f"down_near_{n}", flops=2 * count * OWN * LAST * WIDTH
        )(dense, block, most, others[n])

    return near(0), lambda: near(1)


def meet_kernel(a, b, c, d, e, out_ab, out_cde):
    out_ab[...] = add(a[...], b[...])
    total = c[...].astype(jnp.float32) + d[...].astype(jnp.float32) + e[...].astype(jnp.float32)
    out_cde[...] = total.astype(out_cde.dtype)


def scatter(first, rest, slow, fast):
    def pass_on(array, step):
        return lax.ppermute(array, fast, [(i, (i + step) % RING) for i in range(RING)])

    s02, s12, s13 = first
    r1, r2, r3 = pass_on(s12, 1), trade(s13, slow), pass_on(s02, -1)
    r1, r2, r3, rest = lax.optimization_barrier((r1, r2, r3, rest()))
    s11, s03, s10, s01, s00 = rest
    block = bf16(OWN, WIDTH)
    t11, t03 = vmem_call(meet_kernel, (block, block), "meet")(s11, r1, s03, r2, r3)
    r4, r5 = lax.optimization_barrier((pass_on(t11, 1), pass_on(t03, -1)))
    t10 = vmem_call(sum_kernel, block, "sum_across")(s10, r4)
    return s00, r5, trade(t10, slow), pass_on(s01, 1)


def middle_kernel(a, b, c, d, out_grad, weight, activations, send, aggregated_out, grad_pre_out):
    total = a[...].astype(jnp.float32)
    for part in (b, c, d):
        total = total + part[...].astype(jnp.float32)
    aggregated = total.astype(jnp.bfloat16)
    at = lax.broadcasted_iota(jnp.int32, (OWN, OWN), 0)
    to = lax.broadcasted_iota(jnp.int32, (OWN, OWN), 1)
    half = SIDE // 2
    turn = jnp.where(
        (at // SIDE == to // SIDE) & (to % SIDE == 2 * (at % half) + (at % SIDE) // half), 1.0, 0.0
    ).astype(jnp.bfloat16)
    w = weight[...]
    pre_act = jnp.dot(aggregated, w, preferred_element_type=jnp.float32)
    sig = jax.nn.sigmoid(pre_act)
    act = (pre_act * sig).astype(jnp.bfloat16)
    activations[...] = over_rows(turn, act).astype(jnp.bfloat16)
    cotangent = jnp.dot(turn, out_grad[...], preferred_element_type=jnp.float32)
    grad_pre = (cotangent * sig * (1.0 + pre_act * (1.0 - sig))).astype(jnp.bfloat16)
    grad_agg = lax.dot_general(
        grad_pre, w, (((1,), (1,)), ((), ())), preferred_element_type=jnp.float32
    ).astype(jnp.bfloat16)
    for k in range(PEERS):
        send[k] = grad_agg
    aggregated_out[...] = aggregated
    grad_pre_out[...] = grad_pre


def wgrad_kernel(aggregated, grad_pre, wgrad_near, wgrad_far, local):
    local[...] = over_rows(aggregated[...], grad_pre[...]).astype(jnp.bfloat16)
    core = lax.axis_index("core")
    for k in range(RING):
        for g in range(RING):
            for out, half_of in ((wgrad_near, core), (wgrad_far, 1 - core)):
                rows, cols = wgrad_place(half_of, k, g)
                out[k * PIECE : (k + 1) * PIECE, g * LANES : (g + 1) * LANES] = local[rows, cols]


def wgrad_place(half_of, k, g):
    row = half_of * (WIDTH // 2) + (lax.axis_index("z") ^ k) * PIECE
    col = ((lax.axis_index("x") + g) & (RING - 1)) * LANES
    return pl.ds(pl.multiple_of(row, PIECE), PIECE), pl.ds(pl.multiple_of(col, LANES), LANES)


def add(a, b):
    return (a.astype(jnp.float32) + b.astype(jnp.float32)).astype(jnp.bfloat16)


def pair_kernel(near, other, *outs):
    for k, out in enumerate(outs):
        rows = slice(k * PIECE, (k + 1) * PIECE)
        out[...] = add(near[rows], other[rows])


def sum_kernel(*refs):
    *parts, out = refs
    total = parts[0][...].astype(jnp.float32)
    for part in parts[1:]:
        total = total + part[...].astype(jnp.float32)
    out[...] = total.astype(out.dtype)


def square_kernel(a, b, c, d, out):
    first = a[...].astype(jnp.float32) + b[...].astype(jnp.float32)
    out[...] = (first + (c[...].astype(jnp.float32) + d[...].astype(jnp.float32))).astype(out.dtype)


def turn_kernel(low, high, *outs):
    rows = low.shape[0]
    for g, out in enumerate(outs):
        for n, part in enumerate((low, high)):
            out[n * rows : (n + 1) * rows] = part[:, g * LANES : (g + 1) * LANES]


def join_kernel(*refs):
    *parts, out = refs
    for g, part in enumerate(parts):
        out[:, g * LANES : (g + 1) * LANES] = part[...]


def place_kernel(mine, theirs, out):
    core = lax.axis_index("core")
    scale = 1.0 / math.sqrt(OWN * PEERS * 2 * PEERS)
    for k in range(RING):
        for g in range(RING):
            for part, half_of in ((mine, core), (theirs, 1 - core)):
                value = part[k * PIECE : (k + 1) * PIECE, g * LANES : (g + 1) * LANES].astype(jnp.float32)
                rows, cols = wgrad_place(half_of, k, g)
                out[rows, cols] = value * jnp.float32(scale)


def exchange(parts, axes):
    return lax.all_to_all(parts, axes, 0, 0)


def trade(array, axes, bits=1):
    return lax.ppermute(array, axes, [(i, i ^ bits) for i in range(lax.axis_size(axes))])


def double_kernel(first, second, out):
    rows = first.shape[0]
    out[:rows] = first[...]
    out[rows:] = second[...]


def gather(block, slow, fast, tasks):
    def ahead(array, step):
        return lax.ppermute(array, fast, [(i, (i - step) % RING) for i in range(RING)])

    across = trade(block, slow)
    before, after = ahead(block, -1), ahead(block, 1)
    across, before, after, state = lax.optimization_barrier((across, before, after, tasks[0](None, None)))
    across_before = trade(before, slow)
    across_after = ahead(across, 1)
    beyond = ahead(before, -1)
    across_before, across_after, beyond, state = lax.optimization_barrier(
        (across_before, across_after, beyond, tasks[1](None, state))
    )
    across_beyond = ahead(across_after, 1)
    blocks = (block, after, before, beyond, across, across_after, across_before)
    return lax.optimization_barrier((across_beyond, tasks[2](blocks, state)))


def scatter_ring(pieces, axis, name):
    arrived = [pieces[0]]
    for k in range(1, RING):
        arrived.append(lax.ppermute(pieces[k], axis, [(i, (i + k) % RING) for i in range(RING)]))
    return vmem_call(sum_kernel, bf16(*pieces[0].shape), name)(*arrived)


def gather_ring(piece, axis):
    pieces = [piece]
    for k in range(1, RING):
        pieces.append(lax.ppermute(piece, axis, [(i, (i - k) % RING) for i in range(RING)]))
    return pieces


def per_device(features, out_grad, weight, block_values, block_coords, block_counts):
    raw = (block_coords, block_counts, block_values)
    tasks = (
        lambda blocks, dense: build(0, *raw),
        lambda blocks, dense: build(1, *raw, dense),
        lambda blocks, dense: (dense, down_most(dense, blocks)),
    )
    block, (dense, most) = gather(features, *ROW, tasks)
    parts = scatter(*down_blocks(dense, most, block), *CHIP)

    half = bf16(WIDTH // 2, WIDTH)
    own = bf16(OWN, WIDTH)
    activations, send, aggregated, grad_pre = vmem_call(
        middle_kernel, (own, bf16(PEERS, OWN, WIDTH), own, own), "middle", flops=2 * 2 * OWN * WIDTH * WIDTH
    )(*parts, out_grad, weight)
    wgrads = vmem_call(
        wgrad_kernel,
        (half, half),
        "wgrad",
        scratch=[pltpu.VMEM((WIDTH, WIDTH), jnp.bfloat16)],
        flops=2 * OWN * WIDTH * WIDTH,
    )(aggregated, grad_pre)

    piece = bf16(PIECE, WIDTH)
    ys = ("y_lo", "y_hi")

    def over_core(terms):
        return vmem_call(pair_kernel, (piece,) * RING, "pair")(terms[0], trade(terms[1], "core"))

    def over_z(pieces):
        arrived = [pieces[0]] + [trade(pieces[k], "z", k) for k in range(1, RING)]
        return vmem_call(sum_kernel, piece, "sum_z")(*arrived)

    def over_y(summed):
        return vmem_call(square_kernel, piece, "sum_y")(
            summed, trade(summed, ys, 1), trade(summed, ys, 2), trade(summed, ys, 3)
        )

    mine = exchange(send, CHIP)
    summed = over_y(over_z(over_core(wgrads)))
    summed, mine = lax.optimization_barrier((summed, mine))

    theirs = trade(mine, "core")
    work = 2 * ROWS * ROWS * WIDTH
    vmem = pl.BlockSpec(memory_space=pltpu.VMEM)
    own, far = pl.pallas_call(
        up_kernel,
        out_shape=(jax.ShapeDtypeStruct((ROWS, WIDTH), jnp.float32), bf16(ROWS, ROWS)),
        in_specs=[pl.BlockSpec(memory_space=pltpu.HBM), vmem],
        out_specs=(vmem, vmem),
        scratch_shapes=[
            pltpu.VMEM((ROWS, ROWS), jnp.bfloat16),
            pltpu.VMEM((ROWS, WIDTH), jnp.bfloat16),
            pltpu.SemaphoreType.DMA((ROWS // STEP + 1,)),
        ],
        compiler_params=pltpu.CompilerParams(vmem_limit_bytes=44 << 20),
        cost_estimate=pl.CostEstimate(flops=work, bytes_accessed=12 << 20, transcendentals=0),
        name="up_near",
    )(dense, mine)
    next_piece, own = lax.optimization_barrier((trade(summed, "z", 1), own))
    pair = vmem_call(double_kernel, bf16(2 * PIECE, WIDTH), "double")(summed, next_piece)
    ordered = pltpu.VMEM((ROWS, WIDTH), jnp.bfloat16)
    partial_grad = vmem_call(
        up_add_kernel, bf16(PEERS, OWN, WIDTH), "up_far", scratch=[ordered], flops=work
    )(far, theirs, own)
    pairs = (pair, trade(pair, "z", 2))
    partial_grad, *pairs = lax.optimization_barrier((partial_grad, *pairs))
    received = exchange(partial_grad, ROW)

    column = bf16(WIDTH // 2, LANES)
    columns = vmem_call(turn_kernel, (column,) * RING, "turn")(*pairs)
    summed = scatter_ring(columns, "x", "sum_x")
    columns = gather_ring(summed, "x")
    own_half = vmem_call(join_kernel, half, "join")(*columns)
    weight_grad = vmem_call(place_kernel, jax.ShapeDtypeStruct((WIDTH, WIDTH), jnp.float32), "place")(
        own_half, trade(own_half, "core")
    )

    total = received[0].astype(jnp.float32)
    for k in range(1, PEERS):
        total = total + received[k].astype(jnp.float32)
    feature_grad = total.astype(jnp.bfloat16)
    return (activations, weight_grad, feature_grad)


def solution(mesh):
    fine = Mesh(mesh.devices.reshape(SIZES), AXES)
    return jax.shard_map(
        per_device,
        mesh=fine,
        in_specs=(
            P(COL + ROW, None),
            P(ROW + COL, None),
            P(),
            P(ROW, COL, None, None),
            P(ROW, COL, None, None),
            P(ROW, COL),
        ),
        out_specs=(P(ROW + COL, None), P(), P(COL + ROW, None)),
        check_vma=False,
    )
```

```python
import functools
import math

import jax
import jax.numpy as jnp
from jax import lax
from jax.experimental import pallas as pl
from jax.experimental.pallas import tpu as pltpu
from jax.sharding import Mesh, PartitionSpec as P

AXES = ("y_lo", "z", "y_hi", "x", "core")
SIZES = (2, 4, 2, 4, 2)
ROW = ("y_lo", "z")
CHIP = ("y_hi", "x")
COL = ("y_hi", "x", "core")
SIDE = 64
PEERS = 8
OWN = 192
WIDTH = 512
ROWS = PEERS * OWN
STEP = 256
RING = 4
PARTS = 2
LAST = 2 * SIDE * 2
PIECE = WIDTH // 2 // RING
LANES = WIDTH // RING


def vmem_call(kernel, outs, name, scratch=(), flops=0, moved=1 << 20, limit=16 << 20, aliases={}):
    vmem = pl.BlockSpec(memory_space=pltpu.VMEM)

    def call(*args):
        return pl.pallas_call(
            kernel,
            out_shape=outs,
            in_specs=[vmem] * len(args),
            out_specs=jax.tree.map(lambda _: vmem, outs),
            scratch_shapes=scratch,
            input_output_aliases=aliases,
            compiler_params=pltpu.CompilerParams(vmem_limit_bytes=limit),
            cost_estimate=pl.CostEstimate(flops=flops, bytes_accessed=moved, transcendentals=0),
            name=name,
        )(*args)

    return call


def bf16(*shape):
    return jax.ShapeDtypeStruct(shape, jnp.bfloat16)


def relative(owner, slow, fast):
    apart = (owner >> 2) ^ lax.axis_index(slow)
    ahead = ((owner & (RING - 1)) - lax.axis_index(fast)) & (RING - 1)
    return apart * RING + (ahead ^ (ahead >> 1))


def absolute(place, slow, fast):
    apart, ahead = divmod(place, RING)
    ahead ^= ahead >> 1
    return (lax.axis_index(slow) ^ apart) * RING + ((lax.axis_index(fast) + ahead) & (RING - 1))


LEAVING = ((0, 2), (1, 2), (1, 3), (1, 1), (0, 3), (1, 0), (0, 1), (0, 0))
FIRST = 3


def leaving_place(chip):
    table = sum(place << 4 * (RING * apart + ahead) for place, (apart, ahead) in enumerate(LEAVING))
    apart = (chip >> 2) ^ lax.axis_index("y_hi")
    ahead = ((chip & (RING - 1)) - lax.axis_index("x")) & (RING - 1)
    return (table >> (4 * (RING * apart + ahead))) & 15


def leaving_chip(place):
    apart, ahead = LEAVING[place]
    return (lax.axis_index("y_hi") ^ apart) * RING + ((lax.axis_index("x") + ahead) & (RING - 1))


def build_kernel(part, coords, counts, values, *rest):
    dense = rest[-1]
    rows, cols = dense.shape
    per_owner = OWN // SIDE
    me_core = lax.axis_index("core")

    if part == 0:

        @pl.loop(0, rows // SIDE)
        def _(r):
            dense[pl.ds(pl.multiple_of(r * SIDE, SIDE), SIDE), :] = jnp.zeros((SIDE, cols), dense.dtype)

    count = counts[0, 0]
    lane = lax.broadcasted_iota(jnp.int32, (SIDE, 2 * SIDE), 1)

    groups = (count + 15) >> 4

    @pl.loop((groups * part) // PARTS, (groups * (part + 1)) // PARTS)
    def _(g):
        group = values[0, 0, pl.ds(pl.multiple_of(g * 16, 16), 16), :]
        pairs = group.astype(jnp.float32).reshape(16, SIDE // 2, 2 * SIDE)
        for k in range(16):
            slot = g * 16 + k
            live = slot < count
            block_row = jnp.where(live, coords[0, 0, 0, slot], 0)
            block_col = jnp.where(live, coords[0, 0, 1, slot], 0)
            owner = block_row // per_owner
            half = (owner + me_core) & 1
            at_row = (half * PEERS + leaving_place(owner >> 1)) * per_owner + block_row % per_owner
            at_col = relative(block_col // per_owner, *ROW) * per_owner + block_col % per_owner
            odd = (at_col & 1) == 1
            plain = pairs[k]
            turned = pltpu.roll(plain, SIDE, 1)
            block = jnp.concatenate(
                [jnp.where(odd, turned, plain), jnp.where(odd, plain, turned)], axis=0
            ).astype(dense.dtype)
            first = jnp.where(live, (at_col & 1) * SIDE, 4 * SIDE)
            mask = (lane >= first) & (lane < first + SIDE)
            place = dense.at[
                pl.ds(pl.multiple_of(at_row * SIDE, SIDE), SIDE),
                pl.ds(pl.multiple_of((at_col >> 1) * 2 * SIDE, 2 * SIDE), 2 * SIDE),
            ]
            place[...] = jnp.where(mask, block, place[...])


def build(part, coords, counts, values, *dense):
    vmem = pl.BlockSpec(memory_space=pltpu.VMEM)
    return pl.pallas_call(
        functools.partial(build_kernel, part),
        out_shape=bf16(2 * ROWS, ROWS),
        in_specs=[pl.BlockSpec(memory_space=pltpu.SMEM)] * 2 + [vmem] * (1 + len(dense)),
        out_specs=vmem,
        input_output_aliases={3: 0} if dense else {},
        compiler_params=pltpu.CompilerParams(vmem_limit_bytes=16 << 20),
        cost_estimate=pl.CostEstimate(flops=0, bytes_accessed=8 << 20, transcendentals=0),
        name=f"build_{part}",
    )(coords, counts, values, *dense)


def over_rows(a, b):
    return lax.dot_general(a, b, (((0,), (0,)), ((), ())), preferred_element_type=jnp.float32)


def down_kernel(*refs):
    dense, *blocks, out, panel = refs
    for k, block in enumerate(blocks):
        panel[k * OWN : (k + 1) * OWN] = block[...]
    panel[ROWS - OWN :] = jnp.zeros((OWN, WIDTH), panel.dtype)
    for r in range(0, 2 * ROWS, STEP):
        out[r : r + STEP] = jnp.dot(dense[r : r + STEP], panel[...], preferred_element_type=jnp.float32)


def with_last(dense, block, rows):
    padded = jnp.concatenate([jnp.zeros((LAST - OWN, WIDTH), block.dtype), block[...]], axis=0)
    return jnp.dot(dense[rows, ROWS - LAST :], padded, preferred_element_type=jnp.float32)


def down_far_kernel(first, dense, block, most, out):
    for r in range(0, out.shape[0], OWN):
        rows = slice(ROWS + first + r, ROWS + first + r + OWN)
        out[r : r + OWN] = (most[rows] + with_last(dense, block, rows)).astype(out.dtype)


def down_near_kernel(first, dense, block, most, other, *outs):
    for k, out in enumerate(outs):
        rows = slice(first + k * OWN, first + (k + 1) * OWN)
        total = most[rows] + with_last(dense, block, rows)
        out[...] = (total + other[k * OWN : (k + 1) * OWN].astype(jnp.float32)).astype(out.dtype)


def in_order(rows, ordered):
    for place in range(PEERS):
        ordered[place * OWN : (place + 1) * OWN] = rows[leaving_chip(place)]


def up_kernel(dense, rows, out, far, near, ordered, sems):
    strips = [pl.ds(r, STEP) for r in range(0, ROWS, STEP)]
    copies = [
        pltpu.make_async_copy(dense.at[pl.ds(0, ROWS), strip], near.at[:, strip], sems.at[n])
        for n, strip in enumerate(strips)
    ]
    copies.append(pltpu.make_async_copy(dense.at[pl.ds(ROWS, ROWS)], far, sems.at[len(strips)]))
    for copy in copies:
        copy.start()
    in_order(rows, ordered)
    for copy, r in zip(copies, range(0, ROWS, STEP)):
        copy.wait()
        out[r : r + STEP] = over_rows(near[:, r : r + STEP], ordered[...])
    copies[-1].wait()


def up_add_kernel(tile, rows, other, out, ordered):
    in_order(rows, ordered)
    for r in range(0, ROWS, 2 * OWN):
        total = over_rows(tile[:, r : r + 2 * OWN], ordered[...]) + other[r : r + 2 * OWN]
        for k in range(2):
            out[absolute(r // OWN + k, *ROW)] = total[k * OWN : (k + 1) * OWN].astype(out.dtype)


def down_most(dense, blocks):
    return vmem_call(
        down_kernel,
        jax.ShapeDtypeStruct((2 * ROWS, WIDTH), jnp.float32),
        "down_most",
        scratch=[pltpu.VMEM((ROWS, WIDTH), jnp.bfloat16)],
        flops=4 * ROWS * ROWS * WIDTH,
    )(dense, *blocks)


def down_blocks(dense, most, block):
    runs = ((0, FIRST), (FIRST, PEERS - FIRST))
    others = []
    for n, (first, count) in enumerate(runs):
        kernel = functools.partial(down_far_kernel, first * OWN)
        far = vmem_call(kernel, bf16(count * OWN, WIDTH), f"down_far_{n}", flops=2 * count * OWN * LAST * WIDTH)(
            dense, block, most
        )
        other = trade(far, "core")
        if n == 0:
            other, most = lax.optimization_barrier((other, most))
        others.append(other)

    def near(n):
        first, count = runs[n]
        kernel = functools.partial(down_near_kernel, first * OWN)
        return vmem_call(
            kernel, (bf16(OWN, WIDTH),) * count, f"down_near_{n}", flops=2 * count * OWN * LAST * WIDTH
        )(dense, block, most, others[n])

    return near(0), lambda: near(1)


def meet_kernel(a, b, c, d, e, out_ab, out_cde):
    out_ab[...] = add(a[...], b[...])
    total = c[...].astype(jnp.float32) + d[...].astype(jnp.float32) + e[...].astype(jnp.float32)
    out_cde[...] = total.astype(out_cde.dtype)


def scatter(first, rest, slow, fast):
    def pass_on(array, step):
        return lax.ppermute(array, fast, [(i, (i + step) % RING) for i in range(RING)])

    s02, s12, s13 = first
    r1, r2, r3 = pass_on(s12, 1), trade(s13, slow), pass_on(s02, -1)
    r1, r2, r3, rest = lax.optimization_barrier((r1, r2, r3, rest()))
    s11, s03, s10, s01, s00 = rest
    block = bf16(OWN, WIDTH)
    t11, t03 = vmem_call(meet_kernel, (block, block), "meet")(s11, r1, s03, r2, r3)
    r4, r5 = lax.optimization_barrier((pass_on(t11, 1), pass_on(t03, -1)))
    t10 = vmem_call(sum_kernel, block, "sum_across")(s10, r4)
    return s00, r5, trade(t10, slow), pass_on(s01, 1)


def middle_kernel(a, b, c, d, out_grad, weight, activations, aggregated_out, grad_pre_out, send, grad_agg, sems):
    total = a[...].astype(jnp.float32)
    for part in (b, c, d):
        total = total + part[...].astype(jnp.float32)
    aggregated = total.astype(jnp.bfloat16)
    at = lax.broadcasted_iota(jnp.int32, (OWN, OWN), 0)
    to = lax.broadcasted_iota(jnp.int32, (OWN, OWN), 1)
    half = SIDE // 2
    turn = jnp.where(
        (at // SIDE == to // SIDE) & (to % SIDE == 2 * (at % half) + (at % SIDE) // half), 1.0, 0.0
    ).astype(jnp.bfloat16)
    w = weight[...]
    pre_act = jnp.dot(aggregated, w, preferred_element_type=jnp.float32)
    sig = jax.nn.sigmoid(pre_act)
    cotangent = jnp.dot(turn, out_grad[...], preferred_element_type=jnp.float32)
    grad_pre = (cotangent * sig * (1.0 + pre_act * (1.0 - sig))).astype(jnp.bfloat16)
    grad_agg[...] = lax.dot_general(
        grad_pre, w, (((1,), (1,)), ((), ())), preferred_element_type=jnp.float32
    ).astype(jnp.bfloat16)
    copies = [pltpu.make_async_copy(grad_agg, send.at[k], sems.at[k]) for k in range(PEERS)]
    for copy in copies:
        copy.start()
    act = (pre_act * sig).astype(jnp.bfloat16)
    activations[...] = over_rows(turn, act).astype(jnp.bfloat16)
    aggregated_out[...] = aggregated
    grad_pre_out[...] = grad_pre
    for copy in copies:
        copy.wait()


def wgrad_kernel(aggregated, grad_pre, wgrad_near, wgrad_far, local):
    local[...] = over_rows(aggregated[...], grad_pre[...]).astype(jnp.bfloat16)
    core = lax.axis_index("core")
    for k in range(RING):
        for g in range(RING):
            for out, half_of in ((wgrad_near, core), (wgrad_far, 1 - core)):
                rows, cols = wgrad_place(half_of, k, g)
                out[k * PIECE : (k + 1) * PIECE, g * LANES : (g + 1) * LANES] = local[rows, cols]


def wgrad_place(half_of, k, g):
    row = half_of * (WIDTH // 2) + (lax.axis_index("z") ^ k) * PIECE
    col = ((lax.axis_index("x") + g) & (RING - 1)) * LANES
    return pl.ds(pl.multiple_of(row, PIECE), PIECE), pl.ds(pl.multiple_of(col, LANES), LANES)


def add(a, b):
    return (a.astype(jnp.float32) + b.astype(jnp.float32)).astype(jnp.bfloat16)


def pair_kernel(near, other, *outs):
    for k, out in enumerate(outs):
        rows = slice(k * PIECE, (k + 1) * PIECE)
        out[...] = add(near[rows], other[rows])


def sum_kernel(*refs):
    *parts, out = refs
    total = parts[0][...].astype(jnp.float32)
    for part in parts[1:]:
        total = total + part[...].astype(jnp.float32)
    out[...] = total.astype(out.dtype)


def square_kernel(a, b, c, d, out):
    first = a[...].astype(jnp.float32) + b[...].astype(jnp.float32)
    out[...] = (first + (c[...].astype(jnp.float32) + d[...].astype(jnp.float32))).astype(out.dtype)


def turn_kernel(low, high, *outs):
    rows = low.shape[0]
    for g, out in enumerate(outs):
        for n, part in enumerate((low, high)):
            out[n * rows : (n + 1) * rows] = part[:, g * LANES : (g + 1) * LANES]


def join_kernel(*refs):
    *parts, out = refs
    for g, part in enumerate(parts):
        out[:, g * LANES : (g + 1) * LANES] = part[...]


def place_kernel(mine, theirs, out):
    core = lax.axis_index("core")
    scale = 1.0 / math.sqrt(OWN * PEERS * 2 * PEERS)
    for k in range(RING):
        for g in range(RING):
            for part, half_of in ((mine, core), (theirs, 1 - core)):
                value = part[k * PIECE : (k + 1) * PIECE, g * LANES : (g + 1) * LANES].astype(jnp.float32)
                rows, cols = wgrad_place(half_of, k, g)
                out[rows, cols] = value * jnp.float32(scale)


def exchange(parts, axes):
    return lax.all_to_all(parts, axes, 0, 0)


def trade(array, axes, bits=1):
    return lax.ppermute(array, axes, [(i, i ^ bits) for i in range(lax.axis_size(axes))])


def double_kernel(first, second, out):
    rows = first.shape[0]
    out[:rows] = first[...]
    out[rows:] = second[...]


def gather(block, slow, fast, tasks):
    def ahead(array, step):
        return lax.ppermute(array, fast, [(i, (i - step) % RING) for i in range(RING)])

    across = trade(block, slow)
    before, after = ahead(block, -1), ahead(block, 1)
    across, before, after, state = lax.optimization_barrier((across, before, after, tasks[0](None, None)))
    across_before = trade(before, slow)
    across_after = ahead(across, 1)
    beyond = ahead(before, -1)
    across_before, across_after, beyond, state = lax.optimization_barrier(
        (across_before, across_after, beyond, tasks[1](None, state))
    )
    across_beyond = ahead(across_after, 1)
    blocks = (block, after, before, beyond, across, across_after, across_before)
    return lax.optimization_barrier((across_beyond, tasks[2](blocks, state)))


def scatter_ring(pieces, axis, name):
    arrived = [pieces[0]]
    for k in range(1, RING):
        arrived.append(lax.ppermute(pieces[k], axis, [(i, (i + k) % RING) for i in range(RING)]))
    return vmem_call(sum_kernel, bf16(*pieces[0].shape), name)(*arrived)


def gather_ring(piece, axis):
    pieces = [piece]
    for k in range(1, RING):
        pieces.append(lax.ppermute(piece, axis, [(i, (i - k) % RING) for i in range(RING)]))
    return pieces


def per_device(features, out_grad, weight, block_values, block_coords, block_counts):
    raw = (block_coords, block_counts, block_values)
    tasks = (
        lambda blocks, dense: build(0, *raw),
        lambda blocks, dense: build(1, *raw, dense),
        lambda blocks, dense: (dense, down_most(dense, blocks)),
    )
    block, (dense, most) = gather(features, *ROW, tasks)
    parts = scatter(*down_blocks(dense, most, block), *CHIP)

    half = bf16(WIDTH // 2, WIDTH)
    own = bf16(OWN, WIDTH)
    vmem = pl.BlockSpec(memory_space=pltpu.VMEM)
    activations, aggregated, grad_pre, send = pl.pallas_call(
        middle_kernel,
        out_shape=(own, own, own, bf16(PEERS, OWN, WIDTH)),
        in_specs=[vmem] * 6,
        out_specs=(vmem, vmem, vmem, pl.BlockSpec(memory_space=pltpu.HBM)),
        scratch_shapes=[pltpu.VMEM((OWN, WIDTH), jnp.bfloat16), pltpu.SemaphoreType.DMA((PEERS,))],
        compiler_params=pltpu.CompilerParams(vmem_limit_bytes=16 << 20),
        cost_estimate=pl.CostEstimate(
            flops=2 * 2 * OWN * WIDTH * WIDTH, bytes_accessed=4 << 20, transcendentals=OWN * WIDTH
        ),
        name="middle",
    )(*parts, out_grad, weight)
    wgrads = vmem_call(
        wgrad_kernel,
        (half, half),
        "wgrad",
        scratch=[pltpu.VMEM((WIDTH, WIDTH), jnp.bfloat16)],
        flops=2 * OWN * WIDTH * WIDTH,
    )(aggregated, grad_pre)

    piece = bf16(PIECE, WIDTH)
    ys = ("y_lo", "y_hi")

    def over_core(terms):
        return vmem_call(pair_kernel, (piece,) * RING, "pair")(terms[0], trade(terms[1], "core"))

    def over_z(pieces):
        arrived = [pieces[0]] + [trade(pieces[k], "z", k) for k in range(1, RING)]
        return vmem_call(sum_kernel, piece, "sum_z")(*arrived)

    def over_y(summed):
        return vmem_call(square_kernel, piece, "sum_y")(
            summed, trade(summed, ys, 1), trade(summed, ys, 2), trade(summed, ys, 3)
        )

    mine = exchange(send, CHIP)
    summed = over_y(over_z(over_core(wgrads)))
    summed, mine = lax.optimization_barrier((summed, mine))

    theirs = trade(mine, "core")
    work = 2 * ROWS * ROWS * WIDTH
    own, far = pl.pallas_call(
        up_kernel,
        out_shape=(jax.ShapeDtypeStruct((ROWS, WIDTH), jnp.float32), bf16(ROWS, ROWS)),
        in_specs=[pl.BlockSpec(memory_space=pltpu.HBM), vmem],
        out_specs=(vmem, vmem),
        scratch_shapes=[
            pltpu.VMEM((ROWS, ROWS), jnp.bfloat16),
            pltpu.VMEM((ROWS, WIDTH), jnp.bfloat16),
            pltpu.SemaphoreType.DMA((ROWS // STEP + 1,)),
        ],
        compiler_params=pltpu.CompilerParams(vmem_limit_bytes=44 << 20),
        cost_estimate=pl.CostEstimate(flops=work, bytes_accessed=12 << 20, transcendentals=0),
        name="up_near",
    )(dense, mine)
    next_piece, own = lax.optimization_barrier((trade(summed, "z", 1), own))
    pair = vmem_call(double_kernel, bf16(2 * PIECE, WIDTH), "double")(summed, next_piece)
    ordered = pltpu.VMEM((ROWS, WIDTH), jnp.bfloat16)
    partial_grad = vmem_call(
        up_add_kernel, bf16(PEERS, OWN, WIDTH), "up_far", scratch=[ordered], flops=work
    )(far, theirs, own)
    pairs = (pair, trade(pair, "z", 2))
    partial_grad, *pairs = lax.optimization_barrier((partial_grad, *pairs))
    received = exchange(partial_grad, ROW)

    column = bf16(WIDTH // 2, LANES)
    columns = vmem_call(turn_kernel, (column,) * RING, "turn")(*pairs)
    summed = scatter_ring(columns, "x", "sum_x")
    columns = gather_ring(summed, "x")
    own_half = vmem_call(join_kernel, half, "join")(*columns)
    weight_grad = vmem_call(place_kernel, jax.ShapeDtypeStruct((WIDTH, WIDTH), jnp.float32), "place")(
        own_half, trade(own_half, "core")
    )

    total = received[0].astype(jnp.float32)
    for k in range(1, PEERS):
        total = total + received[k].astype(jnp.float32)
    feature_grad = total.astype(jnp.bfloat16)
    return (activations, weight_grad, feature_grad)


def solution(mesh):
    fine = Mesh(mesh.devices.reshape(SIZES), AXES)
    return jax.shard_map(
        per_device,
        mesh=fine,
        in_specs=(
            P(COL + ROW, None),
            P(ROW + COL, None),
            P(),
            P(ROW, COL, None, None),
            P(ROW, COL, None, None),
            P(ROW, COL),
        ),
        out_specs=(P(ROW + COL, None), P(), P(COL + ROW, None)),
        check_vma=False,
    )
```

```python
import functools
import math

import jax
import jax.numpy as jnp
from jax import lax
from jax.experimental import pallas as pl
from jax.experimental.pallas import tpu as pltpu
from jax.sharding import Mesh, PartitionSpec as P

AXES = ("y_lo", "z", "y_hi", "x", "core")
SIZES = (2, 4, 2, 4, 2)
ROW = ("y_lo", "z")
CHIP = ("y_hi", "x")
COL = ("y_hi", "x", "core")
SIDE = 64
PEERS = 8
OWN = 192
WIDTH = 512
ROWS = PEERS * OWN
STEP = 256
RING = 4
PARTS = 2
LAST = 2 * SIDE * 2
PIECE = WIDTH // 2 // RING
LANES = WIDTH // RING


def vmem_call(kernel, outs, name, scratch=(), flops=0, moved=1 << 20, limit=16 << 20, aliases={}):
    vmem = pl.BlockSpec(memory_space=pltpu.VMEM)

    def call(*args):
        return pl.pallas_call(
            kernel,
            out_shape=outs,
            in_specs=[vmem] * len(args),
            out_specs=jax.tree.map(lambda _: vmem, outs),
            scratch_shapes=scratch,
            input_output_aliases=aliases,
            compiler_params=pltpu.CompilerParams(vmem_limit_bytes=limit),
            cost_estimate=pl.CostEstimate(flops=flops, bytes_accessed=moved, transcendentals=0),
            name=name,
        )(*args)

    return call


def bf16(*shape):
    return jax.ShapeDtypeStruct(shape, jnp.bfloat16)


def relative(owner, slow, fast):
    apart = (owner >> 2) ^ lax.axis_index(slow)
    ahead = ((owner & (RING - 1)) - lax.axis_index(fast)) & (RING - 1)
    return apart * RING + (ahead ^ (ahead >> 1))


def absolute(place, slow, fast):
    apart, ahead = divmod(place, RING)
    ahead ^= ahead >> 1
    return (lax.axis_index(slow) ^ apart) * RING + ((lax.axis_index(fast) + ahead) & (RING - 1))


LEAVING = ((0, 2), (1, 2), (1, 3), (1, 1), (0, 3), (1, 0), (0, 1), (0, 0))
FIRST = 3


def leaving_place(chip):
    table = sum(place << 4 * (RING * apart + ahead) for place, (apart, ahead) in enumerate(LEAVING))
    apart = (chip >> 2) ^ lax.axis_index("y_hi")
    ahead = ((chip & (RING - 1)) - lax.axis_index("x")) & (RING - 1)
    return (table >> (4 * (RING * apart + ahead))) & 15


def leaving_chip(place):
    apart, ahead = LEAVING[place]
    return (lax.axis_index("y_hi") ^ apart) * RING + ((lax.axis_index("x") + ahead) & (RING - 1))


def build_places(coords, counts):
    per_owner = OWN // SIDE
    block_row, block_col = coords[0, 0, 0], coords[0, 0, 1]
    live = lax.iota(jnp.int32, block_row.shape[0]) < counts[0, 0]
    owner = block_row // per_owner
    half = (owner + lax.axis_index("core")) & 1
    at_row = (half * PEERS + leaving_place(owner >> 1)) * per_owner + block_row % per_owner
    at_col = relative(block_col // per_owner, *ROW) * per_owner + block_col % per_owner
    return jnp.where(live, at_row + (at_col << 8), 1 << 16)


def build_kernel(part, places, counts, values, *rest):
    dense = rest[-1]
    rows, cols = dense.shape

    if part == 0:

        @pl.loop(0, rows // SIDE)
        def _(r):
            dense[pl.ds(pl.multiple_of(r * SIDE, SIDE), SIDE), :] = jnp.zeros((SIDE, cols), dense.dtype)

    lane = lax.broadcasted_iota(jnp.int32, (SIDE, 2 * SIDE), 1)
    groups = (counts[0, 0] + 15) >> 4

    @pl.loop((groups * part) // PARTS, (groups * (part + 1)) // PARTS)
    def _(g):
        group = values[0, 0, pl.ds(pl.multiple_of(g * 16, 16), 16), :]
        pairs = group.astype(jnp.float32).reshape(16, SIDE // 2, 2 * SIDE)
        for k in range(16):
            slot = g * 16 + k
            code = places[slot]
            at_row, at_col = code & 255, (code >> 8) & 255
            row, col = at_row * SIDE, (at_col >> 1) * 2 * SIDE
            odd = (at_col & 1) == 1
            first = (at_col & 1) * SIDE + (code >> 16) * 4 * SIDE
            plain = pairs[k]
            turned = pltpu.roll(plain, SIDE, 1)
            block = jnp.concatenate(
                [jnp.where(odd, turned, plain), jnp.where(odd, plain, turned)], axis=0
            ).astype(dense.dtype)
            mask = (lane >= first) & (lane < first + SIDE)
            place = dense.at[
                pl.ds(pl.multiple_of(row, SIDE), SIDE), pl.ds(pl.multiple_of(col, 2 * SIDE), 2 * SIDE)
            ]
            place[...] = jnp.where(mask, block, place[...])


def build(part, places, counts, values, *dense):
    vmem = pl.BlockSpec(memory_space=pltpu.VMEM)
    return pl.pallas_call(
        functools.partial(build_kernel, part),
        out_shape=bf16(2 * ROWS, ROWS),
        in_specs=[pl.BlockSpec(memory_space=pltpu.SMEM)] * 2 + [vmem] * (1 + len(dense)),
        out_specs=vmem,
        input_output_aliases={3: 0} if dense else {},
        compiler_params=pltpu.CompilerParams(vmem_limit_bytes=16 << 20),
        cost_estimate=pl.CostEstimate(flops=0, bytes_accessed=8 << 20, transcendentals=0),
        name=f"build_{part}",
    )(places, counts, values, *dense)


def over_rows(a, b):
    return lax.dot_general(a, b, (((0,), (0,)), ((), ())), preferred_element_type=jnp.float32)


def down_kernel(*refs):
    dense, *blocks, out, panel = refs
    for k, block in enumerate(blocks):
        panel[k * OWN : (k + 1) * OWN] = block[...]
    panel[ROWS - OWN :] = jnp.zeros((OWN, WIDTH), panel.dtype)
    for r in range(0, 2 * ROWS, STEP):
        out[r : r + STEP] = jnp.dot(dense[r : r + STEP], panel[...], preferred_element_type=jnp.float32)


def with_last(dense, block, rows):
    padded = jnp.concatenate([jnp.zeros((LAST - OWN, WIDTH), block.dtype), block[...]], axis=0)
    return jnp.dot(dense[rows, ROWS - LAST :], padded, preferred_element_type=jnp.float32)


def down_far_kernel(first, dense, block, most, out):
    for r in range(0, out.shape[0], OWN):
        rows = slice(ROWS + first + r, ROWS + first + r + OWN)
        out[r : r + OWN] = (most[rows] + with_last(dense, block, rows)).astype(out.dtype)


def down_near_kernel(first, dense, block, most, other, *outs):
    for k, out in enumerate(outs):
        rows = slice(first + k * OWN, first + (k + 1) * OWN)
        total = most[rows] + with_last(dense, block, rows)
        out[...] = (total + other[k * OWN : (k + 1) * OWN].astype(jnp.float32)).astype(out.dtype)


def in_order(rows, ordered):
    for place in range(PEERS):
        ordered[place * OWN : (place + 1) * OWN] = rows[leaving_chip(place)]


def up_kernel(dense, rows, out, far, near, ordered, sems):
    strips = [pl.ds(r, STEP) for r in range(0, ROWS, STEP)]
    copies = [
        pltpu.make_async_copy(dense.at[pl.ds(0, ROWS), strip], near.at[:, strip], sems.at[n])
        for n, strip in enumerate(strips)
    ]
    copies.append(pltpu.make_async_copy(dense.at[pl.ds(ROWS, ROWS)], far, sems.at[len(strips)]))
    for copy in copies:
        copy.start()
    in_order(rows, ordered)
    for copy, r in zip(copies, range(0, ROWS, STEP)):
        copy.wait()
        out[r : r + STEP] = over_rows(near[:, r : r + STEP], ordered[...])
    copies[-1].wait()


def up_add_kernel(tile, rows, other, out, ordered):
    in_order(rows, ordered)
    for r in range(0, ROWS, 2 * OWN):
        total = over_rows(tile[:, r : r + 2 * OWN], ordered[...]) + other[r : r + 2 * OWN]
        for k in range(2):
            out[absolute(r // OWN + k, *ROW)] = total[k * OWN : (k + 1) * OWN].astype(out.dtype)


def down_most(dense, blocks):
    return vmem_call(
        down_kernel,
        jax.ShapeDtypeStruct((2 * ROWS, WIDTH), jnp.float32),
        "down_most",
        scratch=[pltpu.VMEM((ROWS, WIDTH), jnp.bfloat16)],
        flops=4 * ROWS * ROWS * WIDTH,
    )(dense, *blocks)


def down_blocks(dense, most, block):
    runs = ((0, FIRST), (FIRST, PEERS - FIRST))
    others = []
    for n, (first, count) in enumerate(runs):
        kernel = functools.partial(down_far_kernel, first * OWN)
        far = vmem_call(kernel, bf16(count * OWN, WIDTH), f"down_far_{n}", flops=2 * count * OWN * LAST * WIDTH)(
            dense, block, most
        )
        other = trade(far, "core")
        if n == 0:
            other, most = lax.optimization_barrier((other, most))
        others.append(other)

    def near(n):
        first, count = runs[n]
        kernel = functools.partial(down_near_kernel, first * OWN)
        return vmem_call(
            kernel, (bf16(OWN, WIDTH),) * count, f"down_near_{n}", flops=2 * count * OWN * LAST * WIDTH
        )(dense, block, most, others[n])

    return near(0), lambda: near(1)


def meet_kernel(a, b, c, d, e, out_ab, out_cde):
    out_ab[...] = add(a[...], b[...])
    total = c[...].astype(jnp.float32) + d[...].astype(jnp.float32) + e[...].astype(jnp.float32)
    out_cde[...] = total.astype(out_cde.dtype)


def scatter(first, rest, slow, fast):
    def pass_on(array, step):
        return lax.ppermute(array, fast, [(i, (i + step) % RING) for i in range(RING)])

    s02, s12, s13 = first
    r1, r2, r3 = pass_on(s12, 1), trade(s13, slow), pass_on(s02, -1)
    r1, r2, r3, rest = lax.optimization_barrier((r1, r2, r3, rest()))
    s11, s03, s10, s01, s00 = rest
    block = bf16(OWN, WIDTH)
    t11, t03 = vmem_call(meet_kernel, (block, block), "meet")(s11, r1, s03, r2, r3)
    r4, r5 = lax.optimization_barrier((pass_on(t11, 1), pass_on(t03, -1)))
    t10 = vmem_call(sum_kernel, block, "sum_across")(s10, r4)
    return s00, r5, trade(t10, slow), pass_on(s01, 1)


def middle_kernel(a, b, c, d, out_grad, weight, activations, send, aggregated_out, grad_pre_out):
    total = a[...].astype(jnp.float32)
    for part in (b, c, d):
        total = total + part[...].astype(jnp.float32)
    aggregated = total.astype(jnp.bfloat16)
    at = lax.broadcasted_iota(jnp.int32, (OWN, OWN), 0)
    to = lax.broadcasted_iota(jnp.int32, (OWN, OWN), 1)
    half = SIDE // 2
    turn = jnp.where(
        (at // SIDE == to // SIDE) & (to % SIDE == 2 * (at % half) + (at % SIDE) // half), 1.0, 0.0
    ).astype(jnp.bfloat16)
    w = weight[...]
    pre_act = jnp.dot(aggregated, w, preferred_element_type=jnp.float32)
    sig = jax.nn.sigmoid(pre_act)
    act = (pre_act * sig).astype(jnp.bfloat16)
    activations[...] = over_rows(turn, act).astype(jnp.bfloat16)
    cotangent = jnp.dot(turn, out_grad[...], preferred_element_type=jnp.float32)
    grad_pre = (cotangent * sig * (1.0 + pre_act * (1.0 - sig))).astype(jnp.bfloat16)
    grad_agg = lax.dot_general(
        grad_pre, w, (((1,), (1,)), ((), ())), preferred_element_type=jnp.float32
    ).astype(jnp.bfloat16)
    for k in range(PEERS):
        send[k] = grad_agg
    aggregated_out[...] = aggregated
    grad_pre_out[...] = grad_pre


def wgrad_kernel(aggregated, grad_pre, wgrad_near, wgrad_far, local):
    local[...] = over_rows(aggregated[...], grad_pre[...]).astype(jnp.bfloat16)
    core = lax.axis_index("core")
    for k in range(RING):
        for g in range(RING):
            for out, half_of in ((wgrad_near, core), (wgrad_far, 1 - core)):
                rows, cols = wgrad_place(half_of, k, g)
                out[k * PIECE : (k + 1) * PIECE, g * LANES : (g + 1) * LANES] = local[rows, cols]


def wgrad_place(half_of, k, g):
    row = half_of * (WIDTH // 2) + (lax.axis_index("z") ^ k) * PIECE
    col = ((lax.axis_index("x") + g) & (RING - 1)) * LANES
    return pl.ds(pl.multiple_of(row, PIECE), PIECE), pl.ds(pl.multiple_of(col, LANES), LANES)


def add(a, b):
    return (a.astype(jnp.float32) + b.astype(jnp.float32)).astype(jnp.bfloat16)


def pair_kernel(near, other, *outs):
    for k, out in enumerate(outs):
        rows = slice(k * PIECE, (k + 1) * PIECE)
        out[...] = add(near[rows], other[rows])


def sum_kernel(*refs):
    *parts, out = refs
    total = parts[0][...].astype(jnp.float32)
    for part in parts[1:]:
        total = total + part[...].astype(jnp.float32)
    out[...] = total.astype(out.dtype)


def square_kernel(a, b, c, d, out):
    first = a[...].astype(jnp.float32) + b[...].astype(jnp.float32)
    out[...] = (first + (c[...].astype(jnp.float32) + d[...].astype(jnp.float32))).astype(out.dtype)


def turn_kernel(low, high, *outs):
    rows = low.shape[0]
    for g, out in enumerate(outs):
        for n, part in enumerate((low, high)):
            out[n * rows : (n + 1) * rows] = part[:, g * LANES : (g + 1) * LANES]


def join_kernel(*refs):
    *parts, out = refs
    for g, part in enumerate(parts):
        out[:, g * LANES : (g + 1) * LANES] = part[...]


def place_kernel(mine, theirs, out):
    core = lax.axis_index("core")
    scale = 1.0 / math.sqrt(OWN * PEERS * 2 * PEERS)
    for k in range(RING):
        for g in range(RING):
            for part, half_of in ((mine, core), (theirs, 1 - core)):
                value = part[k * PIECE : (k + 1) * PIECE, g * LANES : (g + 1) * LANES].astype(jnp.float32)
                rows, cols = wgrad_place(half_of, k, g)
                out[rows, cols] = value * jnp.float32(scale)


def exchange(parts, axes):
    return lax.all_to_all(parts, axes, 0, 0)


def trade(array, axes, bits=1):
    return lax.ppermute(array, axes, [(i, i ^ bits) for i in range(lax.axis_size(axes))])


def double_kernel(first, second, out):
    rows = first.shape[0]
    out[:rows] = first[...]
    out[rows:] = second[...]


def gather(block, slow, fast, tasks):
    def ahead(array, step):
        return lax.ppermute(array, fast, [(i, (i - step) % RING) for i in range(RING)])

    across = trade(block, slow)
    before, after = ahead(block, -1), ahead(block, 1)
    across, before, after, state = lax.optimization_barrier((across, before, after, tasks[0](None, None)))
    across_before = trade(before, slow)
    across_after = ahead(across, 1)
    beyond = ahead(before, -1)
    across_before, across_after, beyond, state = lax.optimization_barrier(
        (across_before, across_after, beyond, tasks[1](None, state))
    )
    across_beyond = ahead(across_after, 1)
    blocks = (block, after, before, beyond, across, across_after, across_before)
    return lax.optimization_barrier((across_beyond, tasks[2](blocks, state)))


def scatter_ring(pieces, axis, name):
    arrived = [pieces[0]]
    for k in range(1, RING):
        arrived.append(lax.ppermute(pieces[k], axis, [(i, (i + k) % RING) for i in range(RING)]))
    return vmem_call(sum_kernel, bf16(*pieces[0].shape), name)(*arrived)


def gather_ring(piece, axis):
    pieces = [piece]
    for k in range(1, RING):
        pieces.append(lax.ppermute(piece, axis, [(i, (i - k) % RING) for i in range(RING)]))
    return pieces


def per_device(features, out_grad, weight, block_values, block_coords, block_counts):
    raw = (build_places(block_coords, block_counts), block_counts, block_values)
    tasks = (
        lambda blocks, dense: build(0, *raw),
        lambda blocks, dense: build(1, *raw, dense),
        lambda blocks, dense: (dense, down_most(dense, blocks)),
    )
    block, (dense, most) = gather(features, *ROW, tasks)
    parts = scatter(*down_blocks(dense, most, block), *CHIP)

    half = bf16(WIDTH // 2, WIDTH)
    own = bf16(OWN, WIDTH)
    activations, send, aggregated, grad_pre = vmem_call(
        middle_kernel, (own, bf16(PEERS, OWN, WIDTH), own, own), "middle", flops=2 * 2 * OWN * WIDTH * WIDTH
    )(*parts, out_grad, weight)
    wgrads = vmem_call(
        wgrad_kernel,
        (half, half),
        "wgrad",
        scratch=[pltpu.VMEM((WIDTH, WIDTH), jnp.bfloat16)],
        flops=2 * OWN * WIDTH * WIDTH,
    )(aggregated, grad_pre)

    piece = bf16(PIECE, WIDTH)
    ys = ("y_lo", "y_hi")

    def over_core(terms):
        return vmem_call(pair_kernel, (piece,) * RING, "pair")(terms[0], trade(terms[1], "core"))

    def over_z(pieces):
        arrived = [pieces[0]] + [trade(pieces[k], "z", k) for k in range(1, RING)]
        return vmem_call(sum_kernel, piece, "sum_z")(*arrived)

    def over_y(summed):
        return vmem_call(square_kernel, piece, "sum_y")(
            summed, trade(summed, ys, 1), trade(summed, ys, 2), trade(summed, ys, 3)
        )

    mine = exchange(send, CHIP)
    summed = over_y(over_z(over_core(wgrads)))
    summed, mine = lax.optimization_barrier((summed, mine))

    theirs = trade(mine, "core")
    work = 2 * ROWS * ROWS * WIDTH
    vmem = pl.BlockSpec(memory_space=pltpu.VMEM)
    own, far = pl.pallas_call(
        up_kernel,
        out_shape=(jax.ShapeDtypeStruct((ROWS, WIDTH), jnp.float32), bf16(ROWS, ROWS)),
        in_specs=[pl.BlockSpec(memory_space=pltpu.HBM), vmem],
        out_specs=(vmem, vmem),
        scratch_shapes=[
            pltpu.VMEM((ROWS, ROWS), jnp.bfloat16),
            pltpu.VMEM((ROWS, WIDTH), jnp.bfloat16),
            pltpu.SemaphoreType.DMA((ROWS // STEP + 1,)),
        ],
        compiler_params=pltpu.CompilerParams(vmem_limit_bytes=44 << 20),
        cost_estimate=pl.CostEstimate(flops=work, bytes_accessed=12 << 20, transcendentals=0),
        name="up_near",
    )(dense, mine)
    next_piece, own = lax.optimization_barrier((trade(summed, "z", 1), own))
    pair = vmem_call(double_kernel, bf16(2 * PIECE, WIDTH), "double")(summed, next_piece)
    ordered = pltpu.VMEM((ROWS, WIDTH), jnp.bfloat16)
    partial_grad = vmem_call(
        up_add_kernel, bf16(PEERS, OWN, WIDTH), "up_far", scratch=[ordered], flops=work
    )(far, theirs, own)
    pairs = (pair, trade(pair, "z", 2))
    partial_grad, *pairs = lax.optimization_barrier((partial_grad, *pairs))
    received = exchange(partial_grad, ROW)

    column = bf16(WIDTH // 2, LANES)
    columns = vmem_call(turn_kernel, (column,) * RING, "turn")(*pairs)
    summed = scatter_ring(columns, "x", "sum_x")
    columns = gather_ring(summed, "x")
    own_half = vmem_call(join_kernel, half, "join")(*columns)
    weight_grad = vmem_call(place_kernel, jax.ShapeDtypeStruct((WIDTH, WIDTH), jnp.float32), "place")(
        own_half, trade(own_half, "core")
    )

    total = received[0].astype(jnp.float32)
    for k in range(1, PEERS):
        total = total + received[k].astype(jnp.float32)
    feature_grad = total.astype(jnp.bfloat16)
    return (activations, weight_grad, feature_grad)


def solution(mesh):
    fine = Mesh(mesh.devices.reshape(SIZES), AXES)
    return jax.shard_map(
        per_device,
        mesh=fine,
        in_specs=(
            P(COL + ROW, None),
            P(ROW + COL, None),
            P(),
            P(ROW, COL, None, None),
            P(ROW, COL, None, None),
            P(ROW, COL),
        ),
        out_specs=(P(ROW + COL, None), P(), P(COL + ROW, None)),
        check_vma=False,
    )
```

```python
import functools
import math

import jax
import jax.numpy as jnp
from jax import lax
from jax.experimental import pallas as pl
from jax.experimental.pallas import tpu as pltpu
from jax.sharding import Mesh, PartitionSpec as P

AXES = ("y_lo", "z", "y_hi", "x", "core")
SIZES = (2, 4, 2, 4, 2)
ROW = ("y_lo", "z")
CHIP = ("y_hi", "x")
COL = ("y_hi", "x", "core")
SIDE = 64
PEERS = 8
OWN = 192
WIDTH = 512
ROWS = PEERS * OWN
STEP = 256
RING = 4
PARTS = 2
LAST = 2 * SIDE * 2
PIECE = WIDTH // 2 // RING
LANES = WIDTH // RING


def vmem_call(kernel, outs, name, scratch=(), flops=0, moved=1 << 20, limit=16 << 20, aliases={}):
    vmem = pl.BlockSpec(memory_space=pltpu.VMEM)

    def call(*args):
        return pl.pallas_call(
            kernel,
            out_shape=outs,
            in_specs=[vmem] * len(args),
            out_specs=jax.tree.map(lambda _: vmem, outs),
            scratch_shapes=scratch,
            input_output_aliases=aliases,
            compiler_params=pltpu.CompilerParams(vmem_limit_bytes=limit),
            cost_estimate=pl.CostEstimate(flops=flops, bytes_accessed=moved, transcendentals=0),
            name=name,
        )(*args)

    return call


def bf16(*shape):
    return jax.ShapeDtypeStruct(shape, jnp.bfloat16)


def relative(owner, slow, fast):
    apart = (owner >> 2) ^ lax.axis_index(slow)
    ahead = ((owner & (RING - 1)) - lax.axis_index(fast)) & (RING - 1)
    return apart * RING + (ahead ^ (ahead >> 1))


def absolute(place, slow, fast):
    apart, ahead = divmod(place, RING)
    ahead ^= ahead >> 1
    return (lax.axis_index(slow) ^ apart) * RING + ((lax.axis_index(fast) + ahead) & (RING - 1))


LEAVING = ((0, 2), (1, 2), (1, 3), (1, 1), (0, 3), (1, 0), (0, 1), (0, 0))
FIRST = 3


def leaving_place(chip):
    table = sum(place << 4 * (RING * apart + ahead) for place, (apart, ahead) in enumerate(LEAVING))
    apart = (chip >> 2) ^ lax.axis_index("y_hi")
    ahead = ((chip & (RING - 1)) - lax.axis_index("x")) & (RING - 1)
    return (table >> (4 * (RING * apart + ahead))) & 15


def leaving_chip(place):
    apart, ahead = LEAVING[place]
    return (lax.axis_index("y_hi") ^ apart) * RING + ((lax.axis_index("x") + ahead) & (RING - 1))


def build_places(coords, counts):
    per_owner = OWN // SIDE
    block_row, block_col = coords[0, 0, 0], coords[0, 0, 1]
    live = lax.iota(jnp.int32, block_row.shape[0]) < counts[0, 0]
    owner = block_row // per_owner
    half = (owner + lax.axis_index("core")) & 1
    at_row = (half * PEERS + leaving_place(owner >> 1)) * per_owner + block_row % per_owner
    at_col = relative(block_col // per_owner, *ROW) * per_owner + block_col % per_owner
    return jnp.where(live, at_row + (at_col << 8), 1 << 16)


def build_kernel(part, places, counts, values, *rest):
    dense = rest[-1]
    rows, cols = dense.shape

    if part == 0:

        @pl.loop(0, rows // SIDE)
        def _(r):
            dense[pl.ds(pl.multiple_of(r * SIDE, SIDE), SIDE), :] = jnp.zeros((SIDE, cols), dense.dtype)

    lane = lax.broadcasted_iota(jnp.int32, (SIDE, 2 * SIDE), 1)
    groups = (counts[0, 0] + 15) >> 4

    @pl.loop((groups * part) // PARTS, (groups * (part + 1)) // PARTS)
    def _(g):
        group = values[0, 0, pl.ds(pl.multiple_of(g * 16, 16), 16), :]
        pairs = group.astype(jnp.float32).reshape(16, SIDE // 2, 2 * SIDE)
        for k in range(16):
            slot = g * 16 + k
            code = places[slot]
            at_row, at_col = code & 255, (code >> 8) & 255
            row, col = at_row * SIDE, (at_col >> 1) * 2 * SIDE
            odd = (at_col & 1) == 1
            first = (at_col & 1) * SIDE + (code >> 16) * 4 * SIDE
            plain = pairs[k]
            turned = pltpu.roll(plain, SIDE, 1)
            block = jnp.concatenate(
                [jnp.where(odd, turned, plain), jnp.where(odd, plain, turned)], axis=0
            ).astype(dense.dtype)
            mask = (lane >= first) & (lane < first + SIDE)
            place = dense.at[
                pl.ds(pl.multiple_of(row, SIDE), SIDE), pl.ds(pl.multiple_of(col, 2 * SIDE), 2 * SIDE)
            ]
            place[...] = jnp.where(mask, block, place[...])


def build(part, places, counts, values, *dense):
    vmem = pl.BlockSpec(memory_space=pltpu.VMEM)
    return pl.pallas_call(
        functools.partial(build_kernel, part),
        out_shape=bf16(2 * ROWS, ROWS),
        in_specs=[pl.BlockSpec(memory_space=pltpu.SMEM)] * 2 + [vmem] * (1 + len(dense)),
        out_specs=vmem,
        input_output_aliases={3: 0} if dense else {},
        compiler_params=pltpu.CompilerParams(vmem_limit_bytes=16 << 20),
        cost_estimate=pl.CostEstimate(flops=0, bytes_accessed=8 << 20, transcendentals=0),
        name=f"build_{part}",
    )(places, counts, values, *dense)


def over_rows(a, b):
    return lax.dot_general(a, b, (((0,), (0,)), ((), ())), preferred_element_type=jnp.float32)


def down_kernel(*refs):
    dense, *blocks, out, panel = refs
    for k, block in enumerate(blocks):
        panel[k * OWN : (k + 1) * OWN] = block[...]
    panel[ROWS - OWN :] = jnp.zeros((OWN, WIDTH), panel.dtype)
    for r in range(0, 2 * ROWS, STEP):
        out[r : r + STEP] = jnp.dot(dense[r : r + STEP], panel[...], preferred_element_type=jnp.float32)


def with_last(dense, block, rows):
    padded = jnp.concatenate([jnp.zeros((LAST - OWN, WIDTH), block.dtype), block[...]], axis=0)
    return jnp.dot(dense[rows, ROWS - LAST :], padded, preferred_element_type=jnp.float32)


def down_far_kernel(first, dense, block, most, out):
    for r in range(0, out.shape[0], OWN):
        rows = slice(ROWS + first + r, ROWS + first + r + OWN)
        out[r : r + OWN] = (most[rows] + with_last(dense, block, rows)).astype(out.dtype)


def down_near_kernel(first, dense, block, most, other, *outs):
    for k, out in enumerate(outs):
        rows = slice(first + k * OWN, first + (k + 1) * OWN)
        total = most[rows] + with_last(dense, block, rows)
        out[...] = (total + other[k * OWN : (k + 1) * OWN].astype(jnp.float32)).astype(out.dtype)


def in_order(rows, ordered):
    for place in range(PEERS):
        ordered[place * OWN : (place + 1) * OWN] = rows[leaving_chip(place)]


def up_kernel(dense, rows, out, far, near, ordered, sems):
    strips = [pl.ds(r, STEP) for r in range(0, ROWS, STEP)]
    copies = [
        pltpu.make_async_copy(dense.at[pl.ds(0, ROWS), strip], near.at[:, strip], sems.at[n])
        for n, strip in enumerate(strips)
    ]
    copies.append(pltpu.make_async_copy(dense.at[pl.ds(ROWS, ROWS)], far, sems.at[len(strips)]))
    for copy in copies:
        copy.start()
    in_order(rows, ordered)
    for copy, r in zip(copies, range(0, ROWS, STEP)):
        copy.wait()
        out[r : r + STEP] = over_rows(near[:, r : r + STEP], ordered[...])
    copies[-1].wait()


def up_add_kernel(tile, rows, other, out, ordered, done, sems):
    in_order(rows, ordered)
    copies = []
    for r in range(0, ROWS, 2 * OWN):
        total = over_rows(tile[:, r : r + 2 * OWN], ordered[...]) + other[r : r + 2 * OWN]
        for k in range(2):
            place = r // OWN + k
            done[place] = total[k * OWN : (k + 1) * OWN].astype(done.dtype)
            copies.append(pltpu.make_async_copy(done.at[place], out.at[absolute(place, *ROW)], sems.at[place]))
            copies[-1].start()
    for copy in copies:
        copy.wait()


def down_most(dense, blocks):
    return vmem_call(
        down_kernel,
        jax.ShapeDtypeStruct((2 * ROWS, WIDTH), jnp.float32),
        "down_most",
        scratch=[pltpu.VMEM((ROWS, WIDTH), jnp.bfloat16)],
        flops=4 * ROWS * ROWS * WIDTH,
    )(dense, *blocks)


def down_blocks(dense, most, block):
    runs = ((0, FIRST), (FIRST, PEERS - FIRST))
    others = []
    for n, (first, count) in enumerate(runs):
        kernel = functools.partial(down_far_kernel, first * OWN)
        far = vmem_call(kernel, bf16(count * OWN, WIDTH), f"down_far_{n}", flops=2 * count * OWN * LAST * WIDTH)(
            dense, block, most
        )
        other = trade(far, "core")
        if n == 0:
            other, most = lax.optimization_barrier((other, most))
        others.append(other)

    def near(n):
        first, count = runs[n]
        kernel = functools.partial(down_near_kernel, first * OWN)
        return vmem_call(
            kernel, (bf16(OWN, WIDTH),) * count, f"down_near_{n}", flops=2 * count * OWN * LAST * WIDTH
        )(dense, block, most, others[n])

    return near(0), lambda: near(1)


def meet_kernel(a, b, c, d, e, out_ab, out_cde):
    out_ab[...] = add(a[...], b[...])
    total = c[...].astype(jnp.float32) + d[...].astype(jnp.float32) + e[...].astype(jnp.float32)
    out_cde[...] = total.astype(out_cde.dtype)


def scatter(first, rest, slow, fast):
    def pass_on(array, step):
        return lax.ppermute(array, fast, [(i, (i + step) % RING) for i in range(RING)])

    s02, s12, s13 = first
    r1, r2, r3 = pass_on(s12, 1), trade(s13, slow), pass_on(s02, -1)
    r1, r2, r3, rest = lax.optimization_barrier((r1, r2, r3, rest()))
    s11, s03, s10, s01, s00 = rest
    block = bf16(OWN, WIDTH)
    t11, t03 = vmem_call(meet_kernel, (block, block), "meet")(s11, r1, s03, r2, r3)
    r4, r5 = lax.optimization_barrier((pass_on(t11, 1), pass_on(t03, -1)))
    t10 = vmem_call(sum_kernel, block, "sum_across")(s10, r4)
    return s00, r5, trade(t10, slow), pass_on(s01, 1)


def middle_kernel(a, b, c, d, out_grad, weight, activations, send, aggregated_out, grad_pre_out):
    total = a[...].astype(jnp.float32)
    for part in (b, c, d):
        total = total + part[...].astype(jnp.float32)
    aggregated = total.astype(jnp.bfloat16)
    at = lax.broadcasted_iota(jnp.int32, (OWN, OWN), 0)
    to = lax.broadcasted_iota(jnp.int32, (OWN, OWN), 1)
    half = SIDE // 2
    turn = jnp.where(
        (at // SIDE == to // SIDE) & (to % SIDE == 2 * (at % half) + (at % SIDE) // half), 1.0, 0.0
    ).astype(jnp.bfloat16)
    w = weight[...]
    pre_act = jnp.dot(aggregated, w, preferred_element_type=jnp.float32)
    sig = jax.nn.sigmoid(pre_act)
    act = (pre_act * sig).astype(jnp.bfloat16)
    activations[...] = over_rows(turn, act).astype(jnp.bfloat16)
    cotangent = jnp.dot(turn, out_grad[...], preferred_element_type=jnp.float32)
    grad_pre = (cotangent * sig * (1.0 + pre_act * (1.0 - sig))).astype(jnp.bfloat16)
    grad_agg = lax.dot_general(
        grad_pre, w, (((1,), (1,)), ((), ())), preferred_element_type=jnp.float32
    ).astype(jnp.bfloat16)
    for k in range(PEERS):
        send[k] = grad_agg
    aggregated_out[...] = aggregated
    grad_pre_out[...] = grad_pre


def wgrad_kernel(aggregated, grad_pre, wgrad_near, wgrad_far, local):
    local[...] = over_rows(aggregated[...], grad_pre[...]).astype(jnp.bfloat16)
    core = lax.axis_index("core")
    for k in range(RING):
        for g in range(RING):
            for out, half_of in ((wgrad_near, core), (wgrad_far, 1 - core)):
                rows, cols = wgrad_place(half_of, k, g)
                out[k * PIECE : (k + 1) * PIECE, g * LANES : (g + 1) * LANES] = local[rows, cols]


def wgrad_place(half_of, k, g):
    row = half_of * (WIDTH // 2) + (lax.axis_index("z") ^ k) * PIECE
    col = ((lax.axis_index("x") + g) & (RING - 1)) * LANES
    return pl.ds(pl.multiple_of(row, PIECE), PIECE), pl.ds(pl.multiple_of(col, LANES), LANES)


def add(a, b):
    return (a.astype(jnp.float32) + b.astype(jnp.float32)).astype(jnp.bfloat16)


def pair_kernel(near, other, *outs):
    for k, out in enumerate(outs):
        rows = slice(k * PIECE, (k + 1) * PIECE)
        out[...] = add(near[rows], other[rows])


def sum_kernel(*refs):
    *parts, out = refs
    total = parts[0][...].astype(jnp.float32)
    for part in parts[1:]:
        total = total + part[...].astype(jnp.float32)
    out[...] = total.astype(out.dtype)


def total_kernel(parts, out):
    total = parts[0].astype(jnp.float32)
    for k in range(1, PEERS):
        total = total + parts[k].astype(jnp.float32)
    out[...] = total.astype(out.dtype)


def square_kernel(a, b, c, d, out):
    first = a[...].astype(jnp.float32) + b[...].astype(jnp.float32)
    out[...] = (first + (c[...].astype(jnp.float32) + d[...].astype(jnp.float32))).astype(out.dtype)


def turn_kernel(low, high, *outs):
    rows = low.shape[0]
    for g, out in enumerate(outs):
        for n, part in enumerate((low, high)):
            out[n * rows : (n + 1) * rows] = part[:, g * LANES : (g + 1) * LANES]


def join_kernel(*refs):
    *parts, out = refs
    for g, part in enumerate(parts):
        out[:, g * LANES : (g + 1) * LANES] = part[...]


def place_kernel(mine, theirs, out):
    core = lax.axis_index("core")
    scale = 1.0 / math.sqrt(OWN * PEERS * 2 * PEERS)
    for k in range(RING):
        for g in range(RING):
            for part, half_of in ((mine, core), (theirs, 1 - core)):
                value = part[k * PIECE : (k + 1) * PIECE, g * LANES : (g + 1) * LANES].astype(jnp.float32)
                rows, cols = wgrad_place(half_of, k, g)
                out[rows, cols] = value * jnp.float32(scale)


def exchange(parts, axes):
    return lax.all_to_all(parts, axes, 0, 0)


def trade(array, axes, bits=1):
    return lax.ppermute(array, axes, [(i, i ^ bits) for i in range(lax.axis_size(axes))])


def double_kernel(first, second, out):
    rows = first.shape[0]
    out[:rows] = first[...]
    out[rows:] = second[...]


def gather(block, slow, fast, tasks):
    def ahead(array, step):
        return lax.ppermute(array, fast, [(i, (i - step) % RING) for i in range(RING)])

    across = trade(block, slow)
    before, after = ahead(block, -1), ahead(block, 1)
    across, before, after, state = lax.optimization_barrier((across, before, after, tasks[0](None, None)))
    across_before = trade(before, slow)
    across_after = ahead(across, 1)
    beyond = ahead(before, -1)
    across_before, across_after, beyond, state = lax.optimization_barrier(
        (across_before, across_after, beyond, tasks[1](None, state))
    )
    across_beyond = ahead(across_after, 1)
    blocks = (block, after, before, beyond, across, across_after, across_before)
    return lax.optimization_barrier((across_beyond, tasks[2](blocks, state)))


def scatter_ring(pieces, axis, name):
    arrived = [pieces[0]]
    for k in range(1, RING):
        arrived.append(lax.ppermute(pieces[k], axis, [(i, (i + k) % RING) for i in range(RING)]))
    return vmem_call(sum_kernel, bf16(*pieces[0].shape), name)(*arrived)


def gather_ring(piece, axis):
    pieces = [piece]
    for k in range(1, RING):
        pieces.append(lax.ppermute(piece, axis, [(i, (i - k) % RING) for i in range(RING)]))
    return pieces


def per_device(features, out_grad, weight, block_values, block_coords, block_counts):
    raw = (build_places(block_coords, block_counts), block_counts, block_values)
    tasks = (
        lambda blocks, dense: build(0, *raw),
        lambda blocks, dense: build(1, *raw, dense),
        lambda blocks, dense: (dense, down_most(dense, blocks)),
    )
    block, (dense, most) = gather(features, *ROW, tasks)
    parts = scatter(*down_blocks(dense, most, block), *CHIP)

    half = bf16(WIDTH // 2, WIDTH)
    own = bf16(OWN, WIDTH)
    activations, send, aggregated, grad_pre = vmem_call(
        middle_kernel, (own, bf16(PEERS, OWN, WIDTH), own, own), "middle", flops=2 * 2 * OWN * WIDTH * WIDTH
    )(*parts, out_grad, weight)
    wgrads = vmem_call(
        wgrad_kernel,
        (half, half),
        "wgrad",
        scratch=[pltpu.VMEM((WIDTH, WIDTH), jnp.bfloat16)],
        flops=2 * OWN * WIDTH * WIDTH,
    )(aggregated, grad_pre)

    piece = bf16(PIECE, WIDTH)
    ys = ("y_lo", "y_hi")

    def over_core(terms):
        return vmem_call(pair_kernel, (piece,) * RING, "pair")(terms[0], trade(terms[1], "core"))

    def over_z(pieces):
        arrived = [pieces[0]] + [trade(pieces[k], "z", k) for k in range(1, RING)]
        return vmem_call(sum_kernel, piece, "sum_z")(*arrived)

    def over_y(summed):
        return vmem_call(square_kernel, piece, "sum_y")(
            summed, trade(summed, ys, 1), trade(summed, ys, 2), trade(summed, ys, 3)
        )

    mine = exchange(send, CHIP)
    summed = over_y(over_z(over_core(wgrads)))
    summed, mine = lax.optimization_barrier((summed, mine))

    theirs = trade(mine, "core")
    work = 2 * ROWS * ROWS * WIDTH
    vmem = pl.BlockSpec(memory_space=pltpu.VMEM)
    own, far = pl.pallas_call(
        up_kernel,
        out_shape=(jax.ShapeDtypeStruct((ROWS, WIDTH), jnp.float32), bf16(ROWS, ROWS)),
        in_specs=[pl.BlockSpec(memory_space=pltpu.HBM), vmem],
        out_specs=(vmem, vmem),
        scratch_shapes=[
            pltpu.VMEM((ROWS, ROWS), jnp.bfloat16),
            pltpu.VMEM((ROWS, WIDTH), jnp.bfloat16),
            pltpu.SemaphoreType.DMA((ROWS // STEP + 1,)),
        ],
        compiler_params=pltpu.CompilerParams(vmem_limit_bytes=44 << 20),
        cost_estimate=pl.CostEstimate(flops=work, bytes_accessed=12 << 20, transcendentals=0),
        name="up_near",
    )(dense, mine)
    next_piece, own = lax.optimization_barrier((trade(summed, "z", 1), own))
    pair = vmem_call(double_kernel, bf16(2 * PIECE, WIDTH), "double")(summed, next_piece)
    partial_grad = pl.pallas_call(
        up_add_kernel,
        out_shape=bf16(PEERS, OWN, WIDTH),
        in_specs=[vmem] * 3,
        out_specs=pl.BlockSpec(memory_space=pltpu.HBM),
        scratch_shapes=[
            pltpu.VMEM((ROWS, WIDTH), jnp.bfloat16),
            pltpu.VMEM((PEERS, OWN, WIDTH), jnp.bfloat16),
            pltpu.SemaphoreType.DMA((PEERS,)),
        ],
        compiler_params=pltpu.CompilerParams(vmem_limit_bytes=16 << 20),
        cost_estimate=pl.CostEstimate(flops=work, bytes_accessed=12 << 20, transcendentals=0),
        name="up_far",
    )(far, theirs, own)
    pairs = (pair, trade(pair, "z", 2))
    partial_grad, *pairs = lax.optimization_barrier((partial_grad, *pairs))
    received = exchange(partial_grad, ROW)

    column = bf16(WIDTH // 2, LANES)
    columns = vmem_call(turn_kernel, (column,) * RING, "turn")(*pairs)
    summed = scatter_ring(columns, "x", "sum_x")
    columns = gather_ring(summed, "x")
    own_half = vmem_call(join_kernel, half, "join")(*columns)
    weight_grad = vmem_call(place_kernel, jax.ShapeDtypeStruct((WIDTH, WIDTH), jnp.float32), "place")(
        own_half, trade(own_half, "core")
    )

    feature_grad = vmem_call(total_kernel, bf16(OWN, WIDTH), "total")(received)
    return (activations, weight_grad, feature_grad)


def solution(mesh):
    fine = Mesh(mesh.devices.reshape(SIZES), AXES)
    return jax.shard_map(
        per_device,
        mesh=fine,
        in_specs=(
            P(COL + ROW, None),
            P(ROW + COL, None),
            P(),
            P(ROW, COL, None, None),
            P(ROW, COL, None, None),
            P(ROW, COL),
        ),
        out_specs=(P(ROW + COL, None), P(), P(COL + ROW, None)),
        check_vma=False,
    )
```

```python
import functools
import math

import jax
import jax.numpy as jnp
from jax import lax
from jax.experimental import pallas as pl
from jax.experimental.pallas import tpu as pltpu
from jax.sharding import Mesh, PartitionSpec as P

AXES = ("y_lo", "z", "y_hi", "x", "core")
SIZES = (2, 4, 2, 4, 2)
ROW = ("y_lo", "z")
CHIP = ("y_hi", "x")
COL = ("y_hi", "x", "core")
SIDE = 64
PEERS = 8
OWN = 192
WIDTH = 512
ROWS = PEERS * OWN
STEP = 256
RING = 4
PARTS = 2
LAST = 2 * SIDE * 2
PIECE = WIDTH // 2 // RING
LANES = WIDTH // RING


def vmem_call(kernel, outs, name, scratch=(), flops=0, moved=1 << 20, limit=16 << 20, aliases={}):
    vmem = pl.BlockSpec(memory_space=pltpu.VMEM)

    def call(*args):
        return pl.pallas_call(
            kernel,
            out_shape=outs,
            in_specs=[vmem] * len(args),
            out_specs=jax.tree.map(lambda _: vmem, outs),
            scratch_shapes=scratch,
            input_output_aliases=aliases,
            compiler_params=pltpu.CompilerParams(vmem_limit_bytes=limit),
            cost_estimate=pl.CostEstimate(flops=flops, bytes_accessed=moved, transcendentals=0),
            name=name,
        )(*args)

    return call


def bf16(*shape):
    return jax.ShapeDtypeStruct(shape, jnp.bfloat16)


def relative(owner, slow, fast):
    apart = (owner >> 2) ^ lax.axis_index(slow)
    ahead = ((owner & (RING - 1)) - lax.axis_index(fast)) & (RING - 1)
    return apart * RING + (ahead ^ (ahead >> 1))


def absolute(place, slow, fast):
    apart, ahead = divmod(place, RING)
    ahead ^= ahead >> 1
    return (lax.axis_index(slow) ^ apart) * RING + ((lax.axis_index(fast) + ahead) & (RING - 1))


LEAVING = ((0, 2), (1, 2), (1, 3), (1, 1), (0, 3), (1, 0), (0, 1), (0, 0))
FIRST = 3


def leaving_place(chip):
    table = sum(place << 4 * (RING * apart + ahead) for place, (apart, ahead) in enumerate(LEAVING))
    apart = (chip >> 2) ^ lax.axis_index("y_hi")
    ahead = ((chip & (RING - 1)) - lax.axis_index("x")) & (RING - 1)
    return (table >> (4 * (RING * apart + ahead))) & 15


def build_places(coords, counts):
    per_owner = OWN // SIDE
    block_row, block_col = coords[0, 0, 0], coords[0, 0, 1]
    live = lax.iota(jnp.int32, block_row.shape[0]) < counts[0, 0]
    owner = block_row // per_owner
    half = (owner + lax.axis_index("core")) & 1
    at_row = (half * PEERS + leaving_place(owner >> 1)) * per_owner + block_row % per_owner
    at_col = relative(block_col // per_owner, *ROW) * per_owner + block_col % per_owner
    return jnp.where(live, at_row + (at_col << 8), 1 << 16)


def build_kernel(part, places, counts, values, *rest):
    dense = rest[-1]
    rows, cols = dense.shape

    if part == 0:

        @pl.loop(0, rows // SIDE)
        def _(r):
            dense[pl.ds(pl.multiple_of(r * SIDE, SIDE), SIDE), :] = jnp.zeros((SIDE, cols), dense.dtype)

    lane = lax.broadcasted_iota(jnp.int32, (SIDE, 2 * SIDE), 1)
    groups = (counts[0, 0] + 15) >> 4

    @pl.loop((groups * part) // PARTS, (groups * (part + 1)) // PARTS)
    def _(g):
        group = values[0, 0, pl.ds(pl.multiple_of(g * 16, 16), 16), :]
        pairs = group.astype(jnp.float32).reshape(16, SIDE // 2, 2 * SIDE)
        for k in range(16):
            slot = g * 16 + k
            code = places[slot]
            at_row, at_col = code & 255, (code >> 8) & 255
            row, col = at_row * SIDE, (at_col >> 1) * 2 * SIDE
            odd = (at_col & 1) == 1
            first = (at_col & 1) * SIDE + (code >> 16) * 4 * SIDE
            plain = pairs[k]
            turned = pltpu.roll(plain, SIDE, 1)
            block = jnp.concatenate(
                [jnp.where(odd, turned, plain), jnp.where(odd, plain, turned)], axis=0
            ).astype(dense.dtype)
            mask = (lane >= first) & (lane < first + SIDE)
            place = dense.at[
                pl.ds(pl.multiple_of(row, SIDE), SIDE), pl.ds(pl.multiple_of(col, 2 * SIDE), 2 * SIDE)
            ]
            place[...] = jnp.where(mask, block, place[...])


def build(part, places, counts, values, *dense):
    vmem = pl.BlockSpec(memory_space=pltpu.VMEM)
    return pl.pallas_call(
        functools.partial(build_kernel, part),
        out_shape=bf16(2 * ROWS, ROWS),
        in_specs=[pl.BlockSpec(memory_space=pltpu.SMEM)] * 2 + [vmem] * (1 + len(dense)),
        out_specs=vmem,
        input_output_aliases={3: 0} if dense else {},
        compiler_params=pltpu.CompilerParams(vmem_limit_bytes=16 << 20),
        cost_estimate=pl.CostEstimate(flops=0, bytes_accessed=8 << 20, transcendentals=0),
        name=f"build_{part}",
    )(places, counts, values, *dense)


def over_rows(a, b):
    return lax.dot_general(a, b, (((0,), (0,)), ((), ())), preferred_element_type=jnp.float32)


def down_kernel(*refs):
    dense, *blocks, out, panel = refs
    for k, block in enumerate(blocks):
        panel[k * OWN : (k + 1) * OWN] = block[...]
    panel[ROWS - OWN :] = jnp.zeros((OWN, WIDTH), panel.dtype)
    for r in range(0, 2 * ROWS, STEP):
        out[r : r + STEP] = jnp.dot(dense[r : r + STEP], panel[...], preferred_element_type=jnp.float32)


def with_last(dense, block, rows):
    padded = jnp.concatenate([jnp.zeros((LAST - OWN, WIDTH), block.dtype), block[...]], axis=0)
    return jnp.dot(dense[rows, ROWS - LAST :], padded, preferred_element_type=jnp.float32)


def down_far_kernel(first, dense, block, most, out):
    for r in range(0, out.shape[0], OWN):
        rows = slice(ROWS + first + r, ROWS + first + r + OWN)
        out[r : r + OWN] = (most[rows] + with_last(dense, block, rows)).astype(out.dtype)


def down_near_kernel(first, dense, block, most, other, *outs):
    for k, out in enumerate(outs):
        rows = slice(first + k * OWN, first + (k + 1) * OWN)
        total = most[rows] + with_last(dense, block, rows)
        out[...] = (total + other[k * OWN : (k + 1) * OWN].astype(jnp.float32)).astype(out.dtype)


def order_kernel(*refs):
    *pairs, out = refs
    for place, (apart, ahead) in enumerate(LEAVING):
        out[place * OWN : (place + 1) * OWN] = pairs[ahead][apart * OWN : (apart + 1) * OWN]


def up_kernel(dense, rows, out):
    for r in range(0, ROWS, STEP):
        out[r : r + STEP] = over_rows(dense[:ROWS, r : r + STEP], rows[...])


def up_add_kernel(dense, rows, other, out, done, sems):
    copies = []
    for r in range(0, ROWS, 2 * OWN):
        total = over_rows(dense[ROWS:, r : r + 2 * OWN], rows[...]) + other[r : r + 2 * OWN]
        for k in range(2):
            place = r // OWN + k
            done[place] = total[k * OWN : (k + 1) * OWN].astype(done.dtype)
            copies.append(pltpu.make_async_copy(done.at[place], out.at[absolute(place, *ROW)], sems.at[place]))
            copies[-1].start()
    for copy in copies:
        copy.wait()


def down_most(dense, blocks):
    return vmem_call(
        down_kernel,
        jax.ShapeDtypeStruct((2 * ROWS, WIDTH), jnp.float32),
        "down_most",
        scratch=[pltpu.VMEM((ROWS, WIDTH), jnp.bfloat16)],
        flops=4 * ROWS * ROWS * WIDTH,
    )(dense, *blocks)


def down_blocks(dense, most, block):
    runs = ((0, FIRST), (FIRST, PEERS - FIRST))
    others = []
    for n, (first, count) in enumerate(runs):
        kernel = functools.partial(down_far_kernel, first * OWN)
        far = vmem_call(kernel, bf16(count * OWN, WIDTH), f"down_far_{n}", flops=2 * count * OWN * LAST * WIDTH)(
            dense, block, most
        )
        other = trade(far, "core")
        if n == 0:
            other, most = lax.optimization_barrier((other, most))
        others.append(other)

    def near(n):
        first, count = runs[n]
        kernel = functools.partial(down_near_kernel, first * OWN)
        return vmem_call(
            kernel, (bf16(OWN, WIDTH),) * count, f"down_near_{n}", flops=2 * count * OWN * LAST * WIDTH
        )(dense, block, most, others[n])

    return near(0), lambda: near(1)


def meet_kernel(a, b, c, d, e, out_ab, out_cde):
    out_ab[...] = add(a[...], b[...])
    total = c[...].astype(jnp.float32) + d[...].astype(jnp.float32) + e[...].astype(jnp.float32)
    out_cde[...] = total.astype(out_cde.dtype)


def scatter(first, rest, slow, fast):
    def pass_on(array, step):
        return lax.ppermute(array, fast, [(i, (i + step) % RING) for i in range(RING)])

    s02, s12, s13 = first
    r1, r2, r3 = pass_on(s12, 1), trade(s13, slow), pass_on(s02, -1)
    r1, r2, r3, rest = lax.optimization_barrier((r1, r2, r3, rest()))
    s11, s03, s10, s01, s00 = rest
    block = bf16(OWN, WIDTH)
    t11, t03 = vmem_call(meet_kernel, (block, block), "meet")(s11, r1, s03, r2, r3)
    r4, r5 = lax.optimization_barrier((pass_on(t11, 1), pass_on(t03, -1)))
    t10 = vmem_call(sum_kernel, block, "sum_across")(s10, r4)
    return s00, r5, trade(t10, slow), pass_on(s01, 1)


def middle_kernel(a, b, c, d, out_grad, weight, activations, send, aggregated_out, grad_pre_out):
    total = a[...].astype(jnp.float32)
    for part in (b, c, d):
        total = total + part[...].astype(jnp.float32)
    aggregated = total.astype(jnp.bfloat16)
    at = lax.broadcasted_iota(jnp.int32, (OWN, OWN), 0)
    to = lax.broadcasted_iota(jnp.int32, (OWN, OWN), 1)
    half = SIDE // 2
    turn = jnp.where(
        (at // SIDE == to // SIDE) & (to % SIDE == 2 * (at % half) + (at % SIDE) // half), 1.0, 0.0
    ).astype(jnp.bfloat16)
    w = weight[...]
    pre_act = jnp.dot(aggregated, w, preferred_element_type=jnp.float32)
    sig = jax.nn.sigmoid(pre_act)
    act = (pre_act * sig).astype(jnp.bfloat16)
    activations[...] = over_rows(turn, act).astype(jnp.bfloat16)
    cotangent = jnp.dot(turn, out_grad[...], preferred_element_type=jnp.float32)
    grad_pre = (cotangent * sig * (1.0 + pre_act * (1.0 - sig))).astype(jnp.bfloat16)
    grad_agg = lax.dot_general(
        grad_pre, w, (((1,), (1,)), ((), ())), preferred_element_type=jnp.float32
    ).astype(jnp.bfloat16)
    send[...] = grad_agg
    aggregated_out[...] = aggregated
    grad_pre_out[...] = grad_pre


def wgrad_kernel(aggregated, grad_pre, wgrad_near, wgrad_far, local):
    local[...] = over_rows(aggregated[...], grad_pre[...]).astype(jnp.bfloat16)
    core = lax.axis_index("core")
    for k in range(RING):
        for g in range(RING):
            for out, half_of in ((wgrad_near, core), (wgrad_far, 1 - core)):
                rows, cols = wgrad_place(half_of, k, g)
                out[k * PIECE : (k + 1) * PIECE, g * LANES : (g + 1) * LANES] = local[rows, cols]


def wgrad_place(half_of, k, g):
    row = half_of * (WIDTH // 2) + (lax.axis_index("z") ^ k) * PIECE
    col = ((lax.axis_index("x") + g) & (RING - 1)) * LANES
    return pl.ds(pl.multiple_of(row, PIECE), PIECE), pl.ds(pl.multiple_of(col, LANES), LANES)


def add(a, b):
    return (a.astype(jnp.float32) + b.astype(jnp.float32)).astype(jnp.bfloat16)


def pair_kernel(near, other, *outs):
    for k, out in enumerate(outs):
        rows = slice(k * PIECE, (k + 1) * PIECE)
        out[...] = add(near[rows], other[rows])


def sum_kernel(*refs):
    *parts, out = refs
    total = parts[0][...].astype(jnp.float32)
    for part in parts[1:]:
        total = total + part[...].astype(jnp.float32)
    out[...] = total.astype(out.dtype)


def total_kernel(parts, out):
    total = parts[0].astype(jnp.float32)
    for k in range(1, PEERS):
        total = total + parts[k].astype(jnp.float32)
    out[...] = total.astype(out.dtype)


def square_kernel(a, b, c, d, out):
    first = a[...].astype(jnp.float32) + b[...].astype(jnp.float32)
    out[...] = (first + (c[...].astype(jnp.float32) + d[...].astype(jnp.float32))).astype(out.dtype)


def turn_kernel(low, high, *outs):
    rows = low.shape[0]
    for g, out in enumerate(outs):
        for n, part in enumerate((low, high)):
            out[n * rows : (n + 1) * rows] = part[:, g * LANES : (g + 1) * LANES]


def join_kernel(*refs):
    *parts, out = refs
    for g, part in enumerate(parts):
        out[:, g * LANES : (g + 1) * LANES] = part[...]


def place_kernel(mine, theirs, out):
    core = lax.axis_index("core")
    scale = 1.0 / math.sqrt(OWN * PEERS * 2 * PEERS)
    for k in range(RING):
        for g in range(RING):
            for part, half_of in ((mine, core), (theirs, 1 - core)):
                value = part[k * PIECE : (k + 1) * PIECE, g * LANES : (g + 1) * LANES].astype(jnp.float32)
                rows, cols = wgrad_place(half_of, k, g)
                out[rows, cols] = value * jnp.float32(scale)


def exchange(parts, axes):
    return lax.all_to_all(parts, axes, 0, 0)


def trade(array, axes, bits=1):
    return lax.ppermute(array, axes, [(i, i ^ bits) for i in range(lax.axis_size(axes))])


def double_kernel(first, second, out):
    rows = first.shape[0]
    out[:rows] = first[...]
    out[rows:] = second[...]


def gather(block, slow, fast, tasks):
    def ahead(array, step):
        return lax.ppermute(array, fast, [(i, (i - step) % RING) for i in range(RING)])

    across = trade(block, slow)
    before, after = ahead(block, -1), ahead(block, 1)
    across, before, after, state = lax.optimization_barrier((across, before, after, tasks[0](None, None)))
    across_before = trade(before, slow)
    across_after = ahead(across, 1)
    beyond = ahead(before, -1)
    across_before, across_after, beyond, state = lax.optimization_barrier(
        (across_before, across_after, beyond, tasks[1](None, state))
    )
    across_beyond = ahead(across_after, 1)
    blocks = (block, after, before, beyond, across, across_after, across_before)
    return lax.optimization_barrier((across_beyond, tasks[2](blocks, state)))


def scatter_ring(pieces, axis, name):
    arrived = [pieces[0]]
    for k in range(1, RING):
        arrived.append(lax.ppermute(pieces[k], axis, [(i, (i + k) % RING) for i in range(RING)]))
    return vmem_call(sum_kernel, bf16(*pieces[0].shape), name)(*arrived)


def gather_ring(piece, axis):
    pieces = [piece]
    for k in range(1, RING):
        pieces.append(lax.ppermute(piece, axis, [(i, (i - k) % RING) for i in range(RING)]))
    return pieces


def per_device(features, out_grad, weight, block_values, block_coords, block_counts):
    raw = (build_places(block_coords, block_counts), block_counts, block_values)
    tasks = (
        lambda blocks, dense: build(0, *raw),
        lambda blocks, dense: build(1, *raw, dense),
        lambda blocks, dense: (dense, down_most(dense, blocks)),
    )
    block, (dense, most) = gather(features, *ROW, tasks)
    parts = scatter(*down_blocks(dense, most, block), *CHIP)

    half = bf16(WIDTH // 2, WIDTH)
    own = bf16(OWN, WIDTH)
    activations, send, aggregated, grad_pre = vmem_call(
        middle_kernel, (own, own, own, own), "middle", flops=2 * 2 * OWN * WIDTH * WIDTH
    )(*parts, out_grad, weight)
    wgrads = vmem_call(
        wgrad_kernel,
        (half, half),
        "wgrad",
        scratch=[pltpu.VMEM((WIDTH, WIDTH), jnp.bfloat16)],
        flops=2 * OWN * WIDTH * WIDTH,
    )(aggregated, grad_pre)

    piece = bf16(PIECE, WIDTH)
    ys = ("y_lo", "y_hi")

    def over_core(terms):
        return vmem_call(pair_kernel, (piece,) * RING, "pair")(terms[0], trade(terms[1], "core"))

    def over_z(pieces):
        arrived = [pieces[0]] + [trade(pieces[k], "z", k) for k in range(1, RING)]
        return vmem_call(sum_kernel, piece, "sum_z")(*arrived)

    def over_y(summed):
        return vmem_call(square_kernel, piece, "sum_y")(
            summed, trade(summed, ys, 1), trade(summed, ys, 2), trade(summed, ys, 3)
        )

    pair = vmem_call(double_kernel, bf16(2 * OWN, WIDTH), "pair_y")(send, trade(send, "y_hi"))
    wgrads, pair = lax.optimization_barrier((wgrads, pair))
    mine = [pair] + [lax.ppermute(pair, "x", [(i, (i - k) % RING) for i in range(RING)]) for k in range(1, RING)]
    summed = over_y(over_z(over_core(wgrads)))
    low = vmem_call(double_kernel, bf16(2 * PIECE, WIDTH), "double")(summed, trade(summed, "z", 1))
    mine, *pairs = lax.optimization_barrier((mine, low, trade(low, "z", 2)))
    mine = vmem_call(order_kernel, bf16(ROWS, WIDTH), "order")(*mine)

    theirs = trade(mine, "core")
    work = 2 * ROWS * ROWS * WIDTH
    vmem = pl.BlockSpec(memory_space=pltpu.VMEM)
    own = vmem_call(up_kernel, jax.ShapeDtypeStruct((ROWS, WIDTH), jnp.float32), "up_near", flops=work)(dense, mine)
    partial_grad = pl.pallas_call(
        up_add_kernel,
        out_shape=bf16(PEERS, OWN, WIDTH),
        in_specs=[vmem] * 3,
        out_specs=pl.BlockSpec(memory_space=pltpu.HBM),
        scratch_shapes=[pltpu.VMEM((PEERS, OWN, WIDTH), jnp.bfloat16), pltpu.SemaphoreType.DMA((PEERS,))],
        compiler_params=pltpu.CompilerParams(vmem_limit_bytes=16 << 20),
        cost_estimate=pl.CostEstimate(flops=work, bytes_accessed=12 << 20, transcendentals=0),
        name="up_far",
    )(dense, theirs, own)
    received = exchange(partial_grad, ROW)

    column = bf16(WIDTH // 2, LANES)
    columns = vmem_call(turn_kernel, (column,) * RING, "turn")(*pairs)
    summed = scatter_ring(columns, "x", "sum_x")
    columns = gather_ring(summed, "x")
    own_half = vmem_call(join_kernel, half, "join")(*columns)
    weight_grad = vmem_call(place_kernel, jax.ShapeDtypeStruct((WIDTH, WIDTH), jnp.float32), "place")(
        own_half, trade(own_half, "core")
    )

    feature_grad = vmem_call(total_kernel, bf16(OWN, WIDTH), "total")(received)
    return (activations, weight_grad, feature_grad)


def solution(mesh):
    fine = Mesh(mesh.devices.reshape(SIZES), AXES)
    return jax.shard_map(
        per_device,
        mesh=fine,
        in_specs=(
            P(COL + ROW, None),
            P(ROW + COL, None),
            P(),
            P(ROW, COL, None, None),
            P(ROW, COL, None, None),
            P(ROW, COL),
        ),
        out_specs=(P(ROW + COL, None), P(), P(COL + ROW, None)),
        check_vma=False,
    )
```

```python
import functools
import math

import jax
import jax.numpy as jnp
from jax import lax
from jax.experimental import pallas as pl
from jax.experimental.pallas import tpu as pltpu
from jax.sharding import Mesh, PartitionSpec as P

AXES = ("y_lo", "z", "y_hi", "x", "core")
SIZES = (2, 4, 2, 4, 2)
ROW = ("y_lo", "z")
CHIP = ("y_hi", "x")
COL = ("y_hi", "x", "core")
SIDE = 64
PEERS = 8
OWN = 192
WIDTH = 512
ROWS = PEERS * OWN
STEP = 256
RING = 4
PARTS = 2
LAST = 2 * SIDE * 2
PIECE = WIDTH // 2 // RING
LANES = WIDTH // RING


def vmem_call(kernel, outs, name, scratch=(), flops=0, moved=1 << 20, limit=16 << 20, aliases={}):
    vmem = pl.BlockSpec(memory_space=pltpu.VMEM)

    def call(*args):
        return pl.pallas_call(
            kernel,
            out_shape=outs,
            in_specs=[vmem] * len(args),
            out_specs=jax.tree.map(lambda _: vmem, outs),
            scratch_shapes=scratch,
            input_output_aliases=aliases,
            compiler_params=pltpu.CompilerParams(vmem_limit_bytes=limit),
            cost_estimate=pl.CostEstimate(flops=flops, bytes_accessed=moved, transcendentals=0),
            name=name,
        )(*args)

    return call


def bf16(*shape):
    return jax.ShapeDtypeStruct(shape, jnp.bfloat16)


def relative(owner, slow, fast):
    apart = (owner >> 2) ^ lax.axis_index(slow)
    ahead = ((owner & (RING - 1)) - lax.axis_index(fast)) & (RING - 1)
    return apart * RING + (ahead ^ (ahead >> 1))


def absolute(place, slow, fast):
    apart, ahead = divmod(place, RING)
    ahead ^= ahead >> 1
    return (lax.axis_index(slow) ^ apart) * RING + ((lax.axis_index(fast) + ahead) & (RING - 1))


LEAVING = ((0, 2), (1, 2), (1, 3), (1, 1), (0, 3), (1, 0), (0, 1), (0, 0))
FIRST = 3


def leaving_place(chip):
    table = sum(place << 4 * (RING * apart + ahead) for place, (apart, ahead) in enumerate(LEAVING))
    apart = (chip >> 2) ^ lax.axis_index("y_hi")
    ahead = ((chip & (RING - 1)) - lax.axis_index("x")) & (RING - 1)
    return (table >> (4 * (RING * apart + ahead))) & 15


def build_places(coords, counts):
    per_owner = OWN // SIDE
    block_row, block_col = coords[0, 0, 0], coords[0, 0, 1]
    live = lax.iota(jnp.int32, block_row.shape[0]) < counts[0, 0]
    owner = block_row // per_owner
    half = (owner + lax.axis_index("core")) & 1
    at_row = (half * PEERS + leaving_place(owner >> 1)) * per_owner + block_row % per_owner
    at_col = relative(block_col // per_owner, *ROW) * per_owner + block_col % per_owner
    return jnp.where(live, at_row + (at_col << 8), 1 << 16)


def build_kernel(part, places, counts, values, *rest):
    dense = rest[-1]
    rows, cols = dense.shape

    if part == 0:

        @pl.loop(0, rows // SIDE)
        def _(r):
            dense[pl.ds(pl.multiple_of(r * SIDE, SIDE), SIDE), :] = jnp.zeros((SIDE, cols), dense.dtype)

    lane = lax.broadcasted_iota(jnp.int32, (SIDE, 2 * SIDE), 1)
    groups = (counts[0, 0] + 15) >> 4

    @pl.loop((groups * part) // PARTS, (groups * (part + 1)) // PARTS)
    def _(g):
        group = values[0, 0, pl.ds(pl.multiple_of(g * 16, 16), 16), :]
        pairs = group.astype(jnp.float32).reshape(16, SIDE // 2, 2 * SIDE)
        for k in range(16):
            slot = g * 16 + k
            code = places[slot]
            at_row, at_col = code & 255, (code >> 8) & 255
            row, col = at_row * SIDE, (at_col >> 1) * 2 * SIDE
            odd = (at_col & 1) == 1
            first = (at_col & 1) * SIDE + (code >> 16) * 4 * SIDE
            plain = pairs[k]
            turned = pltpu.roll(plain, SIDE, 1)
            block = jnp.concatenate(
                [jnp.where(odd, turned, plain), jnp.where(odd, plain, turned)], axis=0
            ).astype(dense.dtype)
            mask = (lane >= first) & (lane < first + SIDE)
            place = dense.at[
                pl.ds(pl.multiple_of(row, SIDE), SIDE), pl.ds(pl.multiple_of(col, 2 * SIDE), 2 * SIDE)
            ]
            place[...] = jnp.where(mask, block, place[...])


def build(part, places, counts, values, *dense):
    vmem = pl.BlockSpec(memory_space=pltpu.VMEM)
    return pl.pallas_call(
        functools.partial(build_kernel, part),
        out_shape=bf16(2 * ROWS, ROWS),
        in_specs=[pl.BlockSpec(memory_space=pltpu.SMEM)] * 2 + [vmem] * (1 + len(dense)),
        out_specs=vmem,
        input_output_aliases={3: 0} if dense else {},
        compiler_params=pltpu.CompilerParams(vmem_limit_bytes=16 << 20),
        cost_estimate=pl.CostEstimate(flops=0, bytes_accessed=8 << 20, transcendentals=0),
        name=f"build_{part}",
    )(places, counts, values, *dense)


def over_rows(a, b):
    return lax.dot_general(a, b, (((0,), (0,)), ((), ())), preferred_element_type=jnp.float32)


def down_kernel(*refs):
    dense, *blocks, out, panel = refs
    for k, block in enumerate(blocks):
        panel[k * OWN : (k + 1) * OWN] = block[...]
    panel[ROWS - OWN :] = jnp.zeros((OWN, WIDTH), panel.dtype)
    for r in range(0, 2 * ROWS, STEP):
        out[r : r + STEP] = jnp.dot(dense[r : r + STEP], panel[...], preferred_element_type=jnp.float32)


def with_last(dense, block, rows):
    padded = jnp.concatenate([jnp.zeros((LAST - OWN, WIDTH), block.dtype), block[...]], axis=0)
    return jnp.dot(dense[rows, ROWS - LAST :], padded, preferred_element_type=jnp.float32)


def down_far_kernel(first, dense, block, most, out):
    for r in range(0, out.shape[0], OWN):
        rows = slice(ROWS + first + r, ROWS + first + r + OWN)
        out[r : r + OWN] = (most[rows] + with_last(dense, block, rows)).astype(out.dtype)


def down_near_kernel(first, dense, block, most, other, *outs):
    for k, out in enumerate(outs):
        rows = slice(first + k * OWN, first + (k + 1) * OWN)
        total = most[rows] + with_last(dense, block, rows)
        out[...] = (total + other[k * OWN : (k + 1) * OWN].astype(jnp.float32)).astype(out.dtype)


def order_kernel(*refs):
    *pairs, out = refs
    for place, (apart, ahead) in enumerate(LEAVING):
        out[place * OWN : (place + 1) * OWN] = pairs[ahead][apart * OWN : (apart + 1) * OWN]


def up_kernel(dense, rows, out):
    for r in range(0, ROWS, STEP):
        out[r : r + STEP] = over_rows(dense[:ROWS, r : r + STEP], rows[...])


def up_add_kernel(dense, rows, other, out, done, sems):
    copies = []
    for r in range(0, ROWS, 2 * OWN):
        total = over_rows(dense[ROWS:, r : r + 2 * OWN], rows[...]) + other[r : r + 2 * OWN]
        for k in range(2):
            place = r // OWN + k
            done[place] = total[k * OWN : (k + 1) * OWN].astype(done.dtype)
            copies.append(pltpu.make_async_copy(done.at[place], out.at[absolute(place, *ROW)], sems.at[place]))
            copies[-1].start()
    for copy in copies:
        copy.wait()


def down_most(dense, blocks):
    return vmem_call(
        down_kernel,
        jax.ShapeDtypeStruct((2 * ROWS, WIDTH), jnp.float32),
        "down_most",
        scratch=[pltpu.VMEM((ROWS, WIDTH), jnp.bfloat16)],
        flops=4 * ROWS * ROWS * WIDTH,
    )(dense, *blocks)


def down_blocks(dense, most, block):
    runs = ((0, FIRST), (FIRST, PEERS - FIRST))
    others = []
    for n, (first, count) in enumerate(runs):
        kernel = functools.partial(down_far_kernel, first * OWN)
        far = vmem_call(kernel, bf16(count * OWN, WIDTH), f"down_far_{n}", flops=2 * count * OWN * LAST * WIDTH)(
            dense, block, most
        )
        other = trade(far, "core")
        if n == 0:
            other, most = lax.optimization_barrier((other, most))
        others.append(other)

    def near(n):
        first, count = runs[n]
        kernel = functools.partial(down_near_kernel, first * OWN)
        return vmem_call(
            kernel, (bf16(OWN, WIDTH),) * count, f"down_near_{n}", flops=2 * count * OWN * LAST * WIDTH
        )(dense, block, most, others[n])

    return near(0), lambda: near(1)


def meet_kernel(a, b, c, d, e, out_ab, out_cde):
    out_ab[...] = add(a[...], b[...])
    total = c[...].astype(jnp.float32) + d[...].astype(jnp.float32) + e[...].astype(jnp.float32)
    out_cde[...] = total.astype(out_cde.dtype)


def scatter(first, rest, slow, fast):
    def pass_on(array, step):
        return lax.ppermute(array, fast, [(i, (i + step) % RING) for i in range(RING)])

    s02, s12, s13 = first
    r1, r2, r3 = pass_on(s12, 1), trade(s13, slow), pass_on(s02, -1)
    r1, r2, r3, rest = lax.optimization_barrier((r1, r2, r3, rest()))
    s11, s03, s10, s01, s00 = rest
    block = bf16(OWN, WIDTH)
    t11, t03 = vmem_call(meet_kernel, (block, block), "meet")(s11, r1, s03, r2, r3)
    r4, r5 = lax.optimization_barrier((pass_on(t11, 1), pass_on(t03, -1)))
    t10 = vmem_call(sum_kernel, block, "sum_across")(s10, r4)
    return s00, r5, trade(t10, slow), pass_on(s01, 1)


def middle_kernel(a, b, c, d, out_grad, weight, activations, send, aggregated_out, grad_pre_out):
    total = a[...].astype(jnp.float32)
    for part in (b, c, d):
        total = total + part[...].astype(jnp.float32)
    aggregated = total.astype(jnp.bfloat16)
    at = lax.broadcasted_iota(jnp.int32, (OWN, OWN), 0)
    to = lax.broadcasted_iota(jnp.int32, (OWN, OWN), 1)
    half = SIDE // 2
    turn = jnp.where(
        (at // SIDE == to // SIDE) & (to % SIDE == 2 * (at % half) + (at % SIDE) // half), 1.0, 0.0
    ).astype(jnp.bfloat16)
    w = weight[...]
    pre_act = jnp.dot(aggregated, w, preferred_element_type=jnp.float32)
    sig = jax.nn.sigmoid(pre_act)
    act = (pre_act * sig).astype(jnp.bfloat16)
    activations[...] = over_rows(turn, act).astype(jnp.bfloat16)
    cotangent = jnp.dot(turn, out_grad[...], preferred_element_type=jnp.float32)
    grad_pre = (cotangent * sig * (1.0 + pre_act * (1.0 - sig))).astype(jnp.bfloat16)
    grad_agg = lax.dot_general(
        grad_pre, w, (((1,), (1,)), ((), ())), preferred_element_type=jnp.float32
    ).astype(jnp.bfloat16)
    send[...] = grad_agg
    aggregated_out[...] = aggregated
    grad_pre_out[...] = grad_pre


def wgrad_kernel(aggregated, grad_pre, wgrad_near, wgrad_far, local):
    local[...] = over_rows(aggregated[...], grad_pre[...]).astype(jnp.bfloat16)
    core = lax.axis_index("core")
    for k in range(RING):
        for g in range(RING):
            for out, half_of in ((wgrad_near, core), (wgrad_far, 1 - core)):
                rows, cols = wgrad_place(half_of, k, g)
                out[k * PIECE : (k + 1) * PIECE, g * LANES : (g + 1) * LANES] = local[rows, cols]


def wgrad_place(half_of, k, g):
    row = half_of * (WIDTH // 2) + (lax.axis_index("z") ^ k) * PIECE
    col = ((lax.axis_index("x") + g) & (RING - 1)) * LANES
    return pl.ds(pl.multiple_of(row, PIECE), PIECE), pl.ds(pl.multiple_of(col, LANES), LANES)


def add(a, b):
    return (a.astype(jnp.float32) + b.astype(jnp.float32)).astype(jnp.bfloat16)


def pair_kernel(near, other, *outs):
    for k, out in enumerate(outs):
        rows = slice(k * PIECE, (k + 1) * PIECE)
        out[...] = add(near[rows], other[rows])


def sum_kernel(*refs):
    *parts, out = refs
    total = parts[0][...].astype(jnp.float32)
    for part in parts[1:]:
        total = total + part[...].astype(jnp.float32)
    out[...] = total.astype(out.dtype)


def total_kernel(parts, out):
    total = parts[0].astype(jnp.float32)
    for k in range(1, PEERS):
        total = total + parts[k].astype(jnp.float32)
    out[...] = total.astype(out.dtype)


def square_kernel(a, b, c, d, out):
    first = a[...].astype(jnp.float32) + b[...].astype(jnp.float32)
    out[...] = (first + (c[...].astype(jnp.float32) + d[...].astype(jnp.float32))).astype(out.dtype)


def turn_kernel(low, high, *outs):
    rows = low.shape[0]
    for g, out in enumerate(outs):
        for n, part in enumerate((low, high)):
            out[n * rows : (n + 1) * rows] = part[:, g * LANES : (g + 1) * LANES]


def join_kernel(*refs):
    *parts, out = refs
    for g, part in enumerate(parts):
        out[:, g * LANES : (g + 1) * LANES] = part[...]


def place_kernel(mine, theirs, out):
    core = lax.axis_index("core")
    scale = 1.0 / math.sqrt(OWN * PEERS * 2 * PEERS)
    for k in range(RING):
        for g in range(RING):
            for part, half_of in ((mine, core), (theirs, 1 - core)):
                value = part[k * PIECE : (k + 1) * PIECE, g * LANES : (g + 1) * LANES].astype(jnp.float32)
                rows, cols = wgrad_place(half_of, k, g)
                out[rows, cols] = value * jnp.float32(scale)


def exchange(parts, axes):
    return lax.all_to_all(parts, axes, 0, 0)


def trade(array, axes, bits=1):
    return lax.ppermute(array, axes, [(i, i ^ bits) for i in range(lax.axis_size(axes))])


def double_kernel(first, second, out):
    rows = first.shape[0]
    out[:rows] = first[...]
    out[rows:] = second[...]


def gather(block, slow, fast, tasks):
    def ahead(array, step):
        return lax.ppermute(array, fast, [(i, (i - step) % RING) for i in range(RING)])

    across = trade(block, slow)
    before, after = ahead(block, -1), ahead(block, 1)
    across, before, after, state = lax.optimization_barrier((across, before, after, tasks[0](None, None)))
    across_before = trade(before, slow)
    across_after = ahead(across, 1)
    beyond = ahead(before, -1)
    across_before, across_after, beyond, state = lax.optimization_barrier(
        (across_before, across_after, beyond, tasks[1](None, state))
    )
    across_beyond = ahead(across_after, 1)
    blocks = (block, after, before, beyond, across, across_after, across_before)
    return lax.optimization_barrier((across_beyond, tasks[2](blocks, state)))


def scatter_ring(pieces, axis, name):
    arrived = [pieces[0]]
    for k in range(1, RING):
        arrived.append(lax.ppermute(pieces[k], axis, [(i, (i + k) % RING) for i in range(RING)]))
    return vmem_call(sum_kernel, bf16(*pieces[0].shape), name)(*arrived)


def gather_ring(piece, axis):
    pieces = [piece]
    for k in range(1, RING):
        pieces.append(lax.ppermute(piece, axis, [(i, (i - k) % RING) for i in range(RING)]))
    return pieces


def per_device(features, out_grad, weight, block_values, block_coords, block_counts):
    raw = (build_places(block_coords, block_counts), block_counts, block_values)
    tasks = (
        lambda blocks, dense: build(0, *raw),
        lambda blocks, dense: build(1, *raw, dense),
        lambda blocks, dense: (dense, down_most(dense, blocks)),
    )
    block, (dense, most) = gather(features, *ROW, tasks)
    parts = scatter(*down_blocks(dense, most, block), *CHIP)

    half = bf16(WIDTH // 2, WIDTH)
    own = bf16(OWN, WIDTH)
    activations, send, aggregated, grad_pre = vmem_call(
        middle_kernel, (own, own, own, own), "middle", flops=2 * 2 * OWN * WIDTH * WIDTH
    )(*parts, out_grad, weight)
    wgrads = vmem_call(
        wgrad_kernel,
        (half, half),
        "wgrad",
        scratch=[pltpu.VMEM((WIDTH, WIDTH), jnp.bfloat16)],
        flops=2 * OWN * WIDTH * WIDTH,
    )(aggregated, grad_pre)

    piece = bf16(PIECE, WIDTH)
    ys = ("y_lo", "y_hi")

    def over_core(terms):
        return vmem_call(pair_kernel, (piece,) * RING, "pair")(terms[0], trade(terms[1], "core"))

    def over_z(pieces):
        arrived = [pieces[0]] + [trade(pieces[k], "z", k) for k in range(1, RING)]
        return vmem_call(sum_kernel, piece, "sum_z")(*arrived)

    def over_y(summed):
        return vmem_call(square_kernel, piece, "sum_y")(
            summed, trade(summed, ys, 1), trade(summed, ys, 2), trade(summed, ys, 3)
        )

    pair = vmem_call(double_kernel, bf16(2 * OWN, WIDTH), "pair_y")(send, trade(send, "y_hi"))
    mine = [pair] + [lax.ppermute(pair, "x", [(i, (i - k) % RING) for i in range(RING)]) for k in range(1, RING)]
    summed = over_y(over_z(over_core(wgrads)))
    mine, summed, next_piece = lax.optimization_barrier((mine, summed, trade(summed, "z", 1)))
    mine = vmem_call(order_kernel, bf16(ROWS, WIDTH), "order")(*mine)

    theirs = trade(mine, "core")
    work = 2 * ROWS * ROWS * WIDTH
    vmem = pl.BlockSpec(memory_space=pltpu.VMEM)
    own = vmem_call(up_kernel, jax.ShapeDtypeStruct((ROWS, WIDTH), jnp.float32), "up_near", flops=work)(dense, mine)
    low = vmem_call(double_kernel, bf16(2 * PIECE, WIDTH), "double")(summed, next_piece)
    partial_grad = pl.pallas_call(
        up_add_kernel,
        out_shape=bf16(PEERS, OWN, WIDTH),
        in_specs=[vmem] * 3,
        out_specs=pl.BlockSpec(memory_space=pltpu.HBM),
        scratch_shapes=[pltpu.VMEM((PEERS, OWN, WIDTH), jnp.bfloat16), pltpu.SemaphoreType.DMA((PEERS,))],
        compiler_params=pltpu.CompilerParams(vmem_limit_bytes=16 << 20),
        cost_estimate=pl.CostEstimate(flops=work, bytes_accessed=12 << 20, transcendentals=0),
        name="up_far",
    )(dense, theirs, own)
    partial_grad, *pairs = lax.optimization_barrier((partial_grad, low, trade(low, "z", 2)))
    received = exchange(partial_grad, ROW)

    column = bf16(WIDTH // 2, LANES)
    columns = vmem_call(turn_kernel, (column,) * RING, "turn")(*pairs)
    summed = scatter_ring(columns, "x", "sum_x")
    columns = gather_ring(summed, "x")
    own_half = vmem_call(join_kernel, half, "join")(*columns)
    weight_grad = vmem_call(place_kernel, jax.ShapeDtypeStruct((WIDTH, WIDTH), jnp.float32), "place")(
        own_half, trade(own_half, "core")
    )

    feature_grad = vmem_call(total_kernel, bf16(OWN, WIDTH), "total")(received)
    return (activations, weight_grad, feature_grad)


def solution(mesh):
    fine = Mesh(mesh.devices.reshape(SIZES), AXES)
    return jax.shard_map(
        per_device,
        mesh=fine,
        in_specs=(
            P(COL + ROW, None),
            P(ROW + COL, None),
            P(),
            P(ROW, COL, None, None),
            P(ROW, COL, None, None),
            P(ROW, COL),
        ),
        out_specs=(P(ROW + COL, None), P(), P(COL + ROW, None)),
        check_vma=False,
    )
```

```python
import functools
import math

import jax
import jax.numpy as jnp
from jax import lax
from jax.experimental import pallas as pl
from jax.experimental.pallas import tpu as pltpu
from jax.sharding import Mesh, PartitionSpec as P

AXES = ("y_lo", "z", "y_hi", "x", "core")
SIZES = (2, 4, 2, 4, 2)
ROW = ("y_lo", "z")
CHIP = ("y_hi", "x")
COL = ("y_hi", "x", "core")
SIDE = 64
PEERS = 8
OWN = 192
WIDTH = 512
ROWS = PEERS * OWN
STEP = 256
RING = 4
PARTS = 2
LAST = 2 * SIDE * 2
PIECE = WIDTH // 2 // RING
LANES = WIDTH // RING


def vmem_call(kernel, outs, name, scratch=(), flops=0, moved=1 << 20, limit=16 << 20, aliases={}):
    vmem = pl.BlockSpec(memory_space=pltpu.VMEM)

    def call(*args):
        return pl.pallas_call(
            kernel,
            out_shape=outs,
            in_specs=[vmem] * len(args),
            out_specs=jax.tree.map(lambda _: vmem, outs),
            scratch_shapes=scratch,
            input_output_aliases=aliases,
            compiler_params=pltpu.CompilerParams(vmem_limit_bytes=limit),
            cost_estimate=pl.CostEstimate(flops=flops, bytes_accessed=moved, transcendentals=0),
            name=name,
        )(*args)

    return call


def bf16(*shape):
    return jax.ShapeDtypeStruct(shape, jnp.bfloat16)


def relative(owner, slow, fast):
    apart = (owner >> 2) ^ lax.axis_index(slow)
    ahead = ((owner & (RING - 1)) - lax.axis_index(fast)) & (RING - 1)
    return apart * RING + (ahead ^ (ahead >> 1))


def absolute(place, slow, fast):
    apart, ahead = divmod(place, RING)
    ahead ^= ahead >> 1
    return (lax.axis_index(slow) ^ apart) * RING + ((lax.axis_index(fast) + ahead) & (RING - 1))


LEAVING = ((0, 2), (1, 2), (1, 3), (1, 1), (0, 3), (1, 0), (0, 1), (0, 0))
FIRST = 3


def leaving_place(chip):
    table = sum(place << 4 * (RING * apart + ahead) for place, (apart, ahead) in enumerate(LEAVING))
    apart = (chip >> 2) ^ lax.axis_index("y_hi")
    ahead = ((chip & (RING - 1)) - lax.axis_index("x")) & (RING - 1)
    return (table >> (4 * (RING * apart + ahead))) & 15


def leaving_chip(place):
    apart, ahead = LEAVING[place]
    return (lax.axis_index("y_hi") ^ apart) * RING + ((lax.axis_index("x") + ahead) & (RING - 1))


def build_places(coords, counts):
    per_owner = OWN // SIDE
    block_row, block_col = coords[0, 0, 0], coords[0, 0, 1]
    live = lax.iota(jnp.int32, block_row.shape[0]) < counts[0, 0]
    owner = block_row // per_owner
    half = (owner + lax.axis_index("core")) & 1
    at_row = (half * PEERS + leaving_place(owner >> 1)) * per_owner + block_row % per_owner
    at_col = relative(block_col // per_owner, *ROW) * per_owner + block_col % per_owner
    return jnp.where(live, at_row + (at_col << 8), 1 << 16)


def build_kernel(part, places, counts, values, *rest):
    dense = rest[-1]
    rows, cols = dense.shape

    if part == 0:

        @pl.loop(0, rows // SIDE)
        def _(r):
            dense[pl.ds(pl.multiple_of(r * SIDE, SIDE), SIDE), :] = jnp.zeros((SIDE, cols), dense.dtype)

    lane = lax.broadcasted_iota(jnp.int32, (SIDE, 2 * SIDE), 1)
    groups = (counts[0, 0] + 15) >> 4

    @pl.loop((groups * part) // PARTS, (groups * (part + 1)) // PARTS)
    def _(g):
        group = values[0, 0, pl.ds(pl.multiple_of(g * 16, 16), 16), :]
        pairs = group.astype(jnp.float32).reshape(16, SIDE // 2, 2 * SIDE)
        for k in range(16):
            slot = g * 16 + k
            code = places[slot]
            at_row, at_col = code & 255, (code >> 8) & 255
            row, col = at_row * SIDE, (at_col >> 1) * 2 * SIDE
            odd = (at_col & 1) == 1
            first = (at_col & 1) * SIDE + (code >> 16) * 4 * SIDE
            plain = pairs[k]
            turned = pltpu.roll(plain, SIDE, 1)
            block = jnp.concatenate(
                [jnp.where(odd, turned, plain), jnp.where(odd, plain, turned)], axis=0
            ).astype(dense.dtype)
            mask = (lane >= first) & (lane < first + SIDE)
            place = dense.at[
                pl.ds(pl.multiple_of(row, SIDE), SIDE), pl.ds(pl.multiple_of(col, 2 * SIDE), 2 * SIDE)
            ]
            place[...] = jnp.where(mask, block, place[...])


def build(part, places, counts, values, *dense):
    vmem = pl.BlockSpec(memory_space=pltpu.VMEM)
    return pl.pallas_call(
        functools.partial(build_kernel, part),
        out_shape=bf16(2 * ROWS, ROWS),
        in_specs=[pl.BlockSpec(memory_space=pltpu.SMEM)] * 2 + [vmem] * (1 + len(dense)),
        out_specs=vmem,
        input_output_aliases={3: 0} if dense else {},
        compiler_params=pltpu.CompilerParams(vmem_limit_bytes=16 << 20),
        cost_estimate=pl.CostEstimate(flops=0, bytes_accessed=8 << 20, transcendentals=0),
        name=f"build_{part}",
    )(places, counts, values, *dense)


def over_rows(a, b):
    return lax.dot_general(a, b, (((0,), (0,)), ((), ())), preferred_element_type=jnp.float32)


def down_kernel(*refs):
    dense, *blocks, out, panel = refs
    for k, block in enumerate(blocks):
        panel[k * OWN : (k + 1) * OWN] = block[...]
    panel[ROWS - OWN :] = jnp.zeros((OWN, WIDTH), panel.dtype)
    for r in range(0, 2 * ROWS, STEP):
        out[r : r + STEP] = jnp.dot(dense[r : r + STEP], panel[...], preferred_element_type=jnp.float32)


def with_last(dense, block, rows):
    padded = jnp.concatenate([jnp.zeros((LAST - OWN, WIDTH), block.dtype), block[...]], axis=0)
    return jnp.dot(dense[rows, ROWS - LAST :], padded, preferred_element_type=jnp.float32)


def down_far_kernel(first, dense, block, most, out):
    for r in range(0, out.shape[0], OWN):
        rows = slice(ROWS + first + r, ROWS + first + r + OWN)
        out[r : r + OWN] = (most[rows] + with_last(dense, block, rows)).astype(out.dtype)


def down_near_kernel(first, dense, block, most, other, *outs):
    for k, out in enumerate(outs):
        rows = slice(first + k * OWN, first + (k + 1) * OWN)
        total = most[rows] + with_last(dense, block, rows)
        out[...] = (total + other[k * OWN : (k + 1) * OWN].astype(jnp.float32)).astype(out.dtype)


def in_order(rows, ordered):
    for place in range(PEERS):
        ordered[place * OWN : (place + 1) * OWN] = rows[leaving_chip(place)]


def up_kernel(dense, rows, out, far, near, ordered, sems):
    strips = [pl.ds(r, STEP) for r in range(0, ROWS, STEP)]
    copies = [
        pltpu.make_async_copy(dense.at[pl.ds(0, ROWS), strip], near.at[:, strip], sems.at[n])
        for n, strip in enumerate(strips)
    ]
    copies.append(pltpu.make_async_copy(dense.at[pl.ds(ROWS, ROWS)], far, sems.at[len(strips)]))
    for copy in copies:
        copy.start()
    in_order(rows, ordered)
    for copy, r in zip(copies, range(0, ROWS, STEP)):
        copy.wait()
        out[r : r + STEP] = over_rows(near[:, r : r + STEP], ordered[...])
    copies[-1].wait()


def up_add_kernel(tile, rows, other, out, ordered, done, sems):
    in_order(rows, ordered)
    copies = []
    for r in range(0, ROWS, 2 * OWN):
        total = over_rows(tile[:, r : r + 2 * OWN], ordered[...]) + other[r : r + 2 * OWN]
        for k in range(2):
            place = r // OWN + k
            done[place] = total[k * OWN : (k + 1) * OWN].astype(done.dtype)
            copies.append(pltpu.make_async_copy(done.at[place], out.at[absolute(place, *ROW)], sems.at[place]))
            copies[-1].start()
    for copy in copies:
        copy.wait()


def down_most(dense, blocks):
    return vmem_call(
        down_kernel,
        jax.ShapeDtypeStruct((2 * ROWS, WIDTH), jnp.float32),
        "down_most",
        scratch=[pltpu.VMEM((ROWS, WIDTH), jnp.bfloat16)],
        flops=4 * ROWS * ROWS * WIDTH,
    )(dense, *blocks)


def down_blocks(dense, most, block):
    runs = ((0, FIRST), (FIRST, PEERS - FIRST))
    others = []
    for n, (first, count) in enumerate(runs):
        kernel = functools.partial(down_far_kernel, first * OWN)
        far = vmem_call(kernel, bf16(count * OWN, WIDTH), f"down_far_{n}", flops=2 * count * OWN * LAST * WIDTH)(
            dense, block, most
        )
        other = trade(far, "core")
        if n == 0:
            other, most = lax.optimization_barrier((other, most))
        others.append(other)

    def near(n):
        first, count = runs[n]
        kernel = functools.partial(down_near_kernel, first * OWN)
        return vmem_call(
            kernel, (bf16(OWN, WIDTH),) * count, f"down_near_{n}", flops=2 * count * OWN * LAST * WIDTH
        )(dense, block, most, others[n])

    return near(0), lambda: near(1)


def meet_kernel(a, b, c, d, e, out_ab, out_cde):
    out_ab[...] = add(a[...], b[...])
    total = c[...].astype(jnp.float32) + d[...].astype(jnp.float32) + e[...].astype(jnp.float32)
    out_cde[...] = total.astype(out_cde.dtype)


def scatter(first, rest, slow, fast):
    def pass_on(array, step):
        return lax.ppermute(array, fast, [(i, (i + step) % RING) for i in range(RING)])

    s02, s12, s13 = first
    r1, r2, r3 = pass_on(s12, 1), trade(s13, slow), pass_on(s02, -1)
    r1, r2, r3, rest = lax.optimization_barrier((r1, r2, r3, rest()))
    s11, s03, s10, s01, s00 = rest
    block = bf16(OWN, WIDTH)
    t11, t03 = vmem_call(meet_kernel, (block, block), "meet")(s11, r1, s03, r2, r3)
    r4, r5 = lax.optimization_barrier((pass_on(t11, 1), pass_on(t03, -1)))
    t10 = vmem_call(sum_kernel, block, "sum_across")(s10, r4)
    return s00, r5, trade(t10, slow), pass_on(s01, 1)


def middle_kernel(a, b, c, d, out_grad, weight, activations, send, aggregated_out, grad_pre_out):
    total = a[...].astype(jnp.float32)
    for part in (b, c, d):
        total = total + part[...].astype(jnp.float32)
    aggregated = total.astype(jnp.bfloat16)
    at = lax.broadcasted_iota(jnp.int32, (OWN, OWN), 0)
    to = lax.broadcasted_iota(jnp.int32, (OWN, OWN), 1)
    half = SIDE // 2
    turn = jnp.where(
        (at // SIDE == to // SIDE) & (to % SIDE == 2 * (at % half) + (at % SIDE) // half), 1.0, 0.0
    ).astype(jnp.bfloat16)
    w = weight[...]
    pre_act = jnp.dot(aggregated, w, preferred_element_type=jnp.float32)
    sig = jax.nn.sigmoid(pre_act)
    act = (pre_act * sig).astype(jnp.bfloat16)
    activations[...] = over_rows(turn, act).astype(jnp.bfloat16)
    cotangent = jnp.dot(turn, out_grad[...], preferred_element_type=jnp.float32)
    grad_pre = (cotangent * sig * (1.0 + pre_act * (1.0 - sig))).astype(jnp.bfloat16)
    grad_agg = lax.dot_general(
        grad_pre, w, (((1,), (1,)), ((), ())), preferred_element_type=jnp.float32
    ).astype(jnp.bfloat16)
    for k in range(PEERS):
        send[k] = grad_agg
    aggregated_out[...] = aggregated
    grad_pre_out[...] = grad_pre


def wgrad_kernel(aggregated, grad_pre, wgrad_near, wgrad_far, local):
    local[...] = over_rows(aggregated[...], grad_pre[...]).astype(jnp.bfloat16)
    core = lax.axis_index("core")
    for k in range(RING):
        for g in range(RING):
            for out, half_of in ((wgrad_near, core), (wgrad_far, 1 - core)):
                rows, cols = wgrad_place(half_of, k, g)
                out[k * PIECE : (k + 1) * PIECE, g * LANES : (g + 1) * LANES] = local[rows, cols]


def wgrad_place(half_of, k, g):
    row = half_of * (WIDTH // 2) + (lax.axis_index("z") ^ k) * PIECE
    col = ((lax.axis_index("x") + g) & (RING - 1)) * LANES
    return pl.ds(pl.multiple_of(row, PIECE), PIECE), pl.ds(pl.multiple_of(col, LANES), LANES)


def add(a, b):
    return (a.astype(jnp.float32) + b.astype(jnp.float32)).astype(jnp.bfloat16)


def pair_kernel(near, other, *outs):
    for k, out in enumerate(outs):
        rows = slice(k * PIECE, (k + 1) * PIECE)
        out[...] = add(near[rows], other[rows])


def sum_kernel(*refs):
    *parts, out = refs
    total = parts[0][...].astype(jnp.float32)
    for part in parts[1:]:
        total = total + part[...].astype(jnp.float32)
    out[...] = total.astype(out.dtype)


def total_kernel(parts, out):
    total = parts[0].astype(jnp.float32)
    for k in range(1, PEERS):
        total = total + parts[k].astype(jnp.float32)
    out[...] = total.astype(out.dtype)


def square_kernel(a, b, c, d, out):
    first = a[...].astype(jnp.float32) + b[...].astype(jnp.float32)
    out[...] = (first + (c[...].astype(jnp.float32) + d[...].astype(jnp.float32))).astype(out.dtype)


def turn_kernel(low, high, *outs):
    for g, out in enumerate(outs):
        for k in range(RING):
            part = (low, high)[k & 1]
            rows = slice((k >> 1) * PIECE, ((k >> 1) + 1) * PIECE)
            out[k * PIECE : (k + 1) * PIECE] = part[rows, g * LANES : (g + 1) * LANES]


def join_kernel(*refs):
    *parts, out = refs
    for g, part in enumerate(parts):
        out[:, g * LANES : (g + 1) * LANES] = part[...]


def place_kernel(mine, theirs, out):
    core = lax.axis_index("core")
    scale = 1.0 / math.sqrt(OWN * PEERS * 2 * PEERS)
    for k in range(RING):
        for g in range(RING):
            for part, half_of in ((mine, core), (theirs, 1 - core)):
                value = part[k * PIECE : (k + 1) * PIECE, g * LANES : (g + 1) * LANES].astype(jnp.float32)
                rows, cols = wgrad_place(half_of, k, g)
                out[rows, cols] = value * jnp.float32(scale)


def exchange(parts, axes):
    return lax.all_to_all(parts, axes, 0, 0)


def trade(array, axes, bits=1):
    return lax.ppermute(array, axes, [(i, i ^ bits) for i in range(lax.axis_size(axes))])


def double_kernel(first, second, out):
    rows = first.shape[0]
    out[:rows] = first[...]
    out[rows:] = second[...]


def gather(block, slow, fast, tasks):
    def ahead(array, step):
        return lax.ppermute(array, fast, [(i, (i - step) % RING) for i in range(RING)])

    across = trade(block, slow)
    before, after = ahead(block, -1), ahead(block, 1)
    across, before, after, state = lax.optimization_barrier((across, before, after, tasks[0](None, None)))
    across_before = trade(before, slow)
    across_after = ahead(across, 1)
    beyond = ahead(before, -1)
    across_before, across_after, beyond, state = lax.optimization_barrier(
        (across_before, across_after, beyond, tasks[1](None, state))
    )
    across_beyond = ahead(across_after, 1)
    blocks = (block, after, before, beyond, across, across_after, across_before)
    return lax.optimization_barrier((across_beyond, tasks[2](blocks, state)))


def scatter_ring(pieces, axis, name):
    arrived = [pieces[0]]
    for k in range(1, RING):
        arrived.append(lax.ppermute(pieces[k], axis, [(i, (i + k) % RING) for i in range(RING)]))
    return vmem_call(sum_kernel, bf16(*pieces[0].shape), name)(*arrived)


def gather_ring(piece, axis):
    pieces = [piece]
    for k in range(1, RING):
        pieces.append(lax.ppermute(piece, axis, [(i, (i - k) % RING) for i in range(RING)]))
    return pieces


def per_device(features, out_grad, weight, block_values, block_coords, block_counts):
    raw = (build_places(block_coords, block_counts), block_counts, block_values)
    tasks = (
        lambda blocks, dense: build(0, *raw),
        lambda blocks, dense: build(1, *raw, dense),
        lambda blocks, dense: (dense, down_most(dense, blocks)),
    )
    block, (dense, most) = gather(features, *ROW, tasks)
    parts = scatter(*down_blocks(dense, most, block), *CHIP)

    half = bf16(WIDTH // 2, WIDTH)
    own = bf16(OWN, WIDTH)
    activations, send, aggregated, grad_pre = vmem_call(
        middle_kernel, (own, bf16(PEERS, OWN, WIDTH), own, own), "middle", flops=2 * 2 * OWN * WIDTH * WIDTH
    )(*parts, out_grad, weight)
    wgrads = vmem_call(
        wgrad_kernel,
        (half, half),
        "wgrad",
        scratch=[pltpu.VMEM((WIDTH, WIDTH), jnp.bfloat16)],
        flops=2 * OWN * WIDTH * WIDTH,
    )(aggregated, grad_pre)

    piece = bf16(PIECE, WIDTH)
    ys = ("y_lo", "y_hi")

    def over_core(terms):
        return vmem_call(pair_kernel, (piece,) * RING, "pair")(terms[0], trade(terms[1], "core"))

    def over_z(pieces):
        arrived = [pieces[0]] + [trade(pieces[k], "z", k) for k in range(1, RING)]
        return vmem_call(sum_kernel, piece, "sum_z")(*arrived)

    def over_y(summed):
        return vmem_call(square_kernel, piece, "sum_y")(
            summed, trade(summed, ys, 1), trade(summed, ys, 2), trade(summed, ys, 3)
        )

    mine = exchange(send, CHIP)
    summed = over_y(over_z(over_core(wgrads)))
    summed, mine = lax.optimization_barrier((summed, mine))

    theirs = trade(mine, "core")
    work = 2 * ROWS * ROWS * WIDTH
    vmem = pl.BlockSpec(memory_space=pltpu.VMEM)
    own, far = pl.pallas_call(
        up_kernel,
        out_shape=(jax.ShapeDtypeStruct((ROWS, WIDTH), jnp.float32), bf16(ROWS, ROWS)),
        in_specs=[pl.BlockSpec(memory_space=pltpu.HBM), vmem],
        out_specs=(vmem, vmem),
        scratch_shapes=[
            pltpu.VMEM((ROWS, ROWS), jnp.bfloat16),
            pltpu.VMEM((ROWS, WIDTH), jnp.bfloat16),
            pltpu.SemaphoreType.DMA((ROWS // STEP + 1,)),
        ],
        compiler_params=pltpu.CompilerParams(vmem_limit_bytes=44 << 20),
        cost_estimate=pl.CostEstimate(flops=work, bytes_accessed=12 << 20, transcendentals=0),
        name="up_near",
    )(dense, mine)
    next_piece, own = lax.optimization_barrier((trade(summed, "z", 2), own))
    pair = vmem_call(double_kernel, bf16(2 * PIECE, WIDTH), "double")(summed, next_piece)
    partial_grad = pl.pallas_call(
        up_add_kernel,
        out_shape=bf16(PEERS, OWN, WIDTH),
        in_specs=[vmem] * 3,
        out_specs=pl.BlockSpec(memory_space=pltpu.HBM),
        scratch_shapes=[
            pltpu.VMEM((ROWS, WIDTH), jnp.bfloat16),
            pltpu.VMEM((PEERS, OWN, WIDTH), jnp.bfloat16),
            pltpu.SemaphoreType.DMA((PEERS,)),
        ],
        compiler_params=pltpu.CompilerParams(vmem_limit_bytes=16 << 20),
        cost_estimate=pl.CostEstimate(flops=work, bytes_accessed=12 << 20, transcendentals=0),
        name="up_far",
    )(far, theirs, own)
    pairs = (pair, trade(pair, "z", 1))
    partial_grad, *pairs = lax.optimization_barrier((partial_grad, *pairs))
    received = exchange(partial_grad, ROW)

    column = bf16(WIDTH // 2, LANES)
    columns = vmem_call(turn_kernel, (column,) * RING, "turn")(*pairs)
    summed = scatter_ring(columns, "x", "sum_x")
    columns = gather_ring(summed, "x")
    own_half = vmem_call(join_kernel, half, "join")(*columns)
    weight_grad = vmem_call(place_kernel, jax.ShapeDtypeStruct((WIDTH, WIDTH), jnp.float32), "place")(
        own_half, trade(own_half, "core")
    )

    feature_grad = vmem_call(total_kernel, bf16(OWN, WIDTH), "total")(received)
    return (activations, weight_grad, feature_grad)


def solution(mesh):
    fine = Mesh(mesh.devices.reshape(SIZES), AXES)
    return jax.shard_map(
        per_device,
        mesh=fine,
        in_specs=(
            P(COL + ROW, None),
            P(ROW + COL, None),
            P(),
            P(ROW, COL, None, None),
            P(ROW, COL, None, None),
            P(ROW, COL),
        ),
        out_specs=(P(ROW + COL, None), P(), P(COL + ROW, None)),
        check_vma=False,
    )
```
